128 devices in a mesh: seq: 16 (over z, y), head: 8 (over x, core).
Axes of the slice: x: 4, y: 4, z: 4, core: 2. Of those that a mesh axis runs over, the one named last changes fastest.
Arguments:
- normed: bfloat16 [32, 8192], P(None, 'seq'), may hold values from -6 to 6
- qkv_weight: bfloat16 [8192, 10240], P('seq', 'head'), may hold values from -0.0625 to 0.0625
- out_weight: bfloat16 [8192, 8192], P('head', 'seq'), may hold values from -0.0625 to 0.0625
- kv_cache: bfloat16 [1024, 2, 128, 1024], P('seq', None, None, 'head'), may hold values from -160 to 160
- lengths: int32 [8], replicated, may hold values from 1 to 9344, as said below
- slot_request: int32 [1024], P('seq'), may hold values from 0 to 8, as said below
- slot_block: int32 [1024], P('seq'), may hold values from 0 to 72, as said below
- send_list: int32 [16, 16, 4], P('seq'), may hold values from 0 to 64, as said below
- recv_list: int32 [16, 16, 4], P('seq'), may hold values from 0 to 64, as said below
Outputs:
- projected: bfloat16 [32, 8192], P('head', 'seq')
- moved_cache: bfloat16 [1024, 2, 128, 1024], P('seq', None, None, 'head')
The draws below stay inside these ranges and needn't reach their ends.
Inputs may be any that keep to these rules, and one draw needn't show every extreme that they name: `lengths`: every request has at least one block; a request with n blocks has each of the block numbers 0 to n - 1 in exactly one slot, and its length lies in ((n - 1) * 128, n * 128]. `slot_request`: 8 marks an empty slot. `slot_block`: 0 in empty slots. 64 marks an unused entry, and send_list[s, e, c] is unused exactly where recv_list[e, s, c] is; every owned slot is sent exactly once and no empty slot is sent; at most 4 blocks go from one device to another, and some device receives exactly 4 from every device; after the scale-in only half of the seq devices hold blocks. `recv_list`: 64 marks an unused entry; each slot of a device is filled at most once.
All inputs are finite; a program needn't handle non-finite values.
Results may differ from the reference program's by a relative error of at most 0.025.
Values may be sent and summed in bfloat16 or wider, within the bound.
A program may use at most 128 MiB of HBM per device.

```python
import jax
import jax.numpy as jnp
from jax import lax

D = 8192
HEADS = 64
KV_HEADS = 8
HEAD = 128
POS = 4
R = 8
BLOCK = 128
CAP = 4
MOST = 72
ROWS = 32
QKV_WIDTH = 10240
N_SEQ = 16


def shuffle_rows(subkey):
    return jax.random.permutation(subkey, CAP * N_SEQ).astype(jnp.int32)


def layout_tables(key):
    peer_count = N_SEQ
    slot_dev = CAP * N_SEQ
    entry_count = peer_count * slot_dev
    subkeys = jax.random.split(jax.random.fold_in(key, 5), 7)
    device_order = jax.random.permutation(subkeys[0], peer_count).astype(jnp.int32)
    staying = jnp.zeros((peer_count,), jnp.int32).at[device_order[:peer_count // 2]].set(1)
    counts = jax.random.randint(subkeys[1], (peer_count, peer_count), CAP - CAP // 4, CAP + 1).astype(jnp.int32)
    counts = jnp.where(jnp.arange(peer_count, dtype=jnp.int32)[None, :] == device_order[0], CAP, counts) * staying[None, :]
    entry_live = jnp.arange(CAP, dtype=jnp.int32)[None, None, :] < counts[:, :, None]
    live_flag = entry_live.reshape(-1).astype(jnp.int32)
    block_rank = jnp.cumsum(live_flag) - live_flag
    rest_rank = jnp.maximum(block_rank - R - MOST, 0)
    owner_ids = jnp.where(block_rank < R, block_rank, jnp.where(block_rank < R + MOST, 0, 1 + rest_rank % (R - 1)))
    earlier = (owner_ids[:, None] == owner_ids[None, :]) & (live_flag[None, :] == 1) & (block_rank[None, :] < block_rank[:, None])
    block_index = jnp.sum(earlier.astype(jnp.int32), axis=1)
    owner_ids = jnp.where(live_flag == 1, owner_ids, R)
    block_index = jnp.where(live_flag == 1, block_index, 0)
    per_request = jnp.sum((owner_ids[:, None] == jnp.arange(R, dtype=jnp.int32)[None, :]).astype(jnp.int32), axis=0)
    tail_tokens = jax.random.randint(subkeys[4], (R,), 1, BLOCK + 1).astype(jnp.int32)
    tail_tokens = jnp.where(jnp.arange(R, dtype=jnp.int32) == 0, BLOCK, tail_tokens)
    lengths = (per_request - 1) * BLOCK + tail_tokens
    old_perm = jax.vmap(shuffle_rows)(jax.random.split(subkeys[5], peer_count))
    new_perm = jax.vmap(shuffle_rows)(jax.random.split(subkeys[6], peer_count))
    send_table = jnp.where(entry_live, old_perm.reshape(peer_count, peer_count, CAP), slot_dev)
    recv_table = jnp.where(entry_live.transpose(1, 0, 2), new_perm.reshape(peer_count, peer_count, CAP), slot_dev)
    global_old = (jnp.arange(peer_count, dtype=jnp.int32)[:, None] * slot_dev + old_perm).reshape(-1)
    slot_owner = jnp.zeros((entry_count,), jnp.int32).at[global_old].set(owner_ids)
    slot_blocks = jnp.zeros((entry_count,), jnp.int32).at[global_old].set(block_index)
    return (lengths.astype(jnp.int32), slot_owner, slot_blocks, send_table.astype(jnp.int32), recv_table.astype(jnp.int32))


def draw_lengths(key, part):
    return layout_tables(key)[0]


def draw_slot_request(key, part):
    return layout_tables(key)[1]


def draw_slot_block(key, part):
    return layout_tables(key)[2]


def draw_send_list(key, part):
    return layout_tables(key)[3]


def draw_recv_list(key, part):
    return layout_tables(key)[4]


def draw_kv_cache(key, part):
    cache_shape = (CAP * N_SEQ * N_SEQ, 2, BLOCK, KV_HEADS * HEAD)
    base_key = jax.random.fold_in(jax.random.fold_in(key, 11), 0)
    values = jax.random.normal(base_key, cache_shape, jnp.float32)
    return values.astype(jnp.bfloat16)


def level_of(stream_key, dims, cuts, least, largest):
    def one(dim, shards_of):
        steps = jax.random.uniform(jax.random.fold_in(jax.random.fold_in(stream_key, 6), dim), (shards_of,), jnp.float32, least / len(cuts), largest / len(cuts))
        return jnp.repeat(jnp.exp(steps), dims[dim] // shards_of).reshape((-1,) + (1,) * (len(dims) - dim - 1))

    factor_of = one(*cuts[0])
    for cut in cuts[1:]:
        factor_of = factor_of * one(*cut)
    return factor_of


def centred(key, extent, deviation, reach, cuts=(), held_as=jnp.bfloat16):
    entries = jax.random.normal(key, extent, jnp.float32) * deviation
    if len(cuts) > 0:
        entries = level_of(key, extent, cuts, -0.22, 0.18) * entries
    return jnp.clip(entries, min=-reach, max=reach).astype(held_as)


def setup_inputs(seed: int = 0) -> dict:
    arg_keys = jax.random.split(jax.random.key(seed), 10)
    return {
        "normed": centred(arg_keys[0], (ROWS, D), 1.0, 6.0, ((1, 16),)),
        "qkv_weight": centred(arg_keys[1], (D, QKV_WIDTH), D ** -0.5, 0.0625, ((0, 16), (1, 8))),
        "out_weight": centred(arg_keys[2], (HEADS * HEAD, D), (HEADS * HEAD) ** -0.5, 0.0625, ((0, 8), (1, 16))),
        "kv_cache": draw_kv_cache(jax.random.fold_in(arg_keys[9], 71), 0),
        "lengths": draw_lengths(jax.random.fold_in(arg_keys[9], 71), 0),
        "slot_request": draw_slot_request(jax.random.fold_in(arg_keys[9], 71), 0),
        "slot_block": draw_slot_block(jax.random.fold_in(arg_keys[9], 71), 0),
        "send_list": draw_send_list(jax.random.fold_in(arg_keys[9], 71), 0),
        "recv_list": draw_recv_list(jax.random.fold_in(arg_keys[9], 71), 0),
    }


rope_base = 500000.0
neg_large = -1.0e30


def round_half(values):
    return lax.optimization_barrier(values.astype(jnp.bfloat16))


def rotate(values, positions):
    half_width = values.shape[-1] // 2
    frequencies = rope_base ** (-(jnp.arange(half_width, dtype=jnp.float32) * 2.0 / values.shape[-1]))
    angles = positions[..., None] * frequencies
    cosine_table = jnp.cos(angles)
    sine_table = jnp.sin(angles)
    lower_half = values[..., :half_width]
    upper_half = values[..., half_width:]
    return jnp.concatenate([lower_half * cosine_table - upper_half * sine_table, upper_half * cosine_table + lower_half * sine_table], axis=-1)


def reference(normed, qkv_weight, out_weight, kv_cache, lengths, slot_request, slot_block, send_list, recv_list):
    group_size = HEADS // KV_HEADS
    scale_factor = HEAD ** -0.5
    requests = lengths.shape[0]
    slot_count = kv_cache.shape[0]
    projected_qkv = jnp.dot(normed, qkv_weight, preferred_element_type=jnp.float32)
    projected_qkv = projected_qkv.reshape(requests, POS, KV_HEADS, group_size + 2, HEAD)
    positions = (lengths[:, None] + jnp.arange(POS, dtype=jnp.int32)[None, :]).astype(jnp.float32)
    queries = round_half(rotate(projected_qkv[:, :, :, :group_size], positions[:, :, None, None]))
    keys_new = round_half(rotate(projected_qkv[:, :, :, group_size], positions[:, :, None]))
    values_new = round_half(projected_qkv[:, :, :, group_size + 1])
    slot_clip = jnp.minimum(slot_request, requests - 1)
    live_slot = slot_request < requests
    token_pos = slot_block[:, None] * BLOCK + jnp.arange(BLOCK, dtype=jnp.int32)[None, :]
    token_valid = (token_pos < lengths[slot_clip][:, None]) & live_slot[:, None]
    member = slot_request[:, None] == jnp.arange(requests, dtype=jnp.int32)[None, :]
    member_float = member.astype(jnp.float32).T
    cache_view = kv_cache.reshape(slot_count, 2, BLOCK, KV_HEADS, HEAD)
    causal = jnp.arange(POS)[:, None] >= jnp.arange(POS)[None, :]

    def head_part(head_index):
        head_slice = lax.dynamic_index_in_dim(cache_view, head_index, axis=3, keepdims=False)
        head_queries = lax.dynamic_index_in_dim(queries, head_index, axis=2, keepdims=False)
        head_keys_new = lax.dynamic_index_in_dim(keys_new, head_index, axis=2, keepdims=False)
        head_values_new = lax.dynamic_index_in_dim(values_new, head_index, axis=2, keepdims=False)
        gathered = head_queries[slot_clip].astype(jnp.float32)
        scores = jnp.einsum("spgd,sbd->sgpb", gathered, head_slice[:, 0].astype(jnp.float32)) * scale_factor
        scores = jnp.where(token_valid[:, None, None, :], scores, neg_large)
        new_scores = jnp.einsum("rpgd,rqd->rgpq", head_queries.astype(jnp.float32), head_keys_new.astype(jnp.float32)) * scale_factor
        new_scores = jnp.where(causal, new_scores, neg_large)
        slot_max = jnp.max(scores, axis=-1)
        flat_width = group_size * POS
        cache_max = jnp.max(jnp.where(member[:, None, :], slot_max.reshape(slot_count, flat_width)[:, :, None], neg_large), axis=0).T
        top_max = jnp.maximum(cache_max.reshape(requests, group_size, POS), jnp.max(new_scores, axis=-1))
        weights = jnp.where(token_valid[:, None, None, :], jnp.exp(scores - top_max[slot_clip][..., None]), 0.0)
        slot_sum = jnp.sum(weights, axis=-1)
        slot_acc = jnp.einsum("sgpb,sbd->sgpd", round_half(weights).astype(jnp.float32), head_slice[:, 1].astype(jnp.float32))
        request_sum = jnp.dot(member_float, slot_sum.reshape(slot_count, -1), precision=lax.Precision.HIGHEST)
        request_acc = jnp.dot(member_float, slot_acc.reshape(slot_count, -1), precision=lax.Precision.HIGHEST)
        request_acc = request_acc.reshape(requests, group_size, POS, HEAD)
        new_weights = jnp.where(causal, jnp.exp(new_scores - top_max[..., None]), 0.0)
        denominator = request_sum.reshape(requests, group_size, POS) + jnp.sum(new_weights, axis=-1)
        numerator = request_acc + jnp.einsum("rgpq,rqd->rgpd", round_half(new_weights).astype(jnp.float32), head_values_new.astype(jnp.float32))
        return numerator / denominator[..., None]

    per_head = lax.map(head_part, jnp.arange(KV_HEADS, dtype=jnp.int32))
    attended = per_head.transpose(1, 3, 0, 2, 4).reshape(requests * POS, HEADS * HEAD).astype(jnp.bfloat16)
    projected = jnp.dot(attended, out_weight, preferred_element_type=jnp.float32).astype(jnp.bfloat16)
    slot_dev = slot_count // N_SEQ
    device_ids = jnp.arange(N_SEQ, dtype=jnp.int32)
    old_global = device_ids[:, None, None] * slot_dev + jnp.minimum(send_list, slot_dev - 1)
    recv_order = recv_list.transpose(1, 0, 2)
    new_global = jnp.where(recv_order < slot_dev, device_ids[None, :, None] * slot_dev + recv_order, slot_count)
    moved_cache = jnp.zeros_like(kv_cache).at[new_global.reshape(-1)].set(kv_cache[old_global.reshape(-1)], mode="drop")
    return projected, moved_cache
```

```python
import jax
import jax.numpy as jnp
from jax import lax
from jax.sharding import PartitionSpec as P

HEADS = 64
KV_HEADS = 8
HEAD = 128
POS = 4
BLOCK = 128


rope_base = 500000.0
neg_large = -1e30


def rotate(values, positions):
    half_width = values.shape[-1] // 2
    frequencies = rope_base ** (
        -(jnp.arange(half_width, dtype=jnp.float32) * 2.0 / values.shape[-1])
    )
    angles = positions[..., None] * frequencies
    cosine_table = jnp.cos(angles)
    sine_table = jnp.sin(angles)
    lower_half = values[..., :half_width]
    upper_half = values[..., half_width:]
    return jnp.concatenate(
        [
            lower_half * cosine_table - upper_half * sine_table,
            upper_half * cosine_table + lower_half * sine_table,
        ],
        axis=-1,
    )


def body(
    normed,
    qkv_weight,
    out_weight,
    kv_cache,
    lengths,
    slot_request,
    slot_block,
    send_list,
    recv_list,
):
    group_size = HEADS // KV_HEADS
    scale_factor = HEAD ** (-0.5)
    requests = lengths.shape[0]
    slot_count = kv_cache.shape[0]
    projected_qkv = lax.psum(
        jnp.dot(normed, qkv_weight, preferred_element_type=jnp.float32), "seq"
    )
    projected_qkv = projected_qkv.reshape(requests, POS, -1, group_size + 2, HEAD)
    local_kv = projected_qkv.shape[2]
    positions = (lengths[:, None] + jnp.arange(POS, dtype=jnp.int32)[None, :]).astype(jnp.float32)
    queries = rotate(projected_qkv[:, :, :, :group_size], positions[:, :, None, None]).astype(
        jnp.bfloat16
    )
    keys_new = rotate(projected_qkv[:, :, :, group_size], positions[:, :, None]).astype(
        jnp.bfloat16
    )
    values_new = projected_qkv[:, :, :, group_size + 1].astype(jnp.bfloat16)
    flat_send = send_list.reshape(-1)
    outgoing = kv_cache[jnp.minimum(flat_send, slot_count - 1)]
    outgoing = outgoing.reshape((lax.axis_size("seq"), -1) + kv_cache.shape[1:])
    incoming = lax.all_to_all(outgoing, "seq", split_axis=0, concat_axis=0, tiled=True)
    incoming = incoming.reshape((-1,) + kv_cache.shape[1:])
    moved_cache = jnp.zeros_like(kv_cache).at[recv_list.reshape(-1)].set(incoming, mode="drop")
    slot_clip = jnp.minimum(slot_request, requests - 1)
    live_slot = slot_request < requests
    token_pos = slot_block[:, None] * BLOCK + jnp.arange(BLOCK, dtype=jnp.int32)[None, :]
    token_valid = (token_pos < lengths[slot_clip][:, None]) & live_slot[:, None]
    cache_view = kv_cache.reshape(slot_count, 2, BLOCK, local_kv, HEAD)
    gathered = queries[slot_clip]
    scores = (
        jnp.einsum(
            "sptgd,sbtd->stgpb", gathered, cache_view[:, 0], preferred_element_type=jnp.float32
        )
        * scale_factor
    )
    scores = jnp.where(token_valid[:, None, None, None, :], scores, neg_large)
    slot_max = jnp.max(scores, axis=-1)
    weights = jnp.where(
        token_valid[:, None, None, None, :], jnp.exp(scores - slot_max[..., None]), 0.0
    )
    slot_sum = jnp.sum(weights, axis=-1)
    slot_acc = jnp.einsum(
        "stgpb,sbtd->stgpd",
        weights.astype(jnp.bfloat16),
        cache_view[:, 1],
        preferred_element_type=jnp.float32,
    )
    flat_width = local_kv * group_size * POS
    slot_max_flat = slot_max.reshape(slot_count, flat_width)
    member = slot_request[:, None] == jnp.arange(requests, dtype=jnp.int32)[None, :]
    request_max = jnp.max(
        jnp.where(member[:, None, :], slot_max_flat[:, :, None], neg_large), axis=0
    ).T
    rescale = jnp.exp(slot_max_flat - request_max[slot_clip])
    member_float = member.astype(jnp.float32).T
    request_sum = jnp.dot(
        member_float,
        slot_sum.reshape(slot_count, flat_width) * rescale,
        precision=lax.Precision.HIGHEST,
    )
    scaled_acc = (slot_acc.reshape(slot_count, flat_width, HEAD) * rescale[:, :, None]).reshape(
        slot_count, flat_width * HEAD
    )
    request_acc = jnp.dot(member_float, scaled_acc, precision=lax.Precision.HIGHEST).reshape(
        requests, flat_width, HEAD
    )
    total_max = lax.pmax(request_max, "seq")
    adjust = jnp.exp(request_max - total_max)
    total_sum, total_acc = (
        lax.psum((request_sum * adjust).astype(jnp.bfloat16), "seq").astype(jnp.float32),
        lax.psum((request_acc * adjust[:, :, None]).astype(jnp.bfloat16), "seq").astype(
            jnp.float32
        ),
    )
    new_scores = (
        jnp.einsum("rptgd,rqtd->rtgpq", queries, keys_new, preferred_element_type=jnp.float32)
        * scale_factor
    )
    causal = jnp.arange(POS)[:, None] >= jnp.arange(POS)[None, :]
    new_scores = jnp.where(causal, new_scores, neg_large)
    cache_max = total_max.reshape(requests, local_kv, group_size, POS)
    top_max = jnp.maximum(cache_max, jnp.max(new_scores, axis=-1))
    carry_scale = jnp.exp(cache_max - top_max)
    new_weights = jnp.where(causal, jnp.exp(new_scores - top_max[..., None]), 0.0)
    denominator = total_sum.reshape(requests, local_kv, group_size, POS) * carry_scale + jnp.sum(
        new_weights, axis=-1
    )
    numerator = (
        total_acc.reshape(requests, local_kv, group_size, POS, HEAD) * carry_scale[..., None]
    )
    numerator = numerator + jnp.einsum(
        "rtgpq,rqtd->rtgpd",
        new_weights.astype(jnp.bfloat16),
        values_new,
        preferred_element_type=jnp.float32,
    )
    attended = (
        (numerator / denominator[..., None])
        .transpose(0, 3, 1, 2, 4)
        .reshape(requests * POS, -1)
        .astype(jnp.bfloat16)
    )
    projected = lax.psum_scatter(
        jnp.dot(attended, out_weight, preferred_element_type=jnp.float32).astype(jnp.bfloat16),
        "head",
        scatter_dimension=0,
        tiled=True,
    )
    return (projected, moved_cache)


def solution(mesh):
    placed = (
        P(None, "seq"),
        P("seq", "head"),
        P("head", "seq"),
        P("seq", None, None, "head"),
        P(),
        P("seq"),
        P("seq"),
        P("seq", None, None),
        P("seq", None, None),
    )
    return jax.shard_map(
        body,
        mesh=mesh,
        in_specs=placed,
        out_specs=(P("head", "seq"), P("seq", None, None, "head")),
        check_vma=False,
    )
```

```python
import functools

import jax
import jax.numpy as jnp
from jax import lax
from jax.experimental import pallas as pl
from jax.experimental.pallas import tpu as pltpu
from jax.sharding import PartitionSpec as P

HEADS = 64
KV_HEADS = 8
HEAD = 128
POS = 4
BLOCK = 128

MESH = pl.DeviceIdType.MESH

rope_base = 500000.0
neg_large = -1e30


def _barrier(peers):
    barrier = pltpu.get_barrier_semaphore()
    for device in peers:
        pl.semaphore_signal(barrier, inc=1, device_id=device, device_id_type=MESH)
    pl.semaphore_wait(barrier, len(peers))


def _send_all(axis, n, me, src_of, land, send_sem, recv_sem):
    copies = []
    for i in range(1, n):
        peer = lax.rem(me + i, n)
        copy = pltpu.make_async_remote_copy(
            src_ref=src_of(peer),
            dst_ref=land.at[me],
            send_sem=send_sem.at[peer],
            recv_sem=recv_sem.at[me],
            device_id={axis: peer},
            device_id_type=MESH,
        )
        copy.start()
        copies.append(copy)
    return copies


def _wait_all(axis, n, me, land, send_sem, recv_sem):
    for i in range(1, n):
        src = lax.rem(me + n - i, n)
        pltpu.make_async_remote_copy(
            src_ref=land.at[src],
            dst_ref=land.at[src],
            send_sem=send_sem.at[src],
            recv_sem=recv_sem.at[src],
            device_id={axis: src},
            device_id_type=MESH,
        ).wait_recv()


def _qkv_kernel(n, part_ref, cos_ref, sin_ref, out_ref, land_a, mine, land_b, sems):
    me = lax.axis_index("seq")
    land_a[me] = part_ref[me]
    _barrier([{"seq": lax.rem(me + i, n)} for i in range(1, n)])
    sent_a = _send_all("seq", n, me, lambda p: part_ref.at[p], land_a, sems.at[0], sems.at[1])
    _wait_all("seq", n, me, land_a, sems.at[0], sems.at[1])
    total = land_a[0]
    for i in range(1, n):
        total = total + land_a[i]
    turned = pltpu.roll(total, HEAD // 2, 1)
    rotated = (total * cos_ref[...] + turned * sin_ref[...]).astype(mine.dtype)
    mine[...] = rotated
    land_b[me] = rotated
    sent_b = _send_all("seq", n, me, lambda p: mine, land_b, sems.at[2], sems.at[3])
    _wait_all("seq", n, me, land_b, sems.at[2], sems.at[3])
    for copy in sent_a + sent_b:
        copy.wait_send()
    out_ref[...] = land_b[...]


def qkv_exchange(partial, cos_table, sin_table):
    n = partial.shape[0]
    return pl.pallas_call(
        functools.partial(_qkv_kernel, n),
        out_shape=jax.ShapeDtypeStruct(partial.shape, jnp.bfloat16),
        in_specs=[pl.BlockSpec(memory_space=pltpu.VMEM)] * 3,
        out_specs=pl.BlockSpec(memory_space=pltpu.VMEM),
        scratch_shapes=[
            pltpu.VMEM(partial.shape, jnp.float32),
            pltpu.VMEM(partial.shape[1:], jnp.bfloat16),
            pltpu.VMEM(partial.shape, jnp.bfloat16),
            pltpu.SemaphoreType.DMA((4, n)),
        ],
        compiler_params=pltpu.CompilerParams(collective_id=0, has_side_effects=True),
        cost_estimate=pl.CostEstimate(
            flops=0, bytes_accessed=partial.size * 12, transcendentals=0
        ),
    )(partial, cos_table, sin_table)


def _attend_kernel(
    n, m, rows, packed_ref, w_ref, out_ref, land_p, mine, land_a, part_c, land_c, sems
):
    me = lax.axis_index("seq")
    me_h = lax.axis_index("head")
    land_p[me] = packed_ref[me]
    _barrier(
        [{"seq": lax.rem(me + i, n)} for i in range(1, n)]
        + [{"head": lax.rem(me_h + i, m)} for i in range(1, m)]
    )
    sent_p = _send_all("seq", n, me, lambda p: packed_ref.at[p], land_p, sems.at[0], sems.at[1])
    _wait_all("seq", n, me, land_p, sems.at[0], sems.at[1])
    top = land_p[0, rows : 2 * rows]
    for i in range(1, n):
        top = jnp.maximum(top, land_p[i, rows : 2 * rows])
    numerator = jnp.zeros((rows, HEAD), jnp.float32)
    denominator = jnp.zeros((rows, HEAD), jnp.float32)
    for i in range(n):
        scale = jnp.exp(land_p[i, rows : 2 * rows] - top)
        denominator = denominator + land_p[i, 2 * rows : 3 * rows] * scale
        numerator = numerator + land_p[i, :rows] * scale
    attended = (numerator / denominator).astype(mine.dtype)
    mine[...] = attended
    land_a[me] = attended
    sent_a = _send_all("seq", n, me, lambda p: mine, land_a, sems.at[2], sems.at[3])
    _wait_all("seq", n, me, land_a, sems.at[2], sems.at[3])
    heads = n // 2
    projected = None
    for g in range(heads):
        lhs = land_a[2 * g : 2 * g + 2].reshape(2 * rows, HEAD)
        term = jnp.dot(lhs, w_ref[g * HEAD : (g + 1) * HEAD, :], preferred_element_type=jnp.float32)
        projected = term if projected is None else projected + term
    per = part_c.shape[1]
    for j in range(m):
        part_c[j] = projected[j * per : (j + 1) * per]
    land_c[me_h] = part_c[me_h]
    sent_c = _send_all("head", m, me_h, lambda p: part_c.at[p], land_c, sems.at[4], sems.at[5])
    _wait_all("head", m, me_h, land_c, sems.at[4], sems.at[5])
    total = land_c[0]
    for j in range(1, m):
        total = total + land_c[j]
    for copy in sent_p + sent_a + sent_c:
        copy.wait_send()
    out_ref[...] = total.astype(out_ref.dtype)


def attend_exchange(packed, out_weight, m):
    n, three_rows, _ = packed.shape
    rows = three_rows // 3
    width = out_weight.shape[1]
    per = 2 * rows // m
    return pl.pallas_call(
        functools.partial(_attend_kernel, n, m, rows),
        out_shape=jax.ShapeDtypeStruct((per, width), jnp.bfloat16),
        in_specs=[pl.BlockSpec(memory_space=pltpu.VMEM)] * 2,
        out_specs=pl.BlockSpec(memory_space=pltpu.VMEM),
        scratch_shapes=[
            pltpu.VMEM(packed.shape, jnp.float32),
            pltpu.VMEM((rows, HEAD), jnp.bfloat16),
            pltpu.VMEM((n, rows, HEAD), jnp.bfloat16),
            pltpu.VMEM((m, per, width), jnp.float32),
            pltpu.VMEM((m, per, width), jnp.float32),
            pltpu.SemaphoreType.DMA((6, max(n, m))),
        ],
        compiler_params=pltpu.CompilerParams(collective_id=1, has_side_effects=True),
        cost_estimate=pl.CostEstimate(
            flops=2 * 2 * rows * out_weight.shape[0] * width,
            bytes_accessed=packed.size * 8 + out_weight.size * 2,
            transcendentals=n * rows * HEAD,
        ),
    )(packed, out_weight)


def rotate(values, positions):
    half_width = values.shape[-1] // 2
    frequencies = rope_base ** (
        -(jnp.arange(half_width, dtype=jnp.float32) * 2.0 / values.shape[-1])
    )
    angles = positions[..., None] * frequencies
    cosine_table = jnp.cos(angles)
    sine_table = jnp.sin(angles)
    lower_half = values[..., :half_width]
    upper_half = values[..., half_width:]
    return jnp.concatenate(
        [
            lower_half * cosine_table - upper_half * sine_table,
            upper_half * cosine_table + lower_half * sine_table,
        ],
        axis=-1,
    )


def body(
    normed,
    qkv_weight,
    out_weight,
    kv_cache,
    lengths,
    slot_request,
    slot_block,
    send_list,
    recv_list,
):
    group_size = HEADS // KV_HEADS
    scale_factor = HEAD ** (-0.5)
    requests = lengths.shape[0]
    slot_count = kv_cache.shape[0]
    n_seq = lax.axis_size("seq")
    n_head = lax.axis_size("head")
    me_seq = lax.axis_index("seq")
    rows = normed.shape[0]
    rows_per = rows // n_seq
    groups = qkv_weight.shape[1] // HEAD

    partial = jnp.dot(normed, qkv_weight, preferred_element_type=jnp.float32)
    partial = partial.reshape(n_seq, rows_per * groups, HEAD)
    row_ids = me_seq * rows_per + jnp.arange(rows_per, dtype=jnp.int32)
    row_pos = (lengths[row_ids // POS] + row_ids % POS).astype(jnp.float32)
    half_width = HEAD // 2
    frequencies = rope_base ** (-(jnp.arange(half_width, dtype=jnp.float32) * 2.0 / HEAD))
    angles = row_pos[:, None] * frequencies
    cosine, sine = jnp.cos(angles), jnp.sin(angles)
    turned_groups = (jnp.arange(groups) <= group_size)[None, :, None]
    cos_table = jnp.where(
        turned_groups, jnp.concatenate([cosine, cosine], axis=-1)[:, None, :], 1.0
    ).reshape(rows_per * groups, HEAD)
    sin_table = jnp.where(
        turned_groups, jnp.concatenate([-sine, sine], axis=-1)[:, None, :], 0.0
    ).reshape(rows_per * groups, HEAD)
    qkv = qkv_exchange(partial, cos_table, sin_table).reshape(requests, POS, 1, groups, HEAD)
    local_kv = 1

    flat_send = send_list.reshape(-1)
    outgoing = kv_cache[jnp.minimum(flat_send, slot_count - 1)]
    outgoing = outgoing.reshape((lax.axis_size("seq"), -1) + kv_cache.shape[1:])
    outgoing, qkv = lax.optimization_barrier((outgoing, qkv))
    incoming = lax.all_to_all(outgoing, "seq", split_axis=0, concat_axis=0, tiled=True)
    incoming = incoming.reshape((-1,) + kv_cache.shape[1:])
    arrivals = incoming.shape[0]
    source_of = (
        jnp.full((slot_count + 1,), arrivals, jnp.int32)
        .at[recv_list.reshape(-1)]
        .set(jnp.arange(arrivals, dtype=jnp.int32), mode="drop")[:slot_count]
    )
    moved_cache = jnp.where(
        (source_of < arrivals)[:, None, None, None],
        incoming[jnp.minimum(source_of, arrivals - 1)],
        jnp.zeros((), kv_cache.dtype),
    )
    queries = qkv[:, :, :, :group_size]
    keys_new = qkv[:, :, :, group_size]
    values_new = qkv[:, :, :, group_size + 1]

    slot_clip = jnp.minimum(slot_request, requests - 1)
    live_slot = slot_request < requests
    token_pos = slot_block[:, None] * BLOCK + jnp.arange(BLOCK, dtype=jnp.int32)[None, :]
    token_valid = (token_pos < lengths[slot_clip][:, None]) & live_slot[:, None]
    cache_view = kv_cache.reshape(slot_count, 2, BLOCK, local_kv, HEAD)
    gathered = queries[slot_clip]
    scores = (
        jnp.einsum(
            "sptgd,sbtd->stgpb", gathered, cache_view[:, 0], preferred_element_type=jnp.float32
        )
        * scale_factor
    )
    scores = jnp.where(token_valid[:, None, None, None, :], scores, neg_large)
    slot_max = jnp.max(scores, axis=-1)
    weights = jnp.where(
        token_valid[:, None, None, None, :], jnp.exp(scores - slot_max[..., None]), 0.0
    )
    slot_sum = jnp.sum(weights, axis=-1)
    slot_acc = jnp.einsum(
        "stgpb,sbtd->stgpd",
        weights.astype(jnp.bfloat16),
        cache_view[:, 1],
        preferred_element_type=jnp.float32,
    )
    flat_width = local_kv * group_size * POS
    slot_max_flat = slot_max.reshape(slot_count, flat_width)
    member = slot_request[:, None] == jnp.arange(requests, dtype=jnp.int32)[None, :]
    request_max = jnp.max(
        jnp.where(member[:, None, :], slot_max_flat[:, :, None], neg_large), axis=0
    ).T
    rescale = jnp.exp(slot_max_flat - request_max[slot_clip])
    member_float = member.astype(jnp.float32).T
    request_sum = jnp.dot(
        member_float,
        slot_sum.reshape(slot_count, flat_width) * rescale,
        precision=lax.Precision.HIGHEST,
    )
    scaled_acc = (slot_acc.reshape(slot_count, flat_width, HEAD) * rescale[:, :, None]).reshape(
        slot_count, flat_width * HEAD
    )
    request_acc = jnp.dot(member_float, scaled_acc, precision=lax.Precision.HIGHEST).reshape(
        requests, flat_width, HEAD
    )

    new_scores = (
        jnp.einsum("rptgd,rqtd->rtgpq", queries, keys_new, preferred_element_type=jnp.float32)
        * scale_factor
    )
    causal = jnp.arange(POS)[:, None] >= jnp.arange(POS)[None, :]
    new_scores = jnp.where(causal, new_scores, neg_large)
    new_max = jnp.max(new_scores, axis=-1)
    new_weights = jnp.where(causal, jnp.exp(new_scores - new_max[..., None]), 0.0)
    new_sum = jnp.sum(new_weights, axis=-1).reshape(requests, flat_width)
    new_acc = jnp.einsum(
        "rtgpq,rqtd->rtgpd",
        new_weights.astype(jnp.bfloat16),
        values_new,
        preferred_element_type=jnp.float32,
    ).reshape(requests, flat_width, HEAD)
    first = me_seq == 0
    new_max = jnp.where(first, new_max.reshape(requests, flat_width), neg_large)
    new_sum = jnp.where(first, new_sum, 0.0)
    new_acc = jnp.where(first, new_acc, 0.0)
    part_max = jnp.maximum(request_max, new_max)
    keep_old = jnp.exp(request_max - part_max)
    keep_new = jnp.exp(new_max - part_max)
    part_sum = request_sum * keep_old + new_sum * keep_new
    part_acc = request_acc * keep_old[..., None] + new_acc * keep_new[..., None]

    def by_chunk(values):
        lead = values.reshape(2, requests // 2, group_size, POS, -1).transpose(2, 0, 1, 3, 4)
        return lead.reshape(n_seq, requests * group_size * POS // n_seq, -1)

    chunk_rows = requests * flat_width // n_seq
    packed = jnp.concatenate(
        [
            by_chunk(part_acc),
            jnp.broadcast_to(by_chunk(part_max), (n_seq, chunk_rows, HEAD)),
            jnp.broadcast_to(by_chunk(part_sum), (n_seq, chunk_rows, HEAD)),
        ],
        axis=1,
    )
    projected = attend_exchange(packed, out_weight, n_head)
    return (projected, moved_cache)


def solution(mesh):
    placed = (
        P(None, "seq"),
        P("seq", "head"),
        P("head", "seq"),
        P("seq", None, None, "head"),
        P(),
        P("seq"),
        P("seq"),
        P("seq", None, None),
        P("seq", None, None),
    )
    return jax.shard_map(
        body,
        mesh=mesh,
        in_specs=placed,
        out_specs=(P("head", "seq"), P("seq", None, None, "head")),
        check_vma=False,
    )
```

```python
import functools

import jax
import jax.numpy as jnp
from jax import lax
from jax.experimental import pallas as pl
from jax.experimental.pallas import tpu as pltpu
from jax.sharding import PartitionSpec as P

HEADS = 64
KV_HEADS = 8
HEAD = 128
POS = 4
BLOCK = 128

MESH = pl.DeviceIdType.MESH

rope_base = 500000.0
neg_large = -1e30


def _barrier(peers):
    barrier = pltpu.get_barrier_semaphore()
    for device in peers:
        pl.semaphore_signal(barrier, inc=1, device_id=device, device_id_type=MESH)
    pl.semaphore_wait(barrier, len(peers))


def _send_all(axis, n, me, src_of, land, send_sem, recv_sem):
    copies = []
    for i in range(1, n):
        peer = lax.rem(me + i, n)
        copy = pltpu.make_async_remote_copy(
            src_ref=src_of(peer),
            dst_ref=land.at[me],
            send_sem=send_sem.at[peer],
            recv_sem=recv_sem.at[me],
            device_id={axis: peer},
            device_id_type=MESH,
        )
        copy.start()
        copies.append(copy)
    return copies


def _wait_all(axis, n, me, land, send_sem, recv_sem):
    for i in range(1, n):
        src = lax.rem(me + n - i, n)
        pltpu.make_async_remote_copy(
            src_ref=land.at[src],
            dst_ref=land.at[src],
            send_sem=send_sem.at[src],
            recv_sem=recv_sem.at[src],
            device_id={axis: src},
            device_id_type=MESH,
        ).wait_recv()


def _qkv_kernel(n, part_ref, cos_ref, sin_ref, out_ref, land_a, mine, land_b, sems):
    me = lax.axis_index("seq")
    land_a[me] = part_ref[me]
    _barrier([{"seq": lax.rem(me + i, n)} for i in range(1, n)])
    sent_a = _send_all("seq", n, me, lambda p: part_ref.at[p], land_a, sems.at[0], sems.at[1])
    _wait_all("seq", n, me, land_a, sems.at[0], sems.at[1])
    total = land_a[0]
    for i in range(1, n):
        total = total + land_a[i]
    turned = pltpu.roll(total, HEAD // 2, 1)
    rotated = (total * cos_ref[...] + turned * sin_ref[...]).astype(mine.dtype)
    mine[...] = rotated
    land_b[me] = rotated
    sent_b = _send_all("seq", n, me, lambda p: mine, land_b, sems.at[2], sems.at[3])
    _wait_all("seq", n, me, land_b, sems.at[2], sems.at[3])
    for copy in sent_a + sent_b:
        copy.wait_send()
    out_ref[...] = land_b[...]


def qkv_exchange(partial, cos_table, sin_table):
    n = partial.shape[0]
    return pl.pallas_call(
        functools.partial(_qkv_kernel, n),
        out_shape=jax.ShapeDtypeStruct(partial.shape, jnp.bfloat16),
        in_specs=[pl.BlockSpec(memory_space=pltpu.VMEM)] * 3,
        out_specs=pl.BlockSpec(memory_space=pltpu.VMEM),
        scratch_shapes=[
            pltpu.VMEM(partial.shape, jnp.float32),
            pltpu.VMEM(partial.shape[1:], jnp.bfloat16),
            pltpu.VMEM(partial.shape, jnp.bfloat16),
            pltpu.SemaphoreType.DMA((4, n)),
        ],
        compiler_params=pltpu.CompilerParams(collective_id=0, has_side_effects=True),
        cost_estimate=pl.CostEstimate(
            flops=0, bytes_accessed=partial.size * 12, transcendentals=0
        ),
    )(partial, cos_table, sin_table)


def _attend_kernel(
    n, m, rows, packed_ref, w_ref, out_ref, land_p, mine, land_a, part_c, land_c, sems
):
    me = lax.axis_index("seq")
    me_h = lax.axis_index("head")
    land_p[me] = packed_ref[me]
    _barrier(
        [{"seq": lax.rem(me + i, n)} for i in range(1, n)]
        + [{"head": lax.rem(me_h + i, m)} for i in range(1, m)]
    )
    sent_p = _send_all("seq", n, me, lambda p: packed_ref.at[p], land_p, sems.at[0], sems.at[1])
    _wait_all("seq", n, me, land_p, sems.at[0], sems.at[1])
    top = land_p[0, rows:, 0:1]
    for i in range(1, n):
        top = jnp.maximum(top, land_p[i, rows:, 0:1])
    numerator = jnp.zeros((rows, HEAD), jnp.float32)
    denominator = jnp.zeros((rows, 1), jnp.float32)
    for i in range(n):
        scale = jnp.exp(land_p[i, rows:, 0:1] - top)
        denominator = denominator + land_p[i, rows:, 1:2] * scale
        numerator = numerator + land_p[i, :rows] * scale
    attended = (numerator / denominator).astype(mine.dtype)
    mine[...] = attended
    land_a[me] = attended
    sent_a = _send_all("seq", n, me, lambda p: mine, land_a, sems.at[2], sems.at[3])
    _wait_all("seq", n, me, land_a, sems.at[2], sems.at[3])
    heads = n // 2
    projected = None
    for g in range(heads):
        lhs = land_a[2 * g : 2 * g + 2].reshape(2 * rows, HEAD)
        term = jnp.dot(lhs, w_ref[g * HEAD : (g + 1) * HEAD, :], preferred_element_type=jnp.float32)
        projected = term if projected is None else projected + term
    per = part_c.shape[1]
    for j in range(m):
        part_c[j] = projected[j * per : (j + 1) * per]
    land_c[me_h] = part_c[me_h]
    sent_c = _send_all("head", m, me_h, lambda p: part_c.at[p], land_c, sems.at[4], sems.at[5])
    _wait_all("head", m, me_h, land_c, sems.at[4], sems.at[5])
    total = land_c[0]
    for j in range(1, m):
        total = total + land_c[j]
    for copy in sent_p + sent_a + sent_c:
        copy.wait_send()
    out_ref[...] = total.astype(out_ref.dtype)


def attend_exchange(packed, out_weight, m):
    n, two_rows, _ = packed.shape
    rows = two_rows // 2
    width = out_weight.shape[1]
    per = 2 * rows // m
    return pl.pallas_call(
        functools.partial(_attend_kernel, n, m, rows),
        out_shape=jax.ShapeDtypeStruct((per, width), jnp.bfloat16),
        in_specs=[pl.BlockSpec(memory_space=pltpu.VMEM)] * 2,
        out_specs=pl.BlockSpec(memory_space=pltpu.VMEM),
        scratch_shapes=[
            pltpu.VMEM(packed.shape, jnp.float32),
            pltpu.VMEM((rows, HEAD), jnp.bfloat16),
            pltpu.VMEM((n, rows, HEAD), jnp.bfloat16),
            pltpu.VMEM((m, per, width), jnp.float32),
            pltpu.VMEM((m, per, width), jnp.float32),
            pltpu.SemaphoreType.DMA((6, max(n, m))),
        ],
        compiler_params=pltpu.CompilerParams(collective_id=1, has_side_effects=True),
        cost_estimate=pl.CostEstimate(
            flops=2 * 2 * rows * out_weight.shape[0] * width,
            bytes_accessed=packed.size * 8 + out_weight.size * 2,
            transcendentals=n * rows * HEAD,
        ),
    )(packed, out_weight)


def rotate(values, positions):
    half_width = values.shape[-1] // 2
    frequencies = rope_base ** (
        -(jnp.arange(half_width, dtype=jnp.float32) * 2.0 / values.shape[-1])
    )
    angles = positions[..., None] * frequencies
    cosine_table = jnp.cos(angles)
    sine_table = jnp.sin(angles)
    lower_half = values[..., :half_width]
    upper_half = values[..., half_width:]
    return jnp.concatenate(
        [
            lower_half * cosine_table - upper_half * sine_table,
            upper_half * cosine_table + lower_half * sine_table,
        ],
        axis=-1,
    )


def body(
    normed,
    qkv_weight,
    out_weight,
    kv_cache,
    lengths,
    slot_request,
    slot_block,
    send_list,
    recv_list,
):
    group_size = HEADS // KV_HEADS
    scale_factor = HEAD ** (-0.5)
    requests = lengths.shape[0]
    slot_count = kv_cache.shape[0]
    n_seq = lax.axis_size("seq")
    n_head = lax.axis_size("head")
    me_seq = lax.axis_index("seq")
    rows = normed.shape[0]
    rows_per = rows // n_seq
    groups = qkv_weight.shape[1] // HEAD

    partial = jnp.dot(normed, qkv_weight, preferred_element_type=jnp.float32)
    partial = partial.reshape(n_seq, rows_per * groups, HEAD)
    row_ids = me_seq * rows_per + jnp.arange(rows_per, dtype=jnp.int32)
    row_pos = (lengths[row_ids // POS] + row_ids % POS).astype(jnp.float32)
    half_width = HEAD // 2
    frequencies = rope_base ** (-(jnp.arange(half_width, dtype=jnp.float32) * 2.0 / HEAD))
    angles = row_pos[:, None] * frequencies
    cosine, sine = jnp.cos(angles), jnp.sin(angles)
    turned_groups = (jnp.arange(groups) <= group_size)[None, :, None]
    cos_table = jnp.where(
        turned_groups, jnp.concatenate([cosine, cosine], axis=-1)[:, None, :], 1.0
    ).reshape(rows_per * groups, HEAD)
    sin_table = jnp.where(
        turned_groups, jnp.concatenate([-sine, sine], axis=-1)[:, None, :], 0.0
    ).reshape(rows_per * groups, HEAD)
    qkv = qkv_exchange(partial, cos_table, sin_table).reshape(requests, POS, 1, groups, HEAD)
    local_kv = 1

    flat_send = send_list.reshape(-1)
    outgoing = jnp.where(
        (flat_send < slot_count)[:, None, None, None],
        kv_cache[jnp.minimum(flat_send, slot_count - 1)],
        jnp.zeros((), kv_cache.dtype),
    )
    outgoing = outgoing.reshape((lax.axis_size("seq"), -1) + kv_cache.shape[1:])
    outgoing, qkv = lax.optimization_barrier((outgoing, qkv))
    incoming = lax.all_to_all(outgoing, "seq", split_axis=0, concat_axis=0, tiled=True)
    incoming = incoming.reshape((-1,) + kv_cache.shape[1:])
    arrivals = incoming.shape[0]
    recv_flat = recv_list.reshape(-1)
    source_of = (
        jnp.full((slot_count + 1,), arrivals, jnp.int32)
        .at[recv_flat]
        .set(jnp.arange(arrivals, dtype=jnp.int32), mode="drop")[:slot_count]
    )
    zero_entry = jnp.argmax(recv_flat >= slot_count).astype(jnp.int32)
    moved_cache = incoming[jnp.where(source_of < arrivals, source_of, zero_entry)]
    queries = qkv[:, :, :, :group_size]
    keys_new = qkv[:, :, :, group_size]
    values_new = qkv[:, :, :, group_size + 1]

    slot_clip = jnp.minimum(slot_request, requests - 1)
    live_slot = slot_request < requests
    token_pos = slot_block[:, None] * BLOCK + jnp.arange(BLOCK, dtype=jnp.int32)[None, :]
    token_valid = (token_pos < lengths[slot_clip][:, None]) & live_slot[:, None]
    cache_view = kv_cache.reshape(slot_count, 2, BLOCK, local_kv, HEAD)
    gathered = queries[slot_clip]
    scores = (
        jnp.einsum(
            "sptgd,sbtd->stgpb", gathered, cache_view[:, 0], preferred_element_type=jnp.float32
        )
        * scale_factor
    )
    scores = jnp.where(token_valid[:, None, None, None, :], scores, neg_large)
    slot_max = jnp.max(scores, axis=-1)
    weights = jnp.where(
        token_valid[:, None, None, None, :], jnp.exp(scores - slot_max[..., None]), 0.0
    )
    slot_sum = jnp.sum(weights, axis=-1)
    slot_acc = jnp.einsum(
        "stgpb,sbtd->stgpd",
        weights.astype(jnp.bfloat16),
        cache_view[:, 1],
        preferred_element_type=jnp.float32,
    )
    flat_width = local_kv * group_size * POS
    slot_max_flat = slot_max.reshape(slot_count, flat_width)
    member = slot_request[:, None] == jnp.arange(requests, dtype=jnp.int32)[None, :]
    request_max = jnp.max(
        jnp.where(member[:, None, :], slot_max_flat[:, :, None], neg_large), axis=0
    ).T
    rescale = jnp.exp(slot_max_flat - request_max[slot_clip])
    member_float = member.astype(jnp.float32).T
    request_sum = jnp.dot(
        member_float,
        slot_sum.reshape(slot_count, flat_width) * rescale,
        precision=lax.Precision.HIGHEST,
    )
    scaled_acc = (slot_acc.reshape(slot_count, flat_width, HEAD) * rescale[:, :, None]).reshape(
        slot_count, flat_width * HEAD
    )
    request_acc = jnp.dot(member_float, scaled_acc, precision=lax.Precision.HIGHEST).reshape(
        requests, flat_width, HEAD
    )

    new_scores = (
        jnp.einsum("rptgd,rqtd->rtgpq", queries, keys_new, preferred_element_type=jnp.float32)
        * scale_factor
    )
    causal = jnp.arange(POS)[:, None] >= jnp.arange(POS)[None, :]
    new_scores = jnp.where(causal, new_scores, neg_large)
    new_max = jnp.max(new_scores, axis=-1)
    new_weights = jnp.where(causal, jnp.exp(new_scores - new_max[..., None]), 0.0)
    new_sum = jnp.sum(new_weights, axis=-1).reshape(requests, flat_width)
    new_acc = jnp.einsum(
        "rtgpq,rqtd->rtgpd",
        new_weights.astype(jnp.bfloat16),
        values_new,
        preferred_element_type=jnp.float32,
    ).reshape(requests, flat_width, HEAD)
    first = me_seq == 0
    new_max = jnp.where(first, new_max.reshape(requests, flat_width), neg_large)
    new_sum = jnp.where(first, new_sum, 0.0)
    new_acc = jnp.where(first, new_acc, 0.0)
    part_max = jnp.maximum(request_max, new_max)
    keep_old = jnp.exp(request_max - part_max)
    keep_new = jnp.exp(new_max - part_max)
    part_sum = request_sum * keep_old + new_sum * keep_new
    part_acc = request_acc * keep_old[..., None] + new_acc * keep_new[..., None]

    def by_chunk(values):
        lead = values.reshape(2, requests // 2, group_size, POS, -1).transpose(2, 0, 1, 3, 4)
        return lead.reshape(n_seq, requests * group_size * POS // n_seq, -1)

    chunk_rows = requests * flat_width // n_seq
    stats = jnp.concatenate(
        [
            by_chunk(part_max),
            by_chunk(part_sum),
            jnp.zeros((n_seq, chunk_rows, HEAD - 2), jnp.float32),
        ],
        axis=-1,
    )
    packed = jnp.concatenate([by_chunk(part_acc), stats], axis=1)
    projected = attend_exchange(packed, out_weight, n_head)
    return (projected, moved_cache)


def solution(mesh):
    placed = (
        P(None, "seq"),
        P("seq", "head"),
        P("head", "seq"),
        P("seq", None, None, "head"),
        P(),
        P("seq"),
        P("seq"),
        P("seq", None, None),
        P("seq", None, None),
    )
    return jax.shard_map(
        body,
        mesh=mesh,
        in_specs=placed,
        out_specs=(P("head", "seq"), P("seq", None, None, "head")),
        check_vma=False,
    )
```

```python
import functools

import jax
import jax.numpy as jnp
from jax import lax
from jax.experimental import pallas as pl
from jax.experimental.pallas import tpu as pltpu
from jax.sharding import PartitionSpec as P

HEADS = 64
KV_HEADS = 8
HEAD = 128
POS = 4
BLOCK = 128

MESH = pl.DeviceIdType.MESH

rope_base = 500000.0
neg_large = -1e30


def _barrier(peers):
    barrier = pltpu.get_barrier_semaphore()
    for device in peers:
        pl.semaphore_signal(barrier, inc=1, device_id=device, device_id_type=MESH)
    pl.semaphore_wait(barrier, len(peers))


def _send_all(axis, n, me, src_of, land, send_sem, recv_sem):
    copies = []
    for i in range(1, n):
        peer = lax.rem(me + i, n)
        copy = pltpu.make_async_remote_copy(
            src_ref=src_of(peer),
            dst_ref=land.at[me],
            send_sem=send_sem.at[peer],
            recv_sem=recv_sem.at[me],
            device_id={axis: peer},
            device_id_type=MESH,
        )
        copy.start()
        copies.append(copy)
    return copies


def _wait_all(axis, n, me, land, send_sem, recv_sem):
    for i in range(1, n):
        src = lax.rem(me + n - i, n)
        pltpu.make_async_remote_copy(
            src_ref=land.at[src],
            dst_ref=land.at[src],
            send_sem=send_sem.at[src],
            recv_sem=recv_sem.at[src],
            device_id={axis: src},
            device_id_type=MESH,
        ).wait_recv()


def _qkv_kernel(n, part_ref, cos_ref, sin_ref, out_ref, land_a, mine, land_b, sems):
    me = lax.axis_index("seq")
    land_a[me] = part_ref[me]
    _barrier([{"seq": lax.rem(me + i, n)} for i in range(1, n)])
    sent_a = _send_all("seq", n, me, lambda p: part_ref.at[p], land_a, sems.at[0], sems.at[1])
    _wait_all("seq", n, me, land_a, sems.at[0], sems.at[1])
    total = land_a[0]
    for i in range(1, n):
        total = total + land_a[i]
    turned = pltpu.roll(total, HEAD // 2, 1)
    rotated = (total * cos_ref[...] + turned * sin_ref[...]).astype(mine.dtype)
    mine[...] = rotated
    land_b[me] = rotated
    sent_b = _send_all("seq", n, me, lambda p: mine, land_b, sems.at[2], sems.at[3])
    _wait_all("seq", n, me, land_b, sems.at[2], sems.at[3])
    for copy in sent_a + sent_b:
        copy.wait_send()
    out_ref[...] = land_b[...]


def qkv_exchange(partial, cos_table, sin_table):
    n = partial.shape[0]
    return pl.pallas_call(
        functools.partial(_qkv_kernel, n),
        out_shape=jax.ShapeDtypeStruct(partial.shape, jnp.bfloat16),
        in_specs=[pl.BlockSpec(memory_space=pltpu.VMEM)] * 3,
        out_specs=pl.BlockSpec(memory_space=pltpu.VMEM),
        scratch_shapes=[
            pltpu.VMEM(partial.shape, jnp.float32),
            pltpu.VMEM(partial.shape[1:], jnp.bfloat16),
            pltpu.VMEM(partial.shape, jnp.bfloat16),
            pltpu.SemaphoreType.DMA((4, n)),
        ],
        compiler_params=pltpu.CompilerParams(collective_id=0, has_side_effects=True),
        cost_estimate=pl.CostEstimate(
            flops=0, bytes_accessed=partial.size * 12, transcendentals=0
        ),
    )(partial, cos_table, sin_table)


def _attend_kernel(
    n, m, rows, packed_ref, w_ref, out_ref, land_p, mine, land_a, part_c, land_c, sems
):
    me = lax.axis_index("seq")
    me_h = lax.axis_index("head")
    land_p[me] = packed_ref[me]
    _barrier(
        [{"seq": lax.rem(me + i, n)} for i in range(1, n)]
        + [{"head": lax.rem(me_h + i, m)} for i in range(1, m)]
    )
    sent_p = _send_all("seq", n, me, lambda p: packed_ref.at[p], land_p, sems.at[0], sems.at[1])
    _wait_all("seq", n, me, land_p, sems.at[0], sems.at[1])
    top = land_p[0, rows:, 0:1]
    for i in range(1, n):
        top = jnp.maximum(top, land_p[i, rows:, 0:1])
    numerator = jnp.zeros((rows, HEAD), jnp.float32)
    denominator = jnp.zeros((rows, 1), jnp.float32)
    for i in range(n):
        scale = jnp.exp(land_p[i, rows:, 0:1] - top)
        denominator = denominator + land_p[i, rows:, 1:2] * scale
        numerator = numerator + land_p[i, :rows] * scale
    attended = (numerator / denominator).astype(mine.dtype)
    mine[...] = attended
    land_a[me] = attended
    sent_a = _send_all("seq", n, me, lambda p: mine, land_a, sems.at[2], sems.at[3])
    _wait_all("seq", n, me, land_a, sems.at[2], sems.at[3])
    heads = n // 2
    projected = None
    for g in range(heads):
        lhs = land_a[2 * g : 2 * g + 2].reshape(2 * rows, HEAD)
        term = jnp.dot(lhs, w_ref[g * HEAD : (g + 1) * HEAD, :], preferred_element_type=jnp.float32)
        projected = term if projected is None else projected + term
    per = part_c.shape[1]
    for j in range(m):
        part_c[j] = projected[j * per : (j + 1) * per]
    land_c[me_h] = part_c[me_h]
    sent_c = _send_all("head", m, me_h, lambda p: part_c.at[p], land_c, sems.at[4], sems.at[5])
    _wait_all("head", m, me_h, land_c, sems.at[4], sems.at[5])
    total = land_c[0]
    for j in range(1, m):
        total = total + land_c[j]
    for copy in sent_p + sent_a + sent_c:
        copy.wait_send()
    out_ref[...] = total.astype(out_ref.dtype)


def attend_exchange(packed, out_weight, m):
    n, two_rows, _ = packed.shape
    rows = two_rows // 2
    width = out_weight.shape[1]
    per = 2 * rows // m
    return pl.pallas_call(
        functools.partial(_attend_kernel, n, m, rows),
        out_shape=jax.ShapeDtypeStruct((per, width), jnp.bfloat16),
        in_specs=[pl.BlockSpec(memory_space=pltpu.VMEM)] * 2,
        out_specs=pl.BlockSpec(memory_space=pltpu.VMEM),
        scratch_shapes=[
            pltpu.VMEM(packed.shape, jnp.float32),
            pltpu.VMEM((rows, HEAD), jnp.bfloat16),
            pltpu.VMEM((n, rows, HEAD), jnp.bfloat16),
            pltpu.VMEM((m, per, width), jnp.float32),
            pltpu.VMEM((m, per, width), jnp.float32),
            pltpu.SemaphoreType.DMA((6, max(n, m))),
        ],
        compiler_params=pltpu.CompilerParams(collective_id=1, has_side_effects=True),
        cost_estimate=pl.CostEstimate(
            flops=2 * 2 * rows * out_weight.shape[0] * width,
            bytes_accessed=packed.size * 8 + out_weight.size * 2,
            transcendentals=n * rows * HEAD,
        ),
    )(packed, out_weight)


def _pick_kernel(limit, index_ref, src_hbm, out_hbm, buf, sems, out_sem):
    count = buf.shape[0]

    def start(j, carry):
        k = index_ref[j]

        @pl.when(k < limit)
        def _():
            pltpu.make_async_copy(src_hbm.at[jnp.minimum(k, limit - 1)], buf.at[j], sems.at[j]).start()

        @pl.when(k >= limit)
        def _():
            buf[j] = jnp.zeros(buf.shape[1:], buf.dtype)

        return carry

    def finish(j, carry):
        k = index_ref[j]

        @pl.when(k < limit)
        def _():
            pltpu.make_async_copy(src_hbm.at[0], buf.at[j], sems.at[j]).wait()

        return carry

    lax.fori_loop(0, count, start, 0)
    lax.fori_loop(0, count, finish, 0)
    out = pltpu.make_async_copy(buf, out_hbm, out_sem)
    out.start()
    out.wait()


def pick_blocks(index, source, limit):
    count = index.shape[0]
    shape = (count,) + source.shape[1:]
    nbytes = count * source[0].size * source.dtype.itemsize
    return pl.pallas_call(
        functools.partial(_pick_kernel, limit),
        out_shape=jax.ShapeDtypeStruct(shape, source.dtype),
        in_specs=[
            pl.BlockSpec(memory_space=pltpu.SMEM),
            pl.BlockSpec(memory_space=pl.ANY),
        ],
        out_specs=pl.BlockSpec(memory_space=pl.ANY),
        scratch_shapes=[
            pltpu.VMEM(shape, source.dtype),
            pltpu.SemaphoreType.DMA((count,)),
            pltpu.SemaphoreType.DMA(()),
        ],
        cost_estimate=pl.CostEstimate(flops=0, bytes_accessed=2 * nbytes, transcendentals=0),
    )(index, source)


def rotate(values, positions):
    half_width = values.shape[-1] // 2
    frequencies = rope_base ** (
        -(jnp.arange(half_width, dtype=jnp.float32) * 2.0 / values.shape[-1])
    )
    angles = positions[..., None] * frequencies
    cosine_table = jnp.cos(angles)
    sine_table = jnp.sin(angles)
    lower_half = values[..., :half_width]
    upper_half = values[..., half_width:]
    return jnp.concatenate(
        [
            lower_half * cosine_table - upper_half * sine_table,
            upper_half * cosine_table + lower_half * sine_table,
        ],
        axis=-1,
    )


def body(
    normed,
    qkv_weight,
    out_weight,
    kv_cache,
    lengths,
    slot_request,
    slot_block,
    send_list,
    recv_list,
):
    group_size = HEADS // KV_HEADS
    scale_factor = HEAD ** (-0.5)
    requests = lengths.shape[0]
    slot_count = kv_cache.shape[0]
    n_seq = lax.axis_size("seq")
    n_head = lax.axis_size("head")
    me_seq = lax.axis_index("seq")
    rows = normed.shape[0]
    rows_per = rows // n_seq
    groups = qkv_weight.shape[1] // HEAD

    partial = jnp.dot(normed, qkv_weight, preferred_element_type=jnp.float32)
    partial = partial.reshape(n_seq, rows_per * groups, HEAD)
    row_ids = me_seq * rows_per + jnp.arange(rows_per, dtype=jnp.int32)
    row_pos = (lengths[row_ids // POS] + row_ids % POS).astype(jnp.float32)
    half_width = HEAD // 2
    frequencies = rope_base ** (-(jnp.arange(half_width, dtype=jnp.float32) * 2.0 / HEAD))
    angles = row_pos[:, None] * frequencies
    cosine, sine = jnp.cos(angles), jnp.sin(angles)
    turned_groups = (jnp.arange(groups) <= group_size)[None, :, None]
    cos_table = jnp.where(
        turned_groups, jnp.concatenate([cosine, cosine], axis=-1)[:, None, :], 1.0
    ).reshape(rows_per * groups, HEAD)
    sin_table = jnp.where(
        turned_groups, jnp.concatenate([-sine, sine], axis=-1)[:, None, :], 0.0
    ).reshape(rows_per * groups, HEAD)
    qkv = qkv_exchange(partial, cos_table, sin_table).reshape(requests, POS, 1, groups, HEAD)
    local_kv = 1

    flat_send = send_list.reshape(-1)
    outgoing = pick_blocks(jnp.minimum(flat_send, slot_count - 1), kv_cache, slot_count)
    outgoing = outgoing.reshape((lax.axis_size("seq"), -1) + kv_cache.shape[1:])
    outgoing, qkv = lax.optimization_barrier((outgoing, qkv))
    incoming = lax.all_to_all(outgoing, "seq", split_axis=0, concat_axis=0, tiled=True)
    incoming = incoming.reshape((-1,) + kv_cache.shape[1:])
    arrivals = incoming.shape[0]
    source_of = (
        jnp.full((slot_count + 1,), arrivals, jnp.int32)
        .at[recv_list.reshape(-1)]
        .set(jnp.arange(arrivals, dtype=jnp.int32), mode="drop")[:slot_count]
    )
    moved_cache = pick_blocks(source_of, incoming, arrivals)
    queries = qkv[:, :, :, :group_size]
    keys_new = qkv[:, :, :, group_size]
    values_new = qkv[:, :, :, group_size + 1]

    slot_clip = jnp.minimum(slot_request, requests - 1)
    live_slot = slot_request < requests
    token_pos = slot_block[:, None] * BLOCK + jnp.arange(BLOCK, dtype=jnp.int32)[None, :]
    token_valid = (token_pos < lengths[slot_clip][:, None]) & live_slot[:, None]
    cache_view = kv_cache.reshape(slot_count, 2, BLOCK, local_kv, HEAD)
    gathered = queries[slot_clip]
    scores = (
        jnp.einsum(
            "sptgd,sbtd->stgpb", gathered, cache_view[:, 0], preferred_element_type=jnp.float32
        )
        * scale_factor
    )
    scores = jnp.where(token_valid[:, None, None, None, :], scores, neg_large)
    slot_max = jnp.max(scores, axis=-1)
    weights = jnp.where(
        token_valid[:, None, None, None, :], jnp.exp(scores - slot_max[..., None]), 0.0
    )
    slot_sum = jnp.sum(weights, axis=-1)
    slot_acc = jnp.einsum(
        "stgpb,sbtd->stgpd",
        weights.astype(jnp.bfloat16),
        cache_view[:, 1],
        preferred_element_type=jnp.float32,
    )
    flat_width = local_kv * group_size * POS
    slot_max_flat = slot_max.reshape(slot_count, flat_width)
    member = slot_request[:, None] == jnp.arange(requests, dtype=jnp.int32)[None, :]
    request_max = jnp.max(
        jnp.where(member[:, None, :], slot_max_flat[:, :, None], neg_large), axis=0
    ).T
    rescale = jnp.exp(slot_max_flat - request_max[slot_clip])
    member_float = member.astype(jnp.float32).T
    request_sum = jnp.dot(
        member_float,
        slot_sum.reshape(slot_count, flat_width) * rescale,
        precision=lax.Precision.HIGHEST,
    )
    scaled_acc = (slot_acc.reshape(slot_count, flat_width, HEAD) * rescale[:, :, None]).reshape(
        slot_count, flat_width * HEAD
    )
    request_acc = jnp.dot(member_float, scaled_acc, precision=lax.Precision.HIGHEST).reshape(
        requests, flat_width, HEAD
    )

    new_scores = (
        jnp.einsum("rptgd,rqtd->rtgpq", queries, keys_new, preferred_element_type=jnp.float32)
        * scale_factor
    )
    causal = jnp.arange(POS)[:, None] >= jnp.arange(POS)[None, :]
    new_scores = jnp.where(causal, new_scores, neg_large)
    new_max = jnp.max(new_scores, axis=-1)
    new_weights = jnp.where(causal, jnp.exp(new_scores - new_max[..., None]), 0.0)
    new_sum = jnp.sum(new_weights, axis=-1).reshape(requests, flat_width)
    new_acc = jnp.einsum(
        "rtgpq,rqtd->rtgpd",
        new_weights.astype(jnp.bfloat16),
        values_new,
        preferred_element_type=jnp.float32,
    ).reshape(requests, flat_width, HEAD)
    first = me_seq == 0
    new_max = jnp.where(first, new_max.reshape(requests, flat_width), neg_large)
    new_sum = jnp.where(first, new_sum, 0.0)
    new_acc = jnp.where(first, new_acc, 0.0)
    part_max = jnp.maximum(request_max, new_max)
    keep_old = jnp.exp(request_max - part_max)
    keep_new = jnp.exp(new_max - part_max)
    part_sum = request_sum * keep_old + new_sum * keep_new
    part_acc = request_acc * keep_old[..., None] + new_acc * keep_new[..., None]

    def by_chunk(values):
        lead = values.reshape(2, requests // 2, group_size, POS, -1).transpose(2, 0, 1, 3, 4)
        return lead.reshape(n_seq, requests * group_size * POS // n_seq, -1)

    chunk_rows = requests * flat_width // n_seq
    stats = jnp.concatenate(
        [
            by_chunk(part_max),
            by_chunk(part_sum),
            jnp.zeros((n_seq, chunk_rows, HEAD - 2), jnp.float32),
        ],
        axis=-1,
    )
    packed = jnp.concatenate([by_chunk(part_acc), stats], axis=1)
    projected = attend_exchange(packed, out_weight, n_head)
    return (projected, moved_cache)


def solution(mesh):
    placed = (
        P(None, "seq"),
        P("seq", "head"),
        P("head", "seq"),
        P("seq", None, None, "head"),
        P(),
        P("seq"),
        P("seq"),
        P("seq", None, None),
        P("seq", None, None),
    )
    return jax.shard_map(
        body,
        mesh=mesh,
        in_specs=placed,
        out_specs=(P("head", "seq"), P("seq", None, None, "head")),
        check_vma=False,
    )
```

```python
import functools

import jax
import jax.numpy as jnp
from jax import lax
from jax.experimental import pallas as pl
from jax.experimental.pallas import tpu as pltpu
from jax.sharding import PartitionSpec as P

HEADS = 64
KV_HEADS = 8
HEAD = 128
POS = 4
BLOCK = 128

MESH = pl.DeviceIdType.MESH

rope_base = 500000.0
neg_large = -1e30


def _barrier(peers):
    barrier = pltpu.get_barrier_semaphore()
    for device in peers:
        pl.semaphore_signal(barrier, inc=1, device_id=device, device_id_type=MESH)
    pl.semaphore_wait(barrier, len(peers))


def _send_all(axis, n, me, src_of, land, send_sem, recv_sem):
    copies = []
    for i in range(1, n):
        peer = lax.rem(me + i, n)
        copy = pltpu.make_async_remote_copy(
            src_ref=src_of(peer),
            dst_ref=land.at[me],
            send_sem=send_sem.at[peer],
            recv_sem=recv_sem.at[me],
            device_id={axis: peer},
            device_id_type=MESH,
        )
        copy.start()
        copies.append(copy)
    return copies


def _wait_all(axis, n, me, land, send_sem, recv_sem):
    for i in range(1, n):
        src = lax.rem(me + n - i, n)
        pltpu.make_async_remote_copy(
            src_ref=land.at[src],
            dst_ref=land.at[src],
            send_sem=send_sem.at[src],
            recv_sem=recv_sem.at[src],
            device_id={axis: src},
            device_id_type=MESH,
        ).wait_recv()


def _qkv_kernel(
    n, limit, part_ref, cos_ref, sin_ref, pick_ref, kv_hbm, out_ref, sent_hbm,
    land_a, mine, land_b, sems, kv_vmem, sent_vmem, local_sems,
):
    me = lax.axis_index("seq")
    kv_in = pltpu.make_async_copy(kv_hbm, kv_vmem, local_sems.at[0])
    kv_in.start()
    land_a[me] = part_ref[me]
    _barrier([{"seq": lax.rem(me + i, n)} for i in range(1, n)])
    sent_a = _send_all("seq", n, me, lambda p: part_ref.at[p], land_a, sems.at[0], sems.at[1])
    kv_in.wait()

    def pick(j, carry):
        sent_vmem[j] = kv_vmem[jnp.minimum(pick_ref[j], limit - 1)]
        return carry

    lax.fori_loop(0, sent_vmem.shape[0], pick, 0)
    kv_out = pltpu.make_async_copy(sent_vmem, sent_hbm, local_sems.at[1])
    kv_out.start()
    _wait_all("seq", n, me, land_a, sems.at[0], sems.at[1])
    total = land_a[0]
    for i in range(1, n):
        total = total + land_a[i]
    turned = pltpu.roll(total, HEAD // 2, 1)
    rotated = (total * cos_ref[...] + turned * sin_ref[...]).astype(mine.dtype)
    mine[...] = rotated
    land_b[me] = rotated
    sent_b = _send_all("seq", n, me, lambda p: mine, land_b, sems.at[2], sems.at[3])
    _wait_all("seq", n, me, land_b, sems.at[2], sems.at[3])
    for copy in sent_a + sent_b:
        copy.wait_send()
    out_ref[...] = land_b[...]
    kv_out.wait()


def qkv_exchange(partial, cos_table, sin_table, pick, kv_cache):
    n = partial.shape[0]
    picked = (pick.shape[0],) + kv_cache.shape[1:]
    return pl.pallas_call(
        functools.partial(_qkv_kernel, n, kv_cache.shape[0]),
        out_shape=(
            jax.ShapeDtypeStruct(partial.shape, jnp.bfloat16),
            jax.ShapeDtypeStruct(picked, kv_cache.dtype),
        ),
        in_specs=[pl.BlockSpec(memory_space=pltpu.VMEM)] * 3
        + [pl.BlockSpec(memory_space=pltpu.SMEM), pl.BlockSpec(memory_space=pl.ANY)],
        out_specs=(pl.BlockSpec(memory_space=pltpu.VMEM), pl.BlockSpec(memory_space=pl.ANY)),
        scratch_shapes=[
            pltpu.VMEM(partial.shape, jnp.float32),
            pltpu.VMEM(partial.shape[1:], jnp.bfloat16),
            pltpu.VMEM(partial.shape, jnp.bfloat16),
            pltpu.SemaphoreType.DMA((4, n)),
            pltpu.VMEM(kv_cache.shape, kv_cache.dtype),
            pltpu.VMEM(picked, kv_cache.dtype),
            pltpu.SemaphoreType.DMA((2,)),
        ],
        compiler_params=pltpu.CompilerParams(collective_id=0, has_side_effects=True),
        cost_estimate=pl.CostEstimate(
            flops=0,
            bytes_accessed=partial.size * 12 + 2 * kv_cache.size * kv_cache.dtype.itemsize,
            transcendentals=0,
        ),
    )(partial, cos_table, sin_table, pick, kv_cache)


def _attend_kernel(
    n, m, rows, packed_ref, w_ref, out_ref, land_p, mine, land_a, part_c, land_c, sems
):
    me = lax.axis_index("seq")
    me_h = lax.axis_index("head")
    land_p[me] = packed_ref[me]
    _barrier(
        [{"seq": lax.rem(me + i, n)} for i in range(1, n)]
        + [{"head": lax.rem(me_h + i, m)} for i in range(1, m)]
    )
    sent_p = _send_all("seq", n, me, lambda p: packed_ref.at[p], land_p, sems.at[0], sems.at[1])
    _wait_all("seq", n, me, land_p, sems.at[0], sems.at[1])
    top = land_p[0, rows:, 0:1]
    for i in range(1, n):
        top = jnp.maximum(top, land_p[i, rows:, 0:1])
    numerator = jnp.zeros((rows, HEAD), jnp.float32)
    denominator = jnp.zeros((rows, 1), jnp.float32)
    for i in range(n):
        scale = jnp.exp(land_p[i, rows:, 0:1] - top)
        denominator = denominator + land_p[i, rows:, 1:2] * scale
        numerator = numerator + land_p[i, :rows] * scale
    attended = (numerator / denominator).astype(mine.dtype)
    mine[...] = attended
    land_a[me] = attended
    sent_a = _send_all("seq", n, me, lambda p: mine, land_a, sems.at[2], sems.at[3])
    _wait_all("seq", n, me, land_a, sems.at[2], sems.at[3])
    heads = n // 2
    projected = None
    for g in range(heads):
        lhs = land_a[2 * g : 2 * g + 2].reshape(2 * rows, HEAD)
        term = jnp.dot(lhs, w_ref[g * HEAD : (g + 1) * HEAD, :], preferred_element_type=jnp.float32)
        projected = term if projected is None else projected + term
    per = part_c.shape[1]
    for j in range(m):
        part_c[j] = projected[j * per : (j + 1) * per]
    land_c[me_h] = part_c[me_h]
    sent_c = _send_all("head", m, me_h, lambda p: part_c.at[p], land_c, sems.at[4], sems.at[5])
    _wait_all("head", m, me_h, land_c, sems.at[4], sems.at[5])
    total = land_c[0]
    for j in range(1, m):
        total = total + land_c[j]
    for copy in sent_p + sent_a + sent_c:
        copy.wait_send()
    out_ref[...] = total.astype(out_ref.dtype)


def attend_exchange(packed, out_weight, m):
    n, two_rows, _ = packed.shape
    rows = two_rows // 2
    width = out_weight.shape[1]
    per = 2 * rows // m
    return pl.pallas_call(
        functools.partial(_attend_kernel, n, m, rows),
        out_shape=jax.ShapeDtypeStruct((per, width), jnp.bfloat16),
        in_specs=[pl.BlockSpec(memory_space=pltpu.VMEM)] * 2,
        out_specs=pl.BlockSpec(memory_space=pltpu.VMEM),
        scratch_shapes=[
            pltpu.VMEM(packed.shape, jnp.float32),
            pltpu.VMEM((rows, HEAD), jnp.bfloat16),
            pltpu.VMEM((n, rows, HEAD), jnp.bfloat16),
            pltpu.VMEM((m, per, width), jnp.float32),
            pltpu.VMEM((m, per, width), jnp.float32),
            pltpu.SemaphoreType.DMA((6, max(n, m))),
        ],
        compiler_params=pltpu.CompilerParams(collective_id=1, has_side_effects=True),
        cost_estimate=pl.CostEstimate(
            flops=2 * 2 * rows * out_weight.shape[0] * width,
            bytes_accessed=packed.size * 8 + out_weight.size * 2,
            transcendentals=n * rows * HEAD,
        ),
    )(packed, out_weight)


def _pick_kernel(limit, index_ref, src_hbm, out_hbm, buf, sems, out_sem):
    count = buf.shape[0]

    def start(j, carry):
        k = index_ref[j]

        @pl.when(k < limit)
        def _():
            pltpu.make_async_copy(src_hbm.at[jnp.minimum(k, limit - 1)], buf.at[j], sems.at[j]).start()

        @pl.when(k >= limit)
        def _():
            buf[j] = jnp.zeros(buf.shape[1:], buf.dtype)

        return carry

    def send(j, carry):
        k = index_ref[j]

        @pl.when(k < limit)
        def _():
            pltpu.make_async_copy(src_hbm.at[0], buf.at[j], sems.at[j]).wait()

        pltpu.make_async_copy(buf.at[j], out_hbm.at[j], out_sem.at[j]).start()
        return carry

    def finish(j, carry):
        pltpu.make_async_copy(buf.at[j], out_hbm.at[j], out_sem.at[j]).wait()
        return carry

    lax.fori_loop(0, count, start, 0)
    lax.fori_loop(0, count, send, 0)
    lax.fori_loop(0, count, finish, 0)


def pick_blocks(index, source, limit):
    count = index.shape[0]
    shape = (count,) + source.shape[1:]
    nbytes = count * source[0].size * source.dtype.itemsize
    return pl.pallas_call(
        functools.partial(_pick_kernel, limit),
        out_shape=jax.ShapeDtypeStruct(shape, source.dtype),
        in_specs=[
            pl.BlockSpec(memory_space=pltpu.SMEM),
            pl.BlockSpec(memory_space=pl.ANY),
        ],
        out_specs=pl.BlockSpec(memory_space=pl.ANY),
        scratch_shapes=[
            pltpu.VMEM(shape, source.dtype),
            pltpu.SemaphoreType.DMA((count,)),
            pltpu.SemaphoreType.DMA((count,)),
        ],
        cost_estimate=pl.CostEstimate(flops=0, bytes_accessed=2 * nbytes, transcendentals=0),
    )(index, source)


def rotate(values, positions):
    half_width = values.shape[-1] // 2
    frequencies = rope_base ** (
        -(jnp.arange(half_width, dtype=jnp.float32) * 2.0 / values.shape[-1])
    )
    angles = positions[..., None] * frequencies
    cosine_table = jnp.cos(angles)
    sine_table = jnp.sin(angles)
    lower_half = values[..., :half_width]
    upper_half = values[..., half_width:]
    return jnp.concatenate(
        [
            lower_half * cosine_table - upper_half * sine_table,
            upper_half * cosine_table + lower_half * sine_table,
        ],
        axis=-1,
    )


def body(
    normed,
    qkv_weight,
    out_weight,
    kv_cache,
    lengths,
    slot_request,
    slot_block,
    send_list,
    recv_list,
):
    group_size = HEADS // KV_HEADS
    scale_factor = HEAD ** (-0.5)
    requests = lengths.shape[0]
    slot_count = kv_cache.shape[0]
    n_seq = lax.axis_size("seq")
    n_head = lax.axis_size("head")
    me_seq = lax.axis_index("seq")
    rows = normed.shape[0]
    rows_per = rows // n_seq
    groups = qkv_weight.shape[1] // HEAD

    partial = jnp.dot(normed, qkv_weight, preferred_element_type=jnp.float32)
    partial = partial.reshape(n_seq, rows_per * groups, HEAD)
    row_ids = me_seq * rows_per + jnp.arange(rows_per, dtype=jnp.int32)
    row_pos = (lengths[row_ids // POS] + row_ids % POS).astype(jnp.float32)
    half_width = HEAD // 2
    frequencies = rope_base ** (-(jnp.arange(half_width, dtype=jnp.float32) * 2.0 / HEAD))
    angles = row_pos[:, None] * frequencies
    cosine, sine = jnp.cos(angles), jnp.sin(angles)
    turned_groups = (jnp.arange(groups) <= group_size)[None, :, None]
    cos_table = jnp.where(
        turned_groups, jnp.concatenate([cosine, cosine], axis=-1)[:, None, :], 1.0
    ).reshape(rows_per * groups, HEAD)
    sin_table = jnp.where(
        turned_groups, jnp.concatenate([-sine, sine], axis=-1)[:, None, :], 0.0
    ).reshape(rows_per * groups, HEAD)
    qkv, outgoing = qkv_exchange(partial, cos_table, sin_table, send_list.reshape(-1), kv_cache)
    qkv = qkv.reshape(requests, POS, 1, groups, HEAD)
    local_kv = 1

    outgoing = outgoing.reshape((lax.axis_size("seq"), -1) + kv_cache.shape[1:])
    incoming = lax.all_to_all(outgoing, "seq", split_axis=0, concat_axis=0, tiled=True)
    incoming = incoming.reshape((-1,) + kv_cache.shape[1:])
    arrivals = incoming.shape[0]
    source_of = (
        jnp.full((slot_count + 1,), arrivals, jnp.int32)
        .at[recv_list.reshape(-1)]
        .set(jnp.arange(arrivals, dtype=jnp.int32), mode="drop")[:slot_count]
    )
    moved_cache = pick_blocks(source_of, incoming, arrivals)
    queries = qkv[:, :, :, :group_size]
    keys_new = qkv[:, :, :, group_size]
    values_new = qkv[:, :, :, group_size + 1]

    slot_clip = jnp.minimum(slot_request, requests - 1)
    live_slot = slot_request < requests
    token_pos = slot_block[:, None] * BLOCK + jnp.arange(BLOCK, dtype=jnp.int32)[None, :]
    token_valid = (token_pos < lengths[slot_clip][:, None]) & live_slot[:, None]
    cache_view = kv_cache.reshape(slot_count, 2, BLOCK, local_kv, HEAD)
    gathered = queries[slot_clip]
    scores = (
        jnp.einsum(
            "sptgd,sbtd->stgpb", gathered, cache_view[:, 0], preferred_element_type=jnp.float32
        )
        * scale_factor
    )
    scores = jnp.where(token_valid[:, None, None, None, :], scores, neg_large)
    slot_max = jnp.max(scores, axis=-1)
    weights = jnp.where(
        token_valid[:, None, None, None, :], jnp.exp(scores - slot_max[..., None]), 0.0
    )
    slot_sum = jnp.sum(weights, axis=-1)
    slot_acc = jnp.einsum(
        "stgpb,sbtd->stgpd",
        weights.astype(jnp.bfloat16),
        cache_view[:, 1],
        preferred_element_type=jnp.float32,
    )
    flat_width = local_kv * group_size * POS
    slot_max_flat = slot_max.reshape(slot_count, flat_width)
    member = slot_request[:, None] == jnp.arange(requests, dtype=jnp.int32)[None, :]
    request_max = jnp.max(
        jnp.where(member[:, None, :], slot_max_flat[:, :, None], neg_large), axis=0
    ).T
    rescale = jnp.exp(slot_max_flat - request_max[slot_clip])
    member_float = member.astype(jnp.float32).T
    request_sum = jnp.dot(
        member_float,
        slot_sum.reshape(slot_count, flat_width) * rescale,
        precision=lax.Precision.HIGHEST,
    )
    scaled_acc = (slot_acc.reshape(slot_count, flat_width, HEAD) * rescale[:, :, None]).reshape(
        slot_count, flat_width * HEAD
    )
    request_acc = jnp.dot(member_float, scaled_acc, precision=lax.Precision.HIGHEST).reshape(
        requests, flat_width, HEAD
    )

    new_scores = (
        jnp.einsum("rptgd,rqtd->rtgpq", queries, keys_new, preferred_element_type=jnp.float32)
        * scale_factor
    )
    causal = jnp.arange(POS)[:, None] >= jnp.arange(POS)[None, :]
    new_scores = jnp.where(causal, new_scores, neg_large)
    new_max = jnp.max(new_scores, axis=-1)
    new_weights = jnp.where(causal, jnp.exp(new_scores - new_max[..., None]), 0.0)
    new_sum = jnp.sum(new_weights, axis=-1).reshape(requests, flat_width)
    new_acc = jnp.einsum(
        "rtgpq,rqtd->rtgpd",
        new_weights.astype(jnp.bfloat16),
        values_new,
        preferred_element_type=jnp.float32,
    ).reshape(requests, flat_width, HEAD)
    first = me_seq == 0
    new_max = jnp.where(first, new_max.reshape(requests, flat_width), neg_large)
    new_sum = jnp.where(first, new_sum, 0.0)
    new_acc = jnp.where(first, new_acc, 0.0)
    part_max = jnp.maximum(request_max, new_max)
    keep_old = jnp.exp(request_max - part_max)
    keep_new = jnp.exp(new_max - part_max)
    part_sum = request_sum * keep_old + new_sum * keep_new
    part_acc = request_acc * keep_old[..., None] + new_acc * keep_new[..., None]

    def by_chunk(values):
        lead = values.reshape(2, requests // 2, group_size, POS, -1).transpose(2, 0, 1, 3, 4)
        return lead.reshape(n_seq, requests * group_size * POS // n_seq, -1)

    chunk_rows = requests * flat_width // n_seq
    stats = jnp.concatenate(
        [
            by_chunk(part_max),
            by_chunk(part_sum),
            jnp.zeros((n_seq, chunk_rows, HEAD - 2), jnp.float32),
        ],
        axis=-1,
    )
    packed = jnp.concatenate([by_chunk(part_acc), stats], axis=1)
    projected = attend_exchange(packed, out_weight, n_head)
    return (projected, moved_cache)


def solution(mesh):
    placed = (
        P(None, "seq"),
        P("seq", "head"),
        P("head", "seq"),
        P("seq", None, None, "head"),
        P(),
        P("seq"),
        P("seq"),
        P("seq", None, None),
        P("seq", None, None),
    )
    return jax.shard_map(
        body,
        mesh=mesh,
        in_specs=placed,
        out_specs=(P("head", "seq"), P("seq", None, None, "head")),
        check_vma=False,
    )
```

```python
import functools

import jax
import jax.numpy as jnp
from jax import lax
from jax.experimental import pallas as pl
from jax.experimental.pallas import tpu as pltpu
from jax.sharding import PartitionSpec as P

HEADS = 64
KV_HEADS = 8
HEAD = 128
POS = 4
BLOCK = 128

MESH = pl.DeviceIdType.MESH

rope_base = 500000.0
neg_large = -1e30


def _barrier(peers):
    barrier = pltpu.get_barrier_semaphore()
    for device in peers:
        pl.semaphore_signal(barrier, inc=1, device_id=device, device_id_type=MESH)
    pl.semaphore_wait(barrier, len(peers))


def _send_all(axis, n, me, src_of, land, send_sem, recv_sem):
    copies = []
    for i in range(1, n):
        peer = lax.rem(me + i, n)
        copy = pltpu.make_async_remote_copy(
            src_ref=src_of(peer),
            dst_ref=land.at[me],
            send_sem=send_sem.at[peer],
            recv_sem=recv_sem.at[me],
            device_id={axis: peer},
            device_id_type=MESH,
        )
        copy.start()
        copies.append(copy)
    return copies


def _wait_all(axis, n, me, land, send_sem, recv_sem):
    for i in range(1, n):
        src = lax.rem(me + n - i, n)
        pltpu.make_async_remote_copy(
            src_ref=land.at[src],
            dst_ref=land.at[src],
            send_sem=send_sem.at[src],
            recv_sem=recv_sem.at[src],
            device_id={axis: src},
            device_id_type=MESH,
        ).wait_recv()


def _qkv_kernel(
    n, limit, part_ref, freq_ref, lengths_ref, pick_ref, kv_hbm, out_ref, sent_hbm,
    land_a, mine, land_b, sems, kv_vmem, sent_vmem, local_sems,
):
    me = lax.axis_index("seq")
    kv_in = pltpu.make_async_copy(kv_hbm, kv_vmem, local_sems.at[0])
    kv_in.start()
    land_a[me] = part_ref[me]
    _barrier([{"seq": lax.rem(me + i, n)} for i in range(1, n)])
    sent_a = _send_all("seq", n, me, lambda p: part_ref.at[p], land_a, sems.at[0], sems.at[1])
    kv_in.wait()

    def pick(j, carry):
        per = pick_ref.shape[2]
        sent_vmem[j] = kv_vmem[jnp.minimum(pick_ref[0, j // per, j % per], limit - 1)]
        return carry

    lax.fori_loop(0, sent_vmem.shape[0], pick, 0)
    kv_out = pltpu.make_async_copy(sent_vmem, sent_hbm, local_sems.at[1])
    kv_out.start()
    _wait_all("seq", n, me, land_a, sems.at[0], sems.at[1])
    total = land_a[0]
    for i in range(1, n):
        total = total + land_a[i]
    g = total.shape[0] // 2
    first_row = 2 * me
    second_row = first_row + 1
    pos_a = (lengths_ref[first_row // POS] + first_row % POS).astype(jnp.float32)
    pos_b = (lengths_ref[second_row // POS] + second_row % POS).astype(jnp.float32)
    row = lax.broadcasted_iota(jnp.int32, total.shape, 0)
    lane = lax.broadcasted_iota(jnp.int32, total.shape, 1)
    angle = jnp.where(row < g, pos_a, pos_b) * freq_ref[...]
    value_row = (row == g - 1) | (row == 2 * g - 1)
    cosine = jnp.where(value_row, 1.0, jnp.cos(angle))
    sine = jnp.where(value_row, 0.0, jnp.where(lane < HEAD // 2, -jnp.sin(angle), jnp.sin(angle)))
    turned = pltpu.roll(total, HEAD // 2, 1)
    rotated = (total * cosine + turned * sine).astype(mine.dtype)
    mine[...] = rotated
    land_b[me] = rotated
    sent_b = _send_all("seq", n, me, lambda p: mine, land_b, sems.at[2], sems.at[3])
    _wait_all("seq", n, me, land_b, sems.at[2], sems.at[3])
    for copy in sent_a + sent_b:
        copy.wait_send()
    out_ref[...] = land_b[...]
    kv_out.wait()


def qkv_exchange(partial, freq, lengths, pick, kv_cache):
    n = partial.shape[0]
    picked = (pick.size,) + kv_cache.shape[1:]
    return pl.pallas_call(
        functools.partial(_qkv_kernel, n, kv_cache.shape[0]),
        out_shape=(
            jax.ShapeDtypeStruct(partial.shape, jnp.bfloat16),
            jax.ShapeDtypeStruct(picked, kv_cache.dtype),
        ),
        in_specs=[pl.BlockSpec(memory_space=pltpu.VMEM)] * 2
        + [pl.BlockSpec(memory_space=pltpu.SMEM)] * 2
        + [pl.BlockSpec(memory_space=pl.ANY)],
        out_specs=(pl.BlockSpec(memory_space=pltpu.VMEM), pl.BlockSpec(memory_space=pl.ANY)),
        scratch_shapes=[
            pltpu.VMEM(partial.shape, jnp.float32),
            pltpu.VMEM(partial.shape[1:], jnp.bfloat16),
            pltpu.VMEM(partial.shape, jnp.bfloat16),
            pltpu.SemaphoreType.DMA((4, n)),
            pltpu.VMEM(kv_cache.shape, kv_cache.dtype),
            pltpu.VMEM(picked, kv_cache.dtype),
            pltpu.SemaphoreType.DMA((2,)),
        ],
        compiler_params=pltpu.CompilerParams(collective_id=0, has_side_effects=True),
        cost_estimate=pl.CostEstimate(
            flops=0,
            bytes_accessed=partial.size * 12 + 2 * kv_cache.size * kv_cache.dtype.itemsize,
            transcendentals=0,
        ),
    )(partial, freq, lengths, pick, kv_cache)


def _attend_kernel(
    n, m, rows, packed_ref, w_ref, out_ref, land_p, mine, land_a, part_c, land_c, sems
):
    me = lax.axis_index("seq")
    me_h = lax.axis_index("head")
    land_p[me] = packed_ref[me]
    _barrier(
        [{"seq": lax.rem(me + i, n)} for i in range(1, n)]
        + [{"head": lax.rem(me_h + i, m)} for i in range(1, m)]
    )
    sent_p = _send_all("seq", n, me, lambda p: packed_ref.at[p], land_p, sems.at[0], sems.at[1])
    _wait_all("seq", n, me, land_p, sems.at[0], sems.at[1])
    top = land_p[0, rows:, 0:1]
    for i in range(1, n):
        top = jnp.maximum(top, land_p[i, rows:, 0:1])
    numerator = jnp.zeros((rows, HEAD), jnp.float32)
    denominator = jnp.zeros((rows, 1), jnp.float32)
    for i in range(n):
        scale = jnp.exp(land_p[i, rows:, 0:1] - top)
        denominator = denominator + land_p[i, rows:, 1:2] * scale
        numerator = numerator + land_p[i, :rows] * scale
    attended = (numerator / denominator).astype(mine.dtype)
    mine[...] = attended
    land_a[me] = attended
    sent_a = _send_all("seq", n, me, lambda p: mine, land_a, sems.at[2], sems.at[3])
    _wait_all("seq", n, me, land_a, sems.at[2], sems.at[3])
    heads = n // 2
    projected = None
    for g in range(heads):
        lhs = land_a[2 * g : 2 * g + 2].reshape(2 * rows, HEAD)
        term = jnp.dot(lhs, w_ref[g * HEAD : (g + 1) * HEAD, :], preferred_element_type=jnp.float32)
        projected = term if projected is None else projected + term
    per = part_c.shape[1]
    for j in range(m):
        part_c[j] = projected[j * per : (j + 1) * per]
    land_c[me_h] = part_c[me_h]
    sent_c = _send_all("head", m, me_h, lambda p: part_c.at[p], land_c, sems.at[4], sems.at[5])
    _wait_all("head", m, me_h, land_c, sems.at[4], sems.at[5])
    total = land_c[0]
    for j in range(1, m):
        total = total + land_c[j]
    for copy in sent_p + sent_a + sent_c:
        copy.wait_send()
    out_ref[...] = total.astype(out_ref.dtype)


def attend_exchange(packed, out_weight, m):
    n, two_rows, _ = packed.shape
    rows = two_rows // 2
    width = out_weight.shape[1]
    per = 2 * rows // m
    return pl.pallas_call(
        functools.partial(_attend_kernel, n, m, rows),
        out_shape=jax.ShapeDtypeStruct((per, width), jnp.bfloat16),
        in_specs=[pl.BlockSpec(memory_space=pltpu.VMEM)] * 2,
        out_specs=pl.BlockSpec(memory_space=pltpu.VMEM),
        scratch_shapes=[
            pltpu.VMEM(packed.shape, jnp.float32),
            pltpu.VMEM((rows, HEAD), jnp.bfloat16),
            pltpu.VMEM((n, rows, HEAD), jnp.bfloat16),
            pltpu.VMEM((m, per, width), jnp.float32),
            pltpu.VMEM((m, per, width), jnp.float32),
            pltpu.SemaphoreType.DMA((6, max(n, m))),
        ],
        compiler_params=pltpu.CompilerParams(collective_id=1, has_side_effects=True),
        cost_estimate=pl.CostEstimate(
            flops=2 * 2 * rows * out_weight.shape[0] * width,
            bytes_accessed=packed.size * 8 + out_weight.size * 2,
            transcendentals=n * rows * HEAD,
        ),
    )(packed, out_weight)


def _pick_kernel(limit, index_ref, src_hbm, out_hbm, buf, sems, out_sem):
    count = buf.shape[0]

    def start(j, carry):
        k = index_ref[j]

        @pl.when(k < limit)
        def _():
            pltpu.make_async_copy(src_hbm.at[jnp.minimum(k, limit - 1)], buf.at[j], sems.at[j]).start()

        @pl.when(k >= limit)
        def _():
            buf[j] = jnp.zeros(buf.shape[1:], buf.dtype)

        return carry

    def send(j, carry):
        k = index_ref[j]

        @pl.when(k < limit)
        def _():
            pltpu.make_async_copy(src_hbm.at[0], buf.at[j], sems.at[j]).wait()

        pltpu.make_async_copy(buf.at[j], out_hbm.at[j], out_sem.at[j]).start()
        return carry

    def finish(j, carry):
        pltpu.make_async_copy(buf.at[j], out_hbm.at[j], out_sem.at[j]).wait()
        return carry

    lax.fori_loop(0, count, start, 0)
    lax.fori_loop(0, count, send, 0)
    lax.fori_loop(0, count, finish, 0)


def pick_blocks(index, source, limit):
    count = index.shape[0]
    shape = (count,) + source.shape[1:]
    nbytes = count * source[0].size * source.dtype.itemsize
    return pl.pallas_call(
        functools.partial(_pick_kernel, limit),
        out_shape=jax.ShapeDtypeStruct(shape, source.dtype),
        in_specs=[
            pl.BlockSpec(memory_space=pltpu.SMEM),
            pl.BlockSpec(memory_space=pl.ANY),
        ],
        out_specs=pl.BlockSpec(memory_space=pl.ANY),
        scratch_shapes=[
            pltpu.VMEM(shape, source.dtype),
            pltpu.SemaphoreType.DMA((count,)),
            pltpu.SemaphoreType.DMA((count,)),
        ],
        cost_estimate=pl.CostEstimate(flops=0, bytes_accessed=2 * nbytes, transcendentals=0),
    )(index, source)


def rotate(values, positions):
    half_width = values.shape[-1] // 2
    frequencies = rope_base ** (
        -(jnp.arange(half_width, dtype=jnp.float32) * 2.0 / values.shape[-1])
    )
    angles = positions[..., None] * frequencies
    cosine_table = jnp.cos(angles)
    sine_table = jnp.sin(angles)
    lower_half = values[..., :half_width]
    upper_half = values[..., half_width:]
    return jnp.concatenate(
        [
            lower_half * cosine_table - upper_half * sine_table,
            upper_half * cosine_table + lower_half * sine_table,
        ],
        axis=-1,
    )


def body(
    normed,
    qkv_weight,
    out_weight,
    kv_cache,
    lengths,
    slot_request,
    slot_block,
    send_list,
    recv_list,
):
    group_size = HEADS // KV_HEADS
    scale_factor = HEAD ** (-0.5)
    requests = lengths.shape[0]
    slot_count = kv_cache.shape[0]
    n_seq = lax.axis_size("seq")
    n_head = lax.axis_size("head")
    me_seq = lax.axis_index("seq")
    rows = normed.shape[0]
    rows_per = rows // n_seq
    groups = qkv_weight.shape[1] // HEAD

    partial = jnp.dot(normed, qkv_weight, preferred_element_type=jnp.float32)
    partial = partial.reshape(n_seq, rows_per * groups, HEAD)
    half_width = HEAD // 2
    frequencies = rope_base ** (-(jnp.arange(half_width, dtype=jnp.float32) * 2.0 / HEAD))
    freq_row = jnp.concatenate([frequencies, frequencies])[None, :]
    qkv, outgoing = qkv_exchange(partial, freq_row, lengths, send_list, kv_cache)
    qkv = qkv.reshape(requests, POS, 1, groups, HEAD)
    local_kv = 1

    outgoing = outgoing.reshape((lax.axis_size("seq"), -1) + kv_cache.shape[1:])
    incoming = lax.all_to_all(outgoing, "seq", split_axis=0, concat_axis=0, tiled=True)
    incoming = incoming.reshape((-1,) + kv_cache.shape[1:])
    arrivals = incoming.shape[0]
    source_of = (
        jnp.full((slot_count + 1,), arrivals, jnp.int32)
        .at[recv_list.reshape(-1)]
        .set(jnp.arange(arrivals, dtype=jnp.int32), mode="drop")[:slot_count]
    )
    queries = qkv[:, :, :, :group_size]
    keys_new = qkv[:, :, :, group_size]
    values_new = qkv[:, :, :, group_size + 1]

    slot_clip = jnp.minimum(slot_request, requests - 1)
    live_slot = slot_request < requests
    token_pos = slot_block[:, None] * BLOCK + jnp.arange(BLOCK, dtype=jnp.int32)[None, :]
    token_valid = (token_pos < lengths[slot_clip][:, None]) & live_slot[:, None]
    cache_view = kv_cache.reshape(slot_count, 2, BLOCK, local_kv, HEAD)
    gathered = queries[slot_clip]
    scores = (
        jnp.einsum(
            "sptgd,sbtd->stgpb", gathered, cache_view[:, 0], preferred_element_type=jnp.float32
        )
        * scale_factor
    )
    scores = jnp.where(token_valid[:, None, None, None, :], scores, neg_large)
    slot_max = jnp.max(scores, axis=-1)
    weights = jnp.where(
        token_valid[:, None, None, None, :], jnp.exp(scores - slot_max[..., None]), 0.0
    )
    slot_sum = jnp.sum(weights, axis=-1)
    slot_acc = jnp.einsum(
        "stgpb,sbtd->stgpd",
        weights.astype(jnp.bfloat16),
        cache_view[:, 1],
        preferred_element_type=jnp.float32,
    )
    flat_width = local_kv * group_size * POS
    slot_max_flat = slot_max.reshape(slot_count, flat_width)
    member = slot_request[:, None] == jnp.arange(requests, dtype=jnp.int32)[None, :]
    request_max = jnp.max(
        jnp.where(member[:, None, :], slot_max_flat[:, :, None], neg_large), axis=0
    ).T
    rescale = jnp.exp(slot_max_flat - request_max[slot_clip])
    member_float = member.astype(jnp.float32).T
    request_sum = jnp.dot(
        member_float,
        slot_sum.reshape(slot_count, flat_width) * rescale,
        precision=lax.Precision.HIGHEST,
    )
    scaled_acc = (slot_acc.reshape(slot_count, flat_width, HEAD) * rescale[:, :, None]).reshape(
        slot_count, flat_width * HEAD
    )
    request_acc = jnp.dot(member_float, scaled_acc, precision=lax.Precision.HIGHEST).reshape(
        requests, flat_width, HEAD
    )

    new_scores = (
        jnp.einsum("rptgd,rqtd->rtgpq", queries, keys_new, preferred_element_type=jnp.float32)
        * scale_factor
    )
    causal = jnp.arange(POS)[:, None] >= jnp.arange(POS)[None, :]
    new_scores = jnp.where(causal, new_scores, neg_large)
    new_max = jnp.max(new_scores, axis=-1)
    new_weights = jnp.where(causal, jnp.exp(new_scores - new_max[..., None]), 0.0)
    new_sum = jnp.sum(new_weights, axis=-1).reshape(requests, flat_width)
    new_acc = jnp.einsum(
        "rtgpq,rqtd->rtgpd",
        new_weights.astype(jnp.bfloat16),
        values_new,
        preferred_element_type=jnp.float32,
    ).reshape(requests, flat_width, HEAD)
    first = me_seq == 0
    new_max = jnp.where(first, new_max.reshape(requests, flat_width), neg_large)
    new_sum = jnp.where(first, new_sum, 0.0)
    new_acc = jnp.where(first, new_acc, 0.0)
    part_max = jnp.maximum(request_max, new_max)
    keep_old = jnp.exp(request_max - part_max)
    keep_new = jnp.exp(new_max - part_max)
    part_sum = request_sum * keep_old + new_sum * keep_new
    part_acc = request_acc * keep_old[..., None] + new_acc * keep_new[..., None]

    def by_chunk(values):
        lead = values.reshape(2, requests // 2, group_size, POS, -1).transpose(2, 0, 1, 3, 4)
        return lead.reshape(n_seq, requests * group_size * POS // n_seq, -1)

    chunk_rows = requests * flat_width // n_seq
    stats = jnp.concatenate(
        [
            by_chunk(part_max),
            by_chunk(part_sum),
            jnp.zeros((n_seq, chunk_rows, HEAD - 2), jnp.float32),
        ],
        axis=-1,
    )
    packed = jnp.concatenate([by_chunk(part_acc), stats], axis=1)
    source_of, packed = lax.optimization_barrier((source_of, packed))
    projected = attend_exchange(packed, out_weight, n_head)
    moved_cache = pick_blocks(source_of, incoming, arrivals)
    return (projected, moved_cache)


def solution(mesh):
    placed = (
        P(None, "seq"),
        P("seq", "head"),
        P("head", "seq"),
        P("seq", None, None, "head"),
        P(),
        P("seq"),
        P("seq"),
        P("seq", None, None),
        P("seq", None, None),
    )
    return jax.shard_map(
        body,
        mesh=mesh,
        in_specs=placed,
        out_specs=(P("head", "seq"), P("seq", None, None, "head")),
        check_vma=False,
    )
```

```python
import functools

import jax
import numpy as np
import jax.numpy as jnp
from jax import lax
from jax.experimental import pallas as pl
from jax.experimental.pallas import tpu as pltpu
from jax.sharding import PartitionSpec as P

HEADS = 64
KV_HEADS = 8
HEAD = 128
POS = 4
BLOCK = 128

MESH = pl.DeviceIdType.MESH

rope_base = 500000.0
neg_large = -1e30


def _barrier(peers):
    barrier = pltpu.get_barrier_semaphore()
    for device in peers:
        pl.semaphore_signal(barrier, inc=1, device_id=device, device_id_type=MESH)
    pl.semaphore_wait(barrier, len(peers))


def _send_all(axis, n, me, src_of, land, send_sem, recv_sem):
    copies = []
    for i in range(1, n):
        peer = lax.rem(me + i, n)
        copy = pltpu.make_async_remote_copy(
            src_ref=src_of(peer),
            dst_ref=land.at[me],
            send_sem=send_sem.at[peer],
            recv_sem=recv_sem.at[me],
            device_id={axis: peer},
            device_id_type=MESH,
        )
        copy.start()
        copies.append(copy)
    return copies


def _wait_all(axis, n, me, land, send_sem, recv_sem):
    for i in range(1, n):
        src = lax.rem(me + n - i, n)
        pltpu.make_async_remote_copy(
            src_ref=land.at[src],
            dst_ref=land.at[src],
            send_sem=send_sem.at[src],
            recv_sem=recv_sem.at[src],
            device_id={axis: src},
            device_id_type=MESH,
        ).wait_recv()


def _qkv_kernel(
    n, limit, part_ref, freq_ref, lengths_ref, pick_ref, kv_hbm, out_ref, sent_hbm,
    land_a, mine, land_b, sems, kv_vmem, sent_vmem, local_sems,
):
    me = lax.axis_index("seq")
    kv_in = pltpu.make_async_copy(kv_hbm, kv_vmem, local_sems.at[0])
    kv_in.start()
    land_a[me] = part_ref[me]
    _barrier([{"seq": lax.rem(me + i, n)} for i in range(1, n)])
    sent_a = _send_all("seq", n, me, lambda p: part_ref.at[p], land_a, sems.at[0], sems.at[1])
    kv_in.wait()

    def pick(j, carry):
        per = pick_ref.shape[2]
        sent_vmem[j] = kv_vmem[jnp.minimum(pick_ref[0, j // per, j % per], limit - 1)]
        return carry

    lax.fori_loop(0, sent_vmem.shape[0], pick, 0)
    kv_out = pltpu.make_async_copy(sent_vmem, sent_hbm, local_sems.at[1])
    kv_out.start()
    _wait_all("seq", n, me, land_a, sems.at[0], sems.at[1])
    total = land_a[0]
    for i in range(1, n):
        total = total + land_a[i]
    g = total.shape[0] // 2
    first_row = 2 * me
    second_row = first_row + 1
    pos_a = (lengths_ref[first_row // POS] + first_row % POS).astype(jnp.float32)
    pos_b = (lengths_ref[second_row // POS] + second_row % POS).astype(jnp.float32)
    row = lax.broadcasted_iota(jnp.int32, total.shape, 0)
    lane = lax.broadcasted_iota(jnp.int32, total.shape, 1)
    angle = jnp.where(row < g, pos_a, pos_b) * freq_ref[...]
    value_row = (row == g - 1) | (row == 2 * g - 1)
    cosine = jnp.where(value_row, 1.0, jnp.cos(angle))
    sine = jnp.where(value_row, 0.0, jnp.where(lane < HEAD // 2, -jnp.sin(angle), jnp.sin(angle)))
    turned = pltpu.roll(total, HEAD // 2, 1)
    rotated = (total * cosine + turned * sine).astype(mine.dtype)
    mine[...] = rotated
    land_b[me] = rotated
    sent_b = _send_all("seq", n, me, lambda p: mine, land_b, sems.at[2], sems.at[3])
    _wait_all("seq", n, me, land_b, sems.at[2], sems.at[3])
    for copy in sent_a + sent_b:
        copy.wait_send()
    out_ref[...] = land_b[...]
    kv_out.wait()


def qkv_exchange(partial, freq, lengths, pick, kv_cache):
    n = partial.shape[0]
    picked = (pick.size,) + kv_cache.shape[1:]
    return pl.pallas_call(
        functools.partial(_qkv_kernel, n, kv_cache.shape[0]),
        out_shape=(
            jax.ShapeDtypeStruct(partial.shape, jnp.bfloat16),
            jax.ShapeDtypeStruct(picked, kv_cache.dtype),
        ),
        in_specs=[pl.BlockSpec(memory_space=pltpu.VMEM)] * 2
        + [pl.BlockSpec(memory_space=pltpu.SMEM)] * 2
        + [pl.BlockSpec(memory_space=pl.ANY)],
        out_specs=(pl.BlockSpec(memory_space=pltpu.VMEM), pl.BlockSpec(memory_space=pl.ANY)),
        scratch_shapes=[
            pltpu.VMEM(partial.shape, jnp.float32),
            pltpu.VMEM(partial.shape[1:], jnp.bfloat16),
            pltpu.VMEM(partial.shape, jnp.bfloat16),
            pltpu.SemaphoreType.DMA((4, n)),
            pltpu.VMEM(kv_cache.shape, kv_cache.dtype),
            pltpu.VMEM(picked, kv_cache.dtype),
            pltpu.SemaphoreType.DMA((2,)),
        ],
        compiler_params=pltpu.CompilerParams(collective_id=0, has_side_effects=True),
        cost_estimate=pl.CostEstimate(
            flops=0,
            bytes_accessed=partial.size * 12 + 2 * kv_cache.size * kv_cache.dtype.itemsize,
            transcendentals=0,
        ),
    )(partial, freq, lengths, pick, kv_cache)


def _attend_kernel(
    n, m, rows, acc_ref, stats_ref, w_ref, out_ref, land_p, land_s, mine, land_a, part_c, land_c,
    sems,
):
    me = lax.axis_index("seq")
    me_h = lax.axis_index("head")
    land_p[me] = acc_ref[me]
    land_s[me] = stats_ref[me]
    _barrier(
        [{"seq": lax.rem(me + i, n)} for i in range(1, n)]
        + [{"head": lax.rem(me_h + i, m)} for i in range(1, m)]
    )
    sent_p = _send_all("seq", n, me, lambda p: acc_ref.at[p], land_p, sems.at[0], sems.at[1])
    sent_s = _send_all("seq", n, me, lambda p: stats_ref.at[p], land_s, sems.at[6], sems.at[7])
    _wait_all("seq", n, me, land_s, sems.at[6], sems.at[7])
    _wait_all("seq", n, me, land_p, sems.at[0], sems.at[1])
    top = land_s[0, :, 0:1]
    for i in range(1, n):
        top = jnp.maximum(top, land_s[i, :, 0:1])
    numerator = jnp.zeros((rows, HEAD), jnp.float32)
    denominator = jnp.zeros((rows, 1), jnp.float32)
    for i in range(n):
        scale = jnp.exp(land_s[i, :, 0:1] - top)
        denominator = denominator + land_s[i, :, 1:2] * scale
        numerator = numerator + land_p[i].astype(jnp.float32) * scale
    attended = (numerator / denominator).astype(mine.dtype)
    mine[...] = attended
    land_a[me] = attended
    sent_a = _send_all("seq", n, me, lambda p: mine, land_a, sems.at[2], sems.at[3])
    _wait_all("seq", n, me, land_a, sems.at[2], sems.at[3])
    heads = n // 2
    projected = None
    for g in range(heads):
        lhs = land_a[2 * g : 2 * g + 2].reshape(2 * rows, HEAD)
        term = jnp.dot(lhs, w_ref[g * HEAD : (g + 1) * HEAD, :], preferred_element_type=jnp.float32)
        projected = term if projected is None else projected + term
    per = part_c.shape[1]
    for j in range(m):
        part_c[j] = projected[j * per : (j + 1) * per]
    land_c[me_h] = part_c[me_h]
    sent_c = _send_all("head", m, me_h, lambda p: part_c.at[p], land_c, sems.at[4], sems.at[5])
    _wait_all("head", m, me_h, land_c, sems.at[4], sems.at[5])
    total = land_c[0]
    for j in range(1, m):
        total = total + land_c[j]
    for copy in sent_p + sent_s + sent_a + sent_c:
        copy.wait_send()
    out_ref[...] = total.astype(out_ref.dtype)


def attend_exchange(acc, stats, out_weight, m):
    n, rows, _ = acc.shape
    width = out_weight.shape[1]
    per = 2 * rows // m
    return pl.pallas_call(
        functools.partial(_attend_kernel, n, m, rows),
        out_shape=jax.ShapeDtypeStruct((per, width), jnp.bfloat16),
        in_specs=[pl.BlockSpec(memory_space=pltpu.VMEM)] * 3,
        out_specs=pl.BlockSpec(memory_space=pltpu.VMEM),
        scratch_shapes=[
            pltpu.VMEM(acc.shape, acc.dtype),
            pltpu.VMEM(stats.shape, jnp.float32),
            pltpu.VMEM((rows, HEAD), jnp.bfloat16),
            pltpu.VMEM((n, rows, HEAD), jnp.bfloat16),
            pltpu.VMEM((m, per, width), jnp.float32),
            pltpu.VMEM((m, per, width), jnp.float32),
            pltpu.SemaphoreType.DMA((8, max(n, m))),
        ],
        compiler_params=pltpu.CompilerParams(collective_id=1, has_side_effects=True),
        cost_estimate=pl.CostEstimate(
            flops=2 * 2 * rows * out_weight.shape[0] * width,
            bytes_accessed=acc.size * 4 + stats.size * 8 + out_weight.size * 2,
            transcendentals=n * rows * HEAD,
        ),
    )(acc, stats, out_weight)


def _pick_kernel(limit, index_ref, src_hbm, out_hbm, buf, sems, out_sem):
    count = buf.shape[0]

    def start(j, carry):
        k = index_ref[j]

        @pl.when(k < limit)
        def _():
            pltpu.make_async_copy(src_hbm.at[jnp.minimum(k, limit - 1)], buf.at[j], sems.at[j]).start()

        @pl.when(k >= limit)
        def _():
            buf[j] = jnp.zeros(buf.shape[1:], buf.dtype)

        return carry

    def send(j, carry):
        k = index_ref[j]

        @pl.when(k < limit)
        def _():
            pltpu.make_async_copy(src_hbm.at[0], buf.at[j], sems.at[j]).wait()

        pltpu.make_async_copy(buf.at[j], out_hbm.at[j], out_sem.at[j]).start()
        return carry

    def finish(j, carry):
        pltpu.make_async_copy(buf.at[j], out_hbm.at[j], out_sem.at[j]).wait()
        return carry

    lax.fori_loop(0, count, start, 0)
    lax.fori_loop(0, count, send, 0)
    lax.fori_loop(0, count, finish, 0)


def pick_blocks(index, source, limit):
    count = index.shape[0]
    shape = (count,) + source.shape[1:]
    nbytes = count * source[0].size * source.dtype.itemsize
    return pl.pallas_call(
        functools.partial(_pick_kernel, limit),
        out_shape=jax.ShapeDtypeStruct(shape, source.dtype),
        in_specs=[
            pl.BlockSpec(memory_space=pltpu.SMEM),
            pl.BlockSpec(memory_space=pl.ANY),
        ],
        out_specs=pl.BlockSpec(memory_space=pl.ANY),
        scratch_shapes=[
            pltpu.VMEM(shape, source.dtype),
            pltpu.SemaphoreType.DMA((count,)),
            pltpu.SemaphoreType.DMA((count,)),
        ],
        cost_estimate=pl.CostEstimate(flops=0, bytes_accessed=2 * nbytes, transcendentals=0),
    )(index, source)


def rotate(values, positions):
    half_width = values.shape[-1] // 2
    frequencies = rope_base ** (
        -(jnp.arange(half_width, dtype=jnp.float32) * 2.0 / values.shape[-1])
    )
    angles = positions[..., None] * frequencies
    cosine_table = jnp.cos(angles)
    sine_table = jnp.sin(angles)
    lower_half = values[..., :half_width]
    upper_half = values[..., half_width:]
    return jnp.concatenate(
        [
            lower_half * cosine_table - upper_half * sine_table,
            upper_half * cosine_table + lower_half * sine_table,
        ],
        axis=-1,
    )


def body(
    normed,
    qkv_weight,
    out_weight,
    kv_cache,
    lengths,
    slot_request,
    slot_block,
    send_list,
    recv_list,
):
    group_size = HEADS // KV_HEADS
    scale_factor = HEAD ** (-0.5)
    requests = lengths.shape[0]
    slot_count = kv_cache.shape[0]
    n_seq = lax.axis_size("seq")
    n_head = lax.axis_size("head")
    me_seq = lax.axis_index("seq")
    rows = normed.shape[0]
    rows_per = rows // n_seq
    groups = qkv_weight.shape[1] // HEAD

    partial = jnp.dot(normed, qkv_weight, preferred_element_type=jnp.float32)
    partial = partial.reshape(n_seq, rows_per * groups, HEAD)
    half_width = HEAD // 2
    frequencies = np.float32(rope_base) ** (
        -(np.arange(half_width, dtype=np.float32) * np.float32(2.0) / np.float32(HEAD))
    )
    freq_row = jnp.asarray(np.concatenate([frequencies, frequencies])[None, :].astype(np.float32))
    qkv, outgoing = qkv_exchange(partial, freq_row, lengths, send_list, kv_cache)
    qkv = qkv.reshape(requests, POS, 1, groups, HEAD)
    local_kv = 1

    outgoing = outgoing.reshape((lax.axis_size("seq"), -1) + kv_cache.shape[1:])
    incoming = lax.all_to_all(outgoing, "seq", split_axis=0, concat_axis=0, tiled=True)
    incoming = incoming.reshape((-1,) + kv_cache.shape[1:])
    arrivals = incoming.shape[0]
    source_of = (
        jnp.full((slot_count + 1,), arrivals, jnp.int32)
        .at[recv_list.reshape(-1)]
        .set(jnp.arange(arrivals, dtype=jnp.int32), mode="drop")[:slot_count]
    )
    queries = qkv[:, :, :, :group_size]
    keys_new = qkv[:, :, :, group_size]
    values_new = qkv[:, :, :, group_size + 1]

    slot_clip = jnp.minimum(slot_request, requests - 1)
    live_slot = slot_request < requests
    token_pos = slot_block[:, None] * BLOCK + jnp.arange(BLOCK, dtype=jnp.int32)[None, :]
    token_valid = (token_pos < lengths[slot_clip][:, None]) & live_slot[:, None]
    cache_view = kv_cache.reshape(slot_count, 2, BLOCK, local_kv, HEAD)
    gathered = queries[slot_clip]
    scores = (
        jnp.einsum(
            "sptgd,sbtd->stgpb", gathered, cache_view[:, 0], preferred_element_type=jnp.float32
        )
        * scale_factor
    )
    scores = jnp.where(token_valid[:, None, None, None, :], scores, neg_large)
    slot_max = jnp.max(scores, axis=-1)
    weights = jnp.where(
        token_valid[:, None, None, None, :], jnp.exp(scores - slot_max[..., None]), 0.0
    )
    slot_sum = jnp.sum(weights, axis=-1)
    slot_acc = jnp.einsum(
        "stgpb,sbtd->stgpd",
        weights.astype(jnp.bfloat16),
        cache_view[:, 1],
        preferred_element_type=jnp.float32,
    )
    flat_width = local_kv * group_size * POS
    slot_max_flat = slot_max.reshape(slot_count, flat_width)
    member = slot_request[:, None] == jnp.arange(requests, dtype=jnp.int32)[None, :]
    request_max = jnp.max(
        jnp.where(member[:, None, :], slot_max_flat[:, :, None], neg_large), axis=0
    ).T
    rescale = jnp.exp(slot_max_flat - request_max[slot_clip])
    member_float = member.astype(jnp.float32).T
    request_sum = jnp.dot(
        member_float,
        slot_sum.reshape(slot_count, flat_width) * rescale,
        precision=lax.Precision.HIGHEST,
    )
    scaled_acc = (slot_acc.reshape(slot_count, flat_width, HEAD) * rescale[:, :, None]).reshape(
        slot_count, flat_width * HEAD
    )
    request_acc = jnp.dot(member_float, scaled_acc, precision=lax.Precision.HIGHEST).reshape(
        requests, flat_width, HEAD
    )

    new_scores = (
        jnp.einsum("rptgd,rqtd->rtgpq", queries, keys_new, preferred_element_type=jnp.float32)
        * scale_factor
    )
    causal = jnp.arange(POS)[:, None] >= jnp.arange(POS)[None, :]
    new_scores = jnp.where(causal, new_scores, neg_large)
    new_max = jnp.max(new_scores, axis=-1)
    new_weights = jnp.where(causal, jnp.exp(new_scores - new_max[..., None]), 0.0)
    new_sum = jnp.sum(new_weights, axis=-1).reshape(requests, flat_width)
    new_acc = jnp.einsum(
        "rtgpq,rqtd->rtgpd",
        new_weights.astype(jnp.bfloat16),
        values_new,
        preferred_element_type=jnp.float32,
    ).reshape(requests, flat_width, HEAD)
    first = me_seq == 0
    new_max = jnp.where(first, new_max.reshape(requests, flat_width), neg_large)
    new_sum = jnp.where(first, new_sum, 0.0)
    new_acc = jnp.where(first, new_acc, 0.0)
    part_max = jnp.maximum(request_max, new_max)
    keep_old = jnp.exp(request_max - part_max)
    keep_new = jnp.exp(new_max - part_max)
    part_sum = request_sum * keep_old + new_sum * keep_new
    part_acc = request_acc * keep_old[..., None] + new_acc * keep_new[..., None]

    def by_chunk(values):
        lead = values.reshape(2, requests // 2, group_size, POS, -1).transpose(2, 0, 1, 3, 4)
        return lead.reshape(n_seq, requests * group_size * POS // n_seq, -1)

    chunk_rows = requests * flat_width // n_seq
    stats = jnp.concatenate(
        [
            by_chunk(part_max),
            by_chunk(part_sum),
            jnp.zeros((n_seq, chunk_rows, HEAD - 2), jnp.float32),
        ],
        axis=-1,
    )
    acc_chunks = by_chunk(part_acc).astype(jnp.bfloat16)
    source_of, acc_chunks, stats = lax.optimization_barrier((source_of, acc_chunks, stats))
    projected = attend_exchange(acc_chunks, stats, out_weight, n_head)
    moved_cache = pick_blocks(source_of, incoming, arrivals)
    return (projected, moved_cache)


def solution(mesh):
    placed = (
        P(None, "seq"),
        P("seq", "head"),
        P("head", "seq"),
        P("seq", None, None, "head"),
        P(),
        P("seq"),
        P("seq"),
        P("seq", None, None),
        P("seq", None, None),
    )
    return jax.shard_map(
        body,
        mesh=mesh,
        in_specs=placed,
        out_specs=(P("head", "seq"), P("seq", None, None, "head")),
        check_vma=False,
    )
```

```python
import functools

import jax
import numpy as np
import jax.numpy as jnp
from jax import lax
from jax.experimental import pallas as pl
from jax.experimental.pallas import tpu as pltpu
from jax.sharding import PartitionSpec as P

HEADS = 64
KV_HEADS = 8
HEAD = 128
POS = 4
BLOCK = 128

MESH = pl.DeviceIdType.MESH

rope_base = 500000.0
neg_large = -1e30


def _barrier(peers):
    barrier = pltpu.get_barrier_semaphore()
    for device in peers:
        pl.semaphore_signal(barrier, inc=1, device_id=device, device_id_type=MESH)
    pl.semaphore_wait(barrier, len(peers))


def _send_all(axis, n, me, src_of, land, send_sem, recv_sem):
    copies = []
    for i in range(1, n):
        peer = lax.rem(me + i, n)
        copy = pltpu.make_async_remote_copy(
            src_ref=src_of(peer),
            dst_ref=land.at[me],
            send_sem=send_sem.at[peer],
            recv_sem=recv_sem.at[me],
            device_id={axis: peer},
            device_id_type=MESH,
        )
        copy.start()
        copies.append(copy)
    return copies


def _wait_all(axis, n, me, land, send_sem, recv_sem):
    for i in range(1, n):
        src = lax.rem(me + n - i, n)
        pltpu.make_async_remote_copy(
            src_ref=land.at[src],
            dst_ref=land.at[src],
            send_sem=send_sem.at[src],
            recv_sem=recv_sem.at[src],
            device_id={axis: src},
            device_id_type=MESH,
        ).wait_recv()


def _qkv_kernel(
    n, limit, part_ref, freq_ref, lengths_ref, pick_ref, kv_hbm, out_ref, sent_hbm,
    land_a, mine, land_b, sems, kv_vmem, sent_vmem, local_sems,
):
    me = lax.axis_index("seq")
    kv_in = pltpu.make_async_copy(kv_hbm, kv_vmem, local_sems.at[0])
    kv_in.start()
    land_a[me] = part_ref[me]
    _barrier([{"seq": lax.rem(me + i, n)} for i in range(1, n)])
    sent_a = _send_all("seq", n, me, lambda p: part_ref.at[p], land_a, sems.at[0], sems.at[1])
    kv_in.wait()

    def pick(j, carry):
        per = pick_ref.shape[2]
        sent_vmem[j] = kv_vmem[jnp.minimum(pick_ref[0, j // per, j % per], limit - 1)]
        return carry

    lax.fori_loop(0, sent_vmem.shape[0], pick, 0)
    kv_out = pltpu.make_async_copy(sent_vmem, sent_hbm, local_sems.at[1])
    kv_out.start()
    _wait_all("seq", n, me, land_a, sems.at[0], sems.at[1])
    total = land_a[0]
    for i in range(1, n):
        total = total + land_a[i]
    g = total.shape[0] // 2
    first_row = 2 * me
    second_row = first_row + 1
    pos_a = (lengths_ref[first_row // POS] + first_row % POS).astype(jnp.float32)
    pos_b = (lengths_ref[second_row // POS] + second_row % POS).astype(jnp.float32)
    row = lax.broadcasted_iota(jnp.int32, total.shape, 0)
    lane = lax.broadcasted_iota(jnp.int32, total.shape, 1)
    angle = jnp.where(row < g, pos_a, pos_b) * freq_ref[...]
    value_row = (row == g - 1) | (row == 2 * g - 1)
    cosine = jnp.where(value_row, 1.0, jnp.cos(angle))
    sine = jnp.where(value_row, 0.0, jnp.where(lane < HEAD // 2, -jnp.sin(angle), jnp.sin(angle)))
    turned = pltpu.roll(total, HEAD // 2, 1)
    rotated = (total * cosine + turned * sine).astype(mine.dtype)
    mine[...] = rotated
    land_b[me] = rotated
    sent_b = _send_all("seq", n, me, lambda p: mine, land_b, sems.at[2], sems.at[3])
    _wait_all("seq", n, me, land_b, sems.at[2], sems.at[3])
    for copy in sent_a + sent_b:
        copy.wait_send()
    out_ref[...] = land_b[...]
    kv_out.wait()


def qkv_exchange(partial, freq, lengths, pick, kv_cache):
    n = partial.shape[0]
    picked = (pick.size,) + kv_cache.shape[1:]
    return pl.pallas_call(
        functools.partial(_qkv_kernel, n, kv_cache.shape[0]),
        out_shape=(
            jax.ShapeDtypeStruct(partial.shape, jnp.bfloat16),
            jax.ShapeDtypeStruct(picked, kv_cache.dtype),
        ),
        in_specs=[pl.BlockSpec(memory_space=pltpu.VMEM)] * 2
        + [pl.BlockSpec(memory_space=pltpu.SMEM)] * 2
        + [pl.BlockSpec(memory_space=pl.ANY)],
        out_specs=(pl.BlockSpec(memory_space=pltpu.VMEM), pl.BlockSpec(memory_space=pl.ANY)),
        scratch_shapes=[
            pltpu.VMEM(partial.shape, jnp.float32),
            pltpu.VMEM(partial.shape[1:], jnp.bfloat16),
            pltpu.VMEM(partial.shape, jnp.bfloat16),
            pltpu.SemaphoreType.DMA((4, n)),
            pltpu.VMEM(kv_cache.shape, kv_cache.dtype),
            pltpu.VMEM(picked, kv_cache.dtype),
            pltpu.SemaphoreType.DMA((2,)),
        ],
        compiler_params=pltpu.CompilerParams(collective_id=0, has_side_effects=True),
        cost_estimate=pl.CostEstimate(
            flops=0,
            bytes_accessed=partial.size * 12 + 2 * kv_cache.size * kv_cache.dtype.itemsize,
            transcendentals=0,
        ),
    )(partial, freq, lengths, pick, kv_cache)


def _attend_kernel(
    n, m, rows, acc_ref, stats_ref, w_ref, out_ref, land_p, land_s, mine, land_a, part_c, land_c,
    sems,
):
    me = lax.axis_index("seq")
    me_h = lax.axis_index("head")
    land_p[me] = acc_ref[me]
    land_s[me] = stats_ref[me]
    _barrier(
        [{"seq": lax.rem(me + i, n)} for i in range(1, n)]
        + [{"head": lax.rem(me_h + i, m)} for i in range(1, m)]
    )
    sent_p = _send_all("seq", n, me, lambda p: acc_ref.at[p], land_p, sems.at[0], sems.at[1])
    sent_s = _send_all("seq", n, me, lambda p: stats_ref.at[p], land_s, sems.at[6], sems.at[7])
    _wait_all("seq", n, me, land_s, sems.at[6], sems.at[7])
    _wait_all("seq", n, me, land_p, sems.at[0], sems.at[1])
    top = land_s[0, :, 0:1]
    for i in range(1, n):
        top = jnp.maximum(top, land_s[i, :, 0:1])
    numerator = jnp.zeros((rows, HEAD), jnp.float32)
    denominator = jnp.zeros((rows, 1), jnp.float32)
    for i in range(n):
        scale = jnp.exp(land_s[i, :, 0:1] - top)
        denominator = denominator + land_s[i, :, 1:2] * scale
        numerator = numerator + land_p[i].astype(jnp.float32) * scale
    attended = (numerator / denominator).astype(mine.dtype)
    mine[...] = attended
    land_a[me] = attended
    sent_a = _send_all("seq", n, me, lambda p: mine, land_a, sems.at[2], sems.at[3])
    _wait_all("seq", n, me, land_a, sems.at[2], sems.at[3])
    heads = n // 2
    projected = None
    for g in range(heads):
        lhs = land_a[2 * g : 2 * g + 2].reshape(2 * rows, HEAD)
        term = jnp.dot(lhs, w_ref[g * HEAD : (g + 1) * HEAD, :], preferred_element_type=jnp.float32)
        projected = term if projected is None else projected + term
    per = part_c.shape[1]
    for j in range(m):
        part_c[j] = projected[j * per : (j + 1) * per]
    land_c[me_h] = part_c[me_h]
    sent_c = _send_all("head", m, me_h, lambda p: part_c.at[p], land_c, sems.at[4], sems.at[5])
    _wait_all("head", m, me_h, land_c, sems.at[4], sems.at[5])
    total = land_c[0]
    for j in range(1, m):
        total = total + land_c[j]
    for copy in sent_p + sent_s + sent_a + sent_c:
        copy.wait_send()
    out_ref[...] = total.astype(out_ref.dtype)


def attend_exchange(acc, stats, out_weight, m):
    n, rows, _ = acc.shape
    width = out_weight.shape[1]
    per = 2 * rows // m
    return pl.pallas_call(
        functools.partial(_attend_kernel, n, m, rows),
        out_shape=jax.ShapeDtypeStruct((per, width), jnp.bfloat16),
        in_specs=[pl.BlockSpec(memory_space=pltpu.VMEM)] * 3,
        out_specs=pl.BlockSpec(memory_space=pltpu.VMEM),
        scratch_shapes=[
            pltpu.VMEM(acc.shape, acc.dtype),
            pltpu.VMEM(stats.shape, jnp.float32),
            pltpu.VMEM((rows, HEAD), jnp.bfloat16),
            pltpu.VMEM((n, rows, HEAD), jnp.bfloat16),
            pltpu.VMEM((m, per, width), jnp.float32),
            pltpu.VMEM((m, per, width), jnp.float32),
            pltpu.SemaphoreType.DMA((8, max(n, m))),
        ],
        compiler_params=pltpu.CompilerParams(collective_id=1, has_side_effects=True),
        cost_estimate=pl.CostEstimate(
            flops=2 * 2 * rows * out_weight.shape[0] * width,
            bytes_accessed=acc.size * 4 + stats.size * 8 + out_weight.size * 2,
            transcendentals=n * rows * HEAD,
        ),
    )(acc, stats, out_weight)


def _place_kernel(limit, index_ref, src_hbm, out_hbm, buf, blank, in_sem, out_sems):
    load = pltpu.make_async_copy(src_hbm, buf, in_sem)
    load.start()
    blank[...] = jnp.zeros(blank.shape, blank.dtype)
    load.wait()

    def send(j, carry):
        k = index_ref[j]

        @pl.when(k < limit)
        def _():
            pltpu.make_async_copy(buf.at[jnp.minimum(k, limit - 1)], out_hbm.at[j], out_sems.at[j]).start()

        @pl.when(k >= limit)
        def _():
            pltpu.make_async_copy(blank, out_hbm.at[j], out_sems.at[j]).start()

        return carry

    def finish(j, carry):
        pltpu.make_async_copy(blank, out_hbm.at[j], out_sems.at[j]).wait()
        return carry

    count = out_hbm.shape[0]
    lax.fori_loop(0, count, send, 0)
    lax.fori_loop(0, count, finish, 0)


def pick_blocks(index, source, limit):
    count = index.shape[0]
    shape = (count,) + source.shape[1:]
    nbytes = count * source[0].size * source.dtype.itemsize
    return pl.pallas_call(
        functools.partial(_place_kernel, limit),
        out_shape=jax.ShapeDtypeStruct(shape, source.dtype),
        in_specs=[
            pl.BlockSpec(memory_space=pltpu.SMEM),
            pl.BlockSpec(memory_space=pl.ANY),
        ],
        out_specs=pl.BlockSpec(memory_space=pl.ANY),
        scratch_shapes=[
            pltpu.VMEM(source.shape, source.dtype),
            pltpu.VMEM(source.shape[1:], source.dtype),
            pltpu.SemaphoreType.DMA(()),
            pltpu.SemaphoreType.DMA((count,)),
        ],
        cost_estimate=pl.CostEstimate(flops=0, bytes_accessed=2 * nbytes, transcendentals=0),
    )(index, source)


def rotate(values, positions):
    half_width = values.shape[-1] // 2
    frequencies = rope_base ** (
        -(jnp.arange(half_width, dtype=jnp.float32) * 2.0 / values.shape[-1])
    )
    angles = positions[..., None] * frequencies
    cosine_table = jnp.cos(angles)
    sine_table = jnp.sin(angles)
    lower_half = values[..., :half_width]
    upper_half = values[..., half_width:]
    return jnp.concatenate(
        [
            lower_half * cosine_table - upper_half * sine_table,
            upper_half * cosine_table + lower_half * sine_table,
        ],
        axis=-1,
    )


def body(
    normed,
    qkv_weight,
    out_weight,
    kv_cache,
    lengths,
    slot_request,
    slot_block,
    send_list,
    recv_list,
):
    group_size = HEADS // KV_HEADS
    scale_factor = HEAD ** (-0.5)
    requests = lengths.shape[0]
    slot_count = kv_cache.shape[0]
    n_seq = lax.axis_size("seq")
    n_head = lax.axis_size("head")
    me_seq = lax.axis_index("seq")
    rows = normed.shape[0]
    rows_per = rows // n_seq
    groups = qkv_weight.shape[1] // HEAD

    partial = jnp.dot(normed, qkv_weight, preferred_element_type=jnp.float32)
    partial = partial.reshape(n_seq, rows_per * groups, HEAD)
    half_width = HEAD // 2
    frequencies = np.float32(rope_base) ** (
        -(np.arange(half_width, dtype=np.float32) * np.float32(2.0) / np.float32(HEAD))
    )
    freq_row = jnp.asarray(np.concatenate([frequencies, frequencies])[None, :].astype(np.float32))
    qkv, outgoing = qkv_exchange(partial, freq_row, lengths, send_list, kv_cache)
    qkv = qkv.reshape(requests, POS, 1, groups, HEAD)
    local_kv = 1

    outgoing = outgoing.reshape((lax.axis_size("seq"), -1) + kv_cache.shape[1:])
    incoming = lax.all_to_all(outgoing, "seq", split_axis=0, concat_axis=0, tiled=True)
    incoming = incoming.reshape((-1,) + kv_cache.shape[1:])
    arrivals = incoming.shape[0]
    source_of = (
        jnp.full((slot_count + 1,), arrivals, jnp.int32)
        .at[recv_list.reshape(-1)]
        .set(jnp.arange(arrivals, dtype=jnp.int32), mode="drop")[:slot_count]
    )
    queries = qkv[:, :, :, :group_size]
    keys_new = qkv[:, :, :, group_size]
    values_new = qkv[:, :, :, group_size + 1]

    slot_clip = jnp.minimum(slot_request, requests - 1)
    live_slot = slot_request < requests
    token_pos = slot_block[:, None] * BLOCK + jnp.arange(BLOCK, dtype=jnp.int32)[None, :]
    token_valid = (token_pos < lengths[slot_clip][:, None]) & live_slot[:, None]
    cache_view = kv_cache.reshape(slot_count, 2, BLOCK, local_kv, HEAD)
    gathered = queries[slot_clip]
    scores = (
        jnp.einsum(
            "sptgd,sbtd->stgpb", gathered, cache_view[:, 0], preferred_element_type=jnp.float32
        )
        * scale_factor
    )
    scores = jnp.where(token_valid[:, None, None, None, :], scores, neg_large)
    slot_max = jnp.max(scores, axis=-1)
    weights = jnp.where(
        token_valid[:, None, None, None, :], jnp.exp(scores - slot_max[..., None]), 0.0
    )
    slot_sum = jnp.sum(weights, axis=-1)
    slot_acc = jnp.einsum(
        "stgpb,sbtd->stgpd",
        weights.astype(jnp.bfloat16),
        cache_view[:, 1],
        preferred_element_type=jnp.float32,
    )
    flat_width = local_kv * group_size * POS
    slot_max_flat = slot_max.reshape(slot_count, flat_width)
    member = slot_request[:, None] == jnp.arange(requests, dtype=jnp.int32)[None, :]
    request_max = jnp.max(
        jnp.where(member[:, None, :], slot_max_flat[:, :, None], neg_large), axis=0
    ).T
    rescale = jnp.exp(slot_max_flat - request_max[slot_clip])
    member_float = member.astype(jnp.float32).T
    request_sum = jnp.dot(
        member_float,
        slot_sum.reshape(slot_count, flat_width) * rescale,
        precision=lax.Precision.HIGHEST,
    )
    scaled_acc = (slot_acc.reshape(slot_count, flat_width, HEAD) * rescale[:, :, None]).reshape(
        slot_count, flat_width * HEAD
    )
    request_acc = jnp.dot(member_float, scaled_acc, precision=lax.Precision.HIGHEST).reshape(
        requests, flat_width, HEAD
    )

    new_scores = (
        jnp.einsum("rptgd,rqtd->rtgpq", queries, keys_new, preferred_element_type=jnp.float32)
        * scale_factor
    )
    causal = jnp.arange(POS)[:, None] >= jnp.arange(POS)[None, :]
    new_scores = jnp.where(causal, new_scores, neg_large)
    new_max = jnp.max(new_scores, axis=-1)
    new_weights = jnp.where(causal, jnp.exp(new_scores - new_max[..., None]), 0.0)
    new_sum = jnp.sum(new_weights, axis=-1).reshape(requests, flat_width)
    new_acc = jnp.einsum(
        "rtgpq,rqtd->rtgpd",
        new_weights.astype(jnp.bfloat16),
        values_new,
        preferred_element_type=jnp.float32,
    ).reshape(requests, flat_width, HEAD)
    first = me_seq == 0
    new_max = jnp.where(first, new_max.reshape(requests, flat_width), neg_large)
    new_sum = jnp.where(first, new_sum, 0.0)
    new_acc = jnp.where(first, new_acc, 0.0)
    part_max = jnp.maximum(request_max, new_max)
    keep_old = jnp.exp(request_max - part_max)
    keep_new = jnp.exp(new_max - part_max)
    part_sum = request_sum * keep_old + new_sum * keep_new
    part_acc = request_acc * keep_old[..., None] + new_acc * keep_new[..., None]

    def by_chunk(values):
        lead = values.reshape(2, requests // 2, group_size, POS, -1).transpose(2, 0, 1, 3, 4)
        return lead.reshape(n_seq, requests * group_size * POS // n_seq, -1)

    chunk_rows = requests * flat_width // n_seq
    stats = jnp.concatenate(
        [
            by_chunk(part_max),
            by_chunk(part_sum),
            jnp.zeros((n_seq, chunk_rows, HEAD - 2), jnp.float32),
        ],
        axis=-1,
    )
    acc_chunks = by_chunk(part_acc).astype(jnp.bfloat16)
    source_of, acc_chunks, stats = lax.optimization_barrier((source_of, acc_chunks, stats))
    projected = attend_exchange(acc_chunks, stats, out_weight, n_head)
    moved_cache = pick_blocks(source_of, incoming, arrivals)
    return (projected, moved_cache)


def solution(mesh):
    placed = (
        P(None, "seq"),
        P("seq", "head"),
        P("head", "seq"),
        P("seq", None, None, "head"),
        P(),
        P("seq"),
        P("seq"),
        P("seq", None, None),
        P("seq", None, None),
    )
    return jax.shard_map(
        body,
        mesh=mesh,
        in_specs=placed,
        out_specs=(P("head", "seq"), P("seq", None, None, "head")),
        check_vma=False,
    )
```

```python
import functools

import jax
import numpy as np
import jax.numpy as jnp
from jax import lax
from jax.experimental import pallas as pl
from jax.experimental.pallas import tpu as pltpu
from jax.sharding import PartitionSpec as P

HEADS = 64
KV_HEADS = 8
HEAD = 128
POS = 4
BLOCK = 128

MESH = pl.DeviceIdType.MESH

rope_base = 500000.0
neg_large = -1e30


def _barrier(peers):
    barrier = pltpu.get_barrier_semaphore()
    for device in peers:
        pl.semaphore_signal(barrier, inc=1, device_id=device, device_id_type=MESH)
    pl.semaphore_wait(barrier, len(peers))


def _send_all(axis, n, me, src_of, land, send_sem, recv_sem):
    copies = []
    for i in range(1, n):
        peer = lax.rem(me + i, n)
        copy = pltpu.make_async_remote_copy(
            src_ref=src_of(peer),
            dst_ref=land.at[me],
            send_sem=send_sem.at[peer],
            recv_sem=recv_sem.at[me],
            device_id={axis: peer},
            device_id_type=MESH,
        )
        copy.start()
        copies.append(copy)
    return copies


def _wait_all(axis, n, me, land, send_sem, recv_sem):
    for i in range(1, n):
        src = lax.rem(me + n - i, n)
        pltpu.make_async_remote_copy(
            src_ref=land.at[src],
            dst_ref=land.at[src],
            send_sem=send_sem.at[src],
            recv_sem=recv_sem.at[src],
            device_id={axis: src},
            device_id_type=MESH,
        ).wait_recv()


def _qkv_kernel(
    n, limit, part_ref, freq_ref, lengths_ref, pick_ref, kv_hbm, out_ref, sent_hbm,
    land_a, mine, land_b, sems, kv_vmem, sent_vmem, local_sems,
):
    me = lax.axis_index("seq")
    kv_in = pltpu.make_async_copy(kv_hbm, kv_vmem, local_sems.at[0])
    kv_in.start()
    land_a[me] = part_ref[me]
    _barrier([{"seq": lax.rem(me + i, n)} for i in range(1, n)])
    sent_a = _send_all("seq", n, me, lambda p: part_ref.at[p], land_a, sems.at[0], sems.at[1])
    kv_in.wait()

    def pick(j, carry):
        per = pick_ref.shape[2]
        sent_vmem[j] = kv_vmem[jnp.minimum(pick_ref[0, j // per, j % per], limit - 1)]
        return carry

    lax.fori_loop(0, sent_vmem.shape[0], pick, 0)
    kv_out = pltpu.make_async_copy(sent_vmem, sent_hbm, local_sems.at[1])
    kv_out.start()
    _wait_all("seq", n, me, land_a, sems.at[0], sems.at[1])
    total = land_a[0]
    for i in range(1, n):
        total = total + land_a[i]
    g = total.shape[0] // 2
    first_row = 2 * me
    second_row = first_row + 1
    pos_a = (lengths_ref[first_row // POS] + first_row % POS).astype(jnp.float32)
    pos_b = (lengths_ref[second_row // POS] + second_row % POS).astype(jnp.float32)
    row = lax.broadcasted_iota(jnp.int32, total.shape, 0)
    lane = lax.broadcasted_iota(jnp.int32, total.shape, 1)
    angle = jnp.where(row < g, pos_a, pos_b) * freq_ref[...]
    value_row = (row == g - 1) | (row == 2 * g - 1)
    cosine = jnp.where(value_row, 1.0, jnp.cos(angle))
    sine = jnp.where(value_row, 0.0, jnp.where(lane < HEAD // 2, -jnp.sin(angle), jnp.sin(angle)))
    turned = pltpu.roll(total, HEAD // 2, 1)
    rotated = (total * cosine + turned * sine).astype(mine.dtype)
    mine[...] = rotated
    land_b[me] = rotated
    sent_b = _send_all("seq", n, me, lambda p: mine, land_b, sems.at[2], sems.at[3])
    _wait_all("seq", n, me, land_b, sems.at[2], sems.at[3])
    for copy in sent_a + sent_b:
        copy.wait_send()
    out_ref[...] = land_b[...]
    kv_out.wait()


def qkv_exchange(partial, freq, lengths, pick, kv_cache):
    n = partial.shape[0]
    picked = (pick.size,) + kv_cache.shape[1:]
    return pl.pallas_call(
        functools.partial(_qkv_kernel, n, kv_cache.shape[0]),
        out_shape=(
            jax.ShapeDtypeStruct(partial.shape, jnp.bfloat16),
            jax.ShapeDtypeStruct(picked, kv_cache.dtype),
        ),
        in_specs=[pl.BlockSpec(memory_space=pltpu.VMEM)] * 2
        + [pl.BlockSpec(memory_space=pltpu.SMEM)] * 2
        + [pl.BlockSpec(memory_space=pl.ANY)],
        out_specs=(pl.BlockSpec(memory_space=pltpu.VMEM), pl.BlockSpec(memory_space=pl.ANY)),
        scratch_shapes=[
            pltpu.VMEM(partial.shape, jnp.float32),
            pltpu.VMEM(partial.shape[1:], jnp.bfloat16),
            pltpu.VMEM(partial.shape, jnp.bfloat16),
            pltpu.SemaphoreType.DMA((4, n)),
            pltpu.VMEM(kv_cache.shape, kv_cache.dtype),
            pltpu.VMEM(picked, kv_cache.dtype),
            pltpu.SemaphoreType.DMA((2,)),
        ],
        compiler_params=pltpu.CompilerParams(collective_id=0, has_side_effects=True),
        cost_estimate=pl.CostEstimate(
            flops=0,
            bytes_accessed=partial.size * 12 + 2 * kv_cache.size * kv_cache.dtype.itemsize,
            transcendentals=0,
        ),
    )(partial, freq, lengths, pick, kv_cache)


def _attend_kernel(
    n, m, rows, acc_ref, stats_ref, w_ref, out_ref, land_p, land_s, mine, land_a, part_c, land_c,
    sems,
):
    me = lax.axis_index("seq")
    me_h = lax.axis_index("head")
    land_p[me] = acc_ref[me]
    land_s[me] = stats_ref[me]
    _barrier(
        [{"seq": lax.rem(me + i, n)} for i in range(1, n)]
        + [{"head": lax.rem(me_h + i, m)} for i in range(1, m)]
    )
    sent_p = _send_all("seq", n, me, lambda p: acc_ref.at[p], land_p, sems.at[0], sems.at[1])
    sent_s = _send_all("seq", n, me, lambda p: stats_ref.at[p], land_s, sems.at[6], sems.at[7])
    _wait_all("seq", n, me, land_s, sems.at[6], sems.at[7])
    _wait_all("seq", n, me, land_p, sems.at[0], sems.at[1])
    top = land_s[0, :, 0:1]
    for i in range(1, n):
        top = jnp.maximum(top, land_s[i, :, 0:1])
    numerator = jnp.zeros((rows, HEAD), jnp.float32)
    denominator = jnp.zeros((rows, 1), jnp.float32)
    for i in range(n):
        scale = jnp.exp(land_s[i, :, 0:1] - top)
        denominator = denominator + land_s[i, :, 1:2] * scale
        numerator = numerator + land_p[i].astype(jnp.float32) * scale
    attended = (numerator / denominator).astype(mine.dtype)
    mine[...] = attended
    land_a[me] = attended
    sent_a = _send_all("seq", n, me, lambda p: mine, land_a, sems.at[2], sems.at[3])
    _wait_all("seq", n, me, land_a, sems.at[2], sems.at[3])
    heads = n // 2
    projected = None
    for g in range(heads):
        lhs = land_a[2 * g : 2 * g + 2].reshape(2 * rows, HEAD)
        term = jnp.dot(lhs, w_ref[g * HEAD : (g + 1) * HEAD, :], preferred_element_type=jnp.float32)
        projected = term if projected is None else projected + term
    per = part_c.shape[1]
    for j in range(m):
        part_c[j] = projected[j * per : (j + 1) * per]
    land_c[me_h] = part_c[me_h]
    sent_c = _send_all("head", m, me_h, lambda p: part_c.at[p], land_c, sems.at[4], sems.at[5])
    _wait_all("head", m, me_h, land_c, sems.at[4], sems.at[5])
    total = land_c[0]
    for j in range(1, m):
        total = total + land_c[j]
    for copy in sent_p + sent_s + sent_a + sent_c:
        copy.wait_send()
    out_ref[...] = total.astype(out_ref.dtype)


def attend_exchange(acc, stats, out_weight, m):
    n, rows, _ = acc.shape
    width = out_weight.shape[1]
    per = 2 * rows // m
    return pl.pallas_call(
        functools.partial(_attend_kernel, n, m, rows),
        out_shape=jax.ShapeDtypeStruct((per, width), jnp.bfloat16),
        in_specs=[pl.BlockSpec(memory_space=pltpu.VMEM)] * 3,
        out_specs=pl.BlockSpec(memory_space=pltpu.VMEM),
        scratch_shapes=[
            pltpu.VMEM(acc.shape, acc.dtype),
            pltpu.VMEM(stats.shape, jnp.float32),
            pltpu.VMEM((rows, HEAD), jnp.bfloat16),
            pltpu.VMEM((n, rows, HEAD), jnp.bfloat16),
            pltpu.VMEM((m, per, width), jnp.float32),
            pltpu.VMEM((m, per, width), jnp.float32),
            pltpu.SemaphoreType.DMA((8, max(n, m))),
        ],
        compiler_params=pltpu.CompilerParams(collective_id=1, has_side_effects=True),
        cost_estimate=pl.CostEstimate(
            flops=2 * 2 * rows * out_weight.shape[0] * width,
            bytes_accessed=acc.size * 4 + stats.size * 8 + out_weight.size * 2,
            transcendentals=n * rows * HEAD,
        ),
    )(acc, stats, out_weight)


def _migrate_kernel(
    n, scale, requests, req_ref, blk_ref, len_ref, q_ref, kv_ref, sent_hbm,
    m_ref, l_ref, acc_ref, got_hbm, send_sem, recv_sem, local_sem,
):
    me = lax.axis_index("seq")
    _barrier([{"seq": lax.rem(me + i, n)} for i in range(1, n)])
    copies = []
    for i in range(1, n):
        peer = lax.rem(me + i, n)
        copy = pltpu.make_async_remote_copy(
            src_ref=sent_hbm.at[peer],
            dst_ref=got_hbm.at[me],
            send_sem=send_sem.at[peer],
            recv_sem=recv_sem.at[me],
            device_id={"seq": peer},
            device_id_type=MESH,
        )
        copy.start()
        copies.append(copy)
    own = pltpu.make_async_copy(sent_hbm.at[me], got_hbm.at[me], local_sem)
    own.start()

    def slot(s, carry):
        owner = req_ref[s]
        r = jnp.minimum(owner, requests - 1)
        q = q_ref[r]
        keys = kv_ref[s, 0]
        scores = lax.dot_general(
            q, keys, (((1,), (1,)), ((), ())), preferred_element_type=jnp.float32
        ) * scale
        lane = lax.broadcasted_iota(jnp.int32, scores.shape, 1)
        valid = (lane < len_ref[r] - blk_ref[s] * BLOCK) & (owner < requests)
        scores = jnp.where(valid, scores, neg_large)
        top = jnp.max(scores, axis=1, keepdims=True)
        weights = jnp.where(valid, jnp.exp(scores - top), 0.0)
        m_ref[s] = jnp.broadcast_to(top, scores.shape)
        l_ref[s] = jnp.broadcast_to(jnp.sum(weights, axis=1, keepdims=True), scores.shape)
        acc_ref[s] = jnp.dot(
            weights.astype(jnp.bfloat16), kv_ref[s, 1], preferred_element_type=jnp.float32
        )
        return carry

    lax.fori_loop(0, kv_ref.shape[0], slot, 0)
    _wait_all("seq", n, me, got_hbm, send_sem, recv_sem)
    for copy in copies:
        copy.wait_send()
    own.wait()


def migrate_and_attend(slot_request, slot_block, lengths, queries, kv_cache, outgoing, scale):
    n = outgoing.shape[0]
    slots = kv_cache.shape[0]
    rows = queries.shape[1]
    per_slot = (slots, rows, HEAD)
    return pl.pallas_call(
        functools.partial(_migrate_kernel, n, scale, lengths.shape[0]),
        out_shape=(
            jax.ShapeDtypeStruct(per_slot, jnp.float32),
            jax.ShapeDtypeStruct(per_slot, jnp.float32),
            jax.ShapeDtypeStruct(per_slot, jnp.float32),
            jax.ShapeDtypeStruct(outgoing.shape, outgoing.dtype),
        ),
        in_specs=[pl.BlockSpec(memory_space=pltpu.SMEM)] * 3
        + [pl.BlockSpec(memory_space=pltpu.VMEM)] * 2
        + [pl.BlockSpec(memory_space=pl.ANY)],
        out_specs=(
            pl.BlockSpec(memory_space=pltpu.VMEM),
            pl.BlockSpec(memory_space=pltpu.VMEM),
            pl.BlockSpec(memory_space=pltpu.VMEM),
            pl.BlockSpec(memory_space=pl.ANY),
        ),
        scratch_shapes=[
            pltpu.SemaphoreType.DMA((n,)),
            pltpu.SemaphoreType.DMA((n,)),
            pltpu.SemaphoreType.DMA(()),
        ],
        compiler_params=pltpu.CompilerParams(collective_id=2, has_side_effects=True),
        cost_estimate=pl.CostEstimate(
            flops=4 * slots * rows * BLOCK * HEAD,
            bytes_accessed=kv_cache.size * 2 + 2 * outgoing.size * 2,
            transcendentals=slots * rows * BLOCK,
        ),
    )(slot_request, slot_block, lengths, queries, kv_cache, outgoing)


def _pick_kernel(limit, index_ref, src_hbm, out_hbm, buf, sems, out_sem):
    count = buf.shape[0]

    def start(j, carry):
        k = index_ref[j]

        @pl.when(k < limit)
        def _():
            pltpu.make_async_copy(src_hbm.at[jnp.minimum(k, limit - 1)], buf.at[j], sems.at[j]).start()

        @pl.when(k >= limit)
        def _():
            buf[j] = jnp.zeros(buf.shape[1:], buf.dtype)

        return carry

    def send(j, carry):
        k = index_ref[j]

        @pl.when(k < limit)
        def _():
            pltpu.make_async_copy(src_hbm.at[0], buf.at[j], sems.at[j]).wait()

        pltpu.make_async_copy(buf.at[j], out_hbm.at[j], out_sem.at[j]).start()
        return carry

    def finish(j, carry):
        pltpu.make_async_copy(buf.at[j], out_hbm.at[j], out_sem.at[j]).wait()
        return carry

    lax.fori_loop(0, count, start, 0)
    lax.fori_loop(0, count, send, 0)
    lax.fori_loop(0, count, finish, 0)


def pick_blocks(index, source, limit):
    count = index.shape[0]
    shape = (count,) + source.shape[1:]
    nbytes = count * source[0].size * source.dtype.itemsize
    return pl.pallas_call(
        functools.partial(_pick_kernel, limit),
        out_shape=jax.ShapeDtypeStruct(shape, source.dtype),
        in_specs=[
            pl.BlockSpec(memory_space=pltpu.SMEM),
            pl.BlockSpec(memory_space=pl.ANY),
        ],
        out_specs=pl.BlockSpec(memory_space=pl.ANY),
        scratch_shapes=[
            pltpu.VMEM(shape, source.dtype),
            pltpu.SemaphoreType.DMA((count,)),
            pltpu.SemaphoreType.DMA((count,)),
        ],
        cost_estimate=pl.CostEstimate(flops=0, bytes_accessed=2 * nbytes, transcendentals=0),
    )(index, source)


def rotate(values, positions):
    half_width = values.shape[-1] // 2
    frequencies = rope_base ** (
        -(jnp.arange(half_width, dtype=jnp.float32) * 2.0 / values.shape[-1])
    )
    angles = positions[..., None] * frequencies
    cosine_table = jnp.cos(angles)
    sine_table = jnp.sin(angles)
    lower_half = values[..., :half_width]
    upper_half = values[..., half_width:]
    return jnp.concatenate(
        [
            lower_half * cosine_table - upper_half * sine_table,
            upper_half * cosine_table + lower_half * sine_table,
        ],
        axis=-1,
    )


def body(
    normed,
    qkv_weight,
    out_weight,
    kv_cache,
    lengths,
    slot_request,
    slot_block,
    send_list,
    recv_list,
):
    group_size = HEADS // KV_HEADS
    scale_factor = HEAD ** (-0.5)
    requests = lengths.shape[0]
    slot_count = kv_cache.shape[0]
    n_seq = lax.axis_size("seq")
    n_head = lax.axis_size("head")
    me_seq = lax.axis_index("seq")
    rows = normed.shape[0]
    rows_per = rows // n_seq
    groups = qkv_weight.shape[1] // HEAD

    partial = jnp.dot(normed, qkv_weight, preferred_element_type=jnp.float32)
    partial = partial.reshape(n_seq, rows_per * groups, HEAD)
    half_width = HEAD // 2
    frequencies = np.float32(rope_base) ** (
        -(np.arange(half_width, dtype=np.float32) * np.float32(2.0) / np.float32(HEAD))
    )
    freq_row = jnp.asarray(np.concatenate([frequencies, frequencies])[None, :].astype(np.float32))
    qkv, outgoing = qkv_exchange(partial, freq_row, lengths, send_list, kv_cache)
    qkv = qkv.reshape(requests, POS, 1, groups, HEAD)
    local_kv = 1

    outgoing = outgoing.reshape((lax.axis_size("seq"), -1) + kv_cache.shape[1:])
    arrivals = outgoing.shape[0] * outgoing.shape[1]
    source_of = (
        jnp.full((slot_count + 1,), arrivals, jnp.int32)
        .at[recv_list.reshape(-1)]
        .set(jnp.arange(arrivals, dtype=jnp.int32), mode="drop")[:slot_count]
    )
    queries = qkv[:, :, :, :group_size]
    keys_new = qkv[:, :, :, group_size]
    values_new = qkv[:, :, :, group_size + 1]

    slot_clip = jnp.minimum(slot_request, requests - 1)
    per_request_q = queries[:, :, 0].transpose(0, 2, 1, 3).reshape(requests, group_size * POS, HEAD)
    slot_m, slot_l, slot_a, incoming = migrate_and_attend(
        slot_request, slot_block, lengths, per_request_q, kv_cache, outgoing, scale_factor
    )
    incoming = incoming.reshape((-1,) + kv_cache.shape[1:])
    slot_max = slot_m[:, :, 0]
    slot_sum = slot_l[:, :, 0]
    slot_acc = slot_a
    flat_width = local_kv * group_size * POS
    slot_max_flat = slot_max
    member = slot_request[:, None] == jnp.arange(requests, dtype=jnp.int32)[None, :]
    request_max = jnp.max(
        jnp.where(member[:, None, :], slot_max_flat[:, :, None], neg_large), axis=0
    ).T
    rescale = jnp.exp(slot_max_flat - request_max[slot_clip])
    member_float = member.astype(jnp.float32).T
    request_sum = jnp.dot(
        member_float,
        slot_sum.reshape(slot_count, flat_width) * rescale,
        precision=lax.Precision.HIGHEST,
    )
    scaled_acc = (slot_acc.reshape(slot_count, flat_width, HEAD) * rescale[:, :, None]).reshape(
        slot_count, flat_width * HEAD
    )
    request_acc = jnp.dot(member_float, scaled_acc, precision=lax.Precision.HIGHEST).reshape(
        requests, flat_width, HEAD
    )

    new_scores = (
        jnp.einsum("rptgd,rqtd->rtgpq", queries, keys_new, preferred_element_type=jnp.float32)
        * scale_factor
    )
    causal = jnp.arange(POS)[:, None] >= jnp.arange(POS)[None, :]
    new_scores = jnp.where(causal, new_scores, neg_large)
    new_max = jnp.max(new_scores, axis=-1)
    new_weights = jnp.where(causal, jnp.exp(new_scores - new_max[..., None]), 0.0)
    new_sum = jnp.sum(new_weights, axis=-1).reshape(requests, flat_width)
    new_acc = jnp.einsum(
        "rtgpq,rqtd->rtgpd",
        new_weights.astype(jnp.bfloat16),
        values_new,
        preferred_element_type=jnp.float32,
    ).reshape(requests, flat_width, HEAD)
    first = me_seq == 0
    new_max = jnp.where(first, new_max.reshape(requests, flat_width), neg_large)
    new_sum = jnp.where(first, new_sum, 0.0)
    new_acc = jnp.where(first, new_acc, 0.0)
    part_max = jnp.maximum(request_max, new_max)
    keep_old = jnp.exp(request_max - part_max)
    keep_new = jnp.exp(new_max - part_max)
    part_sum = request_sum * keep_old + new_sum * keep_new
    part_acc = request_acc * keep_old[..., None] + new_acc * keep_new[..., None]

    def by_chunk(values):
        lead = values.reshape(2, requests // 2, group_size, POS, -1).transpose(2, 0, 1, 3, 4)
        return lead.reshape(n_seq, requests * group_size * POS // n_seq, -1)

    chunk_rows = requests * flat_width // n_seq
    stats = jnp.concatenate(
        [
            by_chunk(part_max),
            by_chunk(part_sum),
            jnp.zeros((n_seq, chunk_rows, HEAD - 2), jnp.float32),
        ],
        axis=-1,
    )
    acc_chunks = by_chunk(part_acc).astype(jnp.bfloat16)
    source_of, acc_chunks, stats = lax.optimization_barrier((source_of, acc_chunks, stats))
    projected = attend_exchange(acc_chunks, stats, out_weight, n_head)
    moved_cache = pick_blocks(source_of, incoming, arrivals)
    return (projected, moved_cache)


def solution(mesh):
    placed = (
        P(None, "seq"),
        P("seq", "head"),
        P("head", "seq"),
        P("seq", None, None, "head"),
        P(),
        P("seq"),
        P("seq"),
        P("seq", None, None),
        P("seq", None, None),
    )
    return jax.shard_map(
        body,
        mesh=mesh,
        in_specs=placed,
        out_specs=(P("head", "seq"), P("seq", None, None, "head")),
        check_vma=False,
    )
```

```python
import functools

import jax
import numpy as np
import jax.numpy as jnp
from jax import lax
from jax.experimental import pallas as pl
from jax.experimental.pallas import tpu as pltpu
from jax.sharding import PartitionSpec as P

HEADS = 64
KV_HEADS = 8
HEAD = 128
POS = 4
BLOCK = 128

MESH = pl.DeviceIdType.MESH

rope_base = 500000.0
neg_large = -1e30


def _barrier(peers):
    barrier = pltpu.get_barrier_semaphore()
    for device in peers:
        pl.semaphore_signal(barrier, inc=1, device_id=device, device_id_type=MESH)
    pl.semaphore_wait(barrier, len(peers))


def _send_all(axis, n, me, src_of, land, send_sem, recv_sem):
    copies = []
    for i in range(1, n):
        peer = lax.rem(me + i, n)
        copy = pltpu.make_async_remote_copy(
            src_ref=src_of(peer),
            dst_ref=land.at[me],
            send_sem=send_sem.at[peer],
            recv_sem=recv_sem.at[me],
            device_id={axis: peer},
            device_id_type=MESH,
        )
        copy.start()
        copies.append(copy)
    return copies


def _wait_all(axis, n, me, land, send_sem, recv_sem):
    for i in range(1, n):
        src = lax.rem(me + n - i, n)
        pltpu.make_async_remote_copy(
            src_ref=land.at[src],
            dst_ref=land.at[src],
            send_sem=send_sem.at[src],
            recv_sem=recv_sem.at[src],
            device_id={axis: src},
            device_id_type=MESH,
        ).wait_recv()


def _qkv_kernel(
    n, limit, x_hbm, w_hbm, freq_ref, lengths_ref, pick_hbm, kv_hbm, out_ref, sent_hbm,
    x_vmem, w_vmem, part_ref, pick_ref, land_a, mine, land_b, sems, kv_vmem, sent_vmem, local_sems,
):
    me = lax.axis_index("seq")
    loads = [
        pltpu.make_async_copy(x_hbm, x_vmem, local_sems.at[2]),
        pltpu.make_async_copy(w_hbm, w_vmem, local_sems.at[3]),
        pltpu.make_async_copy(pick_hbm, pick_ref, local_sems.at[4]),
    ]
    for load in loads:
        load.start()
    kv_in = pltpu.make_async_copy(kv_hbm, kv_vmem, local_sems.at[0])
    kv_in.start()
    barrier = pltpu.get_barrier_semaphore()
    for i in range(1, n):
        pl.semaphore_signal(
            barrier, inc=1, device_id={"seq": lax.rem(me + i, n)}, device_id_type=MESH
        )
    for load in loads:
        load.wait()
    product = jnp.dot(x_vmem[...], w_vmem[...], preferred_element_type=jnp.float32)
    groups = product.shape[1] // HEAD
    per = part_ref.shape[1] // groups
    for j in range(n):
        for k in range(per):
            row = product[per * j + k : per * j + k + 1]
            for g in range(groups):
                part_ref[j, k * groups + g : k * groups + g + 1, :] = row[:, g * HEAD : (g + 1) * HEAD]
    land_a[me] = part_ref[me]
    pl.semaphore_wait(barrier, n - 1)
    sent_a = _send_all("seq", n, me, lambda p: part_ref.at[p], land_a, sems.at[0], sems.at[1])
    kv_in.wait()

    def pick(j, carry):
        per = pick_ref.shape[1]
        sent_vmem[j] = kv_vmem[jnp.minimum(pick_ref[0, j % per, j // per], limit - 1)]
        return carry

    lax.fori_loop(0, sent_vmem.shape[0], pick, 0)
    kv_out = pltpu.make_async_copy(sent_vmem, sent_hbm, local_sems.at[1])
    kv_out.start()
    _wait_all("seq", n, me, land_a, sems.at[0], sems.at[1])
    total = land_a[0]
    for i in range(1, n):
        total = total + land_a[i]
    g = total.shape[0] // 2
    first_row = 2 * me
    second_row = first_row + 1
    pos_a = (lengths_ref[first_row // POS] + first_row % POS).astype(jnp.float32)
    pos_b = (lengths_ref[second_row // POS] + second_row % POS).astype(jnp.float32)
    row = lax.broadcasted_iota(jnp.int32, total.shape, 0)
    lane = lax.broadcasted_iota(jnp.int32, total.shape, 1)
    angle = jnp.where(row < g, pos_a, pos_b) * freq_ref[...]
    value_row = (row == g - 1) | (row == 2 * g - 1)
    cosine = jnp.where(value_row, 1.0, jnp.cos(angle))
    sine = jnp.where(value_row, 0.0, jnp.where(lane < HEAD // 2, -jnp.sin(angle), jnp.sin(angle)))
    turned = pltpu.roll(total, HEAD // 2, 1)
    rotated = (total * cosine + turned * sine).astype(mine.dtype)
    mine[...] = rotated
    land_b[me] = rotated
    sent_b = _send_all("seq", n, me, lambda p: mine, land_b, sems.at[2], sems.at[3])
    _wait_all("seq", n, me, land_b, sems.at[2], sems.at[3])
    for copy in sent_a + sent_b:
        copy.wait_send()
    out_ref[...] = land_b[...]
    kv_out.wait()


def qkv_exchange(normed, qkv_weight, freq, lengths, pick, kv_cache, n):
    rows = normed.shape[0]
    groups = qkv_weight.shape[1] // HEAD
    chunk = (n, rows // n * groups, HEAD)
    picked = (pick.size,) + kv_cache.shape[1:]
    return pl.pallas_call(
        functools.partial(_qkv_kernel, n, kv_cache.shape[0]),
        out_shape=(
            jax.ShapeDtypeStruct(chunk, jnp.bfloat16),
            jax.ShapeDtypeStruct(picked, kv_cache.dtype),
        ),
        in_specs=[pl.BlockSpec(memory_space=pl.ANY)] * 2
        + [pl.BlockSpec(memory_space=pltpu.VMEM), pl.BlockSpec(memory_space=pltpu.SMEM)]
        + [pl.BlockSpec(memory_space=pl.ANY)] * 2,
        out_specs=(pl.BlockSpec(memory_space=pltpu.VMEM), pl.BlockSpec(memory_space=pl.ANY)),
        scratch_shapes=[
            pltpu.VMEM(normed.shape, normed.dtype),
            pltpu.VMEM(qkv_weight.shape, qkv_weight.dtype),
            pltpu.VMEM(chunk, jnp.float32),
            pltpu.SMEM(pick.shape, pick.dtype),
            pltpu.VMEM(chunk, jnp.float32),
            pltpu.VMEM(chunk[1:], jnp.bfloat16),
            pltpu.VMEM(chunk, jnp.bfloat16),
            pltpu.SemaphoreType.DMA((4, n)),
            pltpu.VMEM(kv_cache.shape, kv_cache.dtype),
            pltpu.VMEM(picked, kv_cache.dtype),
            pltpu.SemaphoreType.DMA((5,)),
        ],
        compiler_params=pltpu.CompilerParams(collective_id=0, has_side_effects=True),
        cost_estimate=pl.CostEstimate(
            flops=2 * rows * normed.shape[1] * qkv_weight.shape[1],
            bytes_accessed=qkv_weight.size * 2 + 2 * kv_cache.size * kv_cache.dtype.itemsize,
            transcendentals=0,
        ),
    )(normed, qkv_weight, freq, lengths, pick, kv_cache)


def _attend_kernel(
    n, m, rows, acc_ref, stats_ref, w_ref, out_ref, land_p, land_s, mine, land_a, part_c, land_c,
    sems,
):
    me = lax.axis_index("seq")
    me_h = lax.axis_index("head")
    land_p[me] = acc_ref[me]
    land_s[me] = stats_ref[me]
    _barrier(
        [{"seq": lax.rem(me + i, n)} for i in range(1, n)]
        + [{"head": lax.rem(me_h + i, m)} for i in range(1, m)]
    )
    sent_p = _send_all("seq", n, me, lambda p: acc_ref.at[p], land_p, sems.at[0], sems.at[1])
    sent_s = _send_all("seq", n, me, lambda p: stats_ref.at[p], land_s, sems.at[6], sems.at[7])
    _wait_all("seq", n, me, land_s, sems.at[6], sems.at[7])
    _wait_all("seq", n, me, land_p, sems.at[0], sems.at[1])
    top = land_s[0, :, 0:1]
    for i in range(1, n):
        top = jnp.maximum(top, land_s[i, :, 0:1])
    numerator = jnp.zeros((rows, HEAD), jnp.float32)
    denominator = jnp.zeros((rows, 1), jnp.float32)
    for i in range(n):
        scale = jnp.exp(land_s[i, :, 0:1] - top)
        denominator = denominator + land_s[i, :, 1:2] * scale
        numerator = numerator + land_p[i].astype(jnp.float32) * scale
    attended = (numerator / denominator).astype(mine.dtype)
    mine[...] = attended
    land_a[me] = attended
    sent_a = _send_all("seq", n, me, lambda p: mine, land_a, sems.at[2], sems.at[3])
    _wait_all("seq", n, me, land_a, sems.at[2], sems.at[3])
    heads = n // 2
    projected = None
    for g in range(heads):
        lhs = land_a[2 * g : 2 * g + 2].reshape(2 * rows, HEAD)
        term = jnp.dot(lhs, w_ref[g * HEAD : (g + 1) * HEAD, :], preferred_element_type=jnp.float32)
        projected = term if projected is None else projected + term
    per = part_c.shape[1]
    for j in range(m):
        part_c[j] = projected[j * per : (j + 1) * per]
    land_c[me_h] = part_c[me_h]
    sent_c = _send_all("head", m, me_h, lambda p: part_c.at[p], land_c, sems.at[4], sems.at[5])
    _wait_all("head", m, me_h, land_c, sems.at[4], sems.at[5])
    total = land_c[0]
    for j in range(1, m):
        total = total + land_c[j]
    for copy in sent_p + sent_s + sent_a + sent_c:
        copy.wait_send()
    out_ref[...] = total.astype(out_ref.dtype)


def attend_exchange(acc, stats, out_weight, m):
    n, rows, _ = acc.shape
    width = out_weight.shape[1]
    per = 2 * rows // m
    return pl.pallas_call(
        functools.partial(_attend_kernel, n, m, rows),
        out_shape=jax.ShapeDtypeStruct((per, width), jnp.bfloat16),
        in_specs=[pl.BlockSpec(memory_space=pltpu.VMEM)] * 3,
        out_specs=pl.BlockSpec(memory_space=pltpu.VMEM),
        scratch_shapes=[
            pltpu.VMEM(acc.shape, acc.dtype),
            pltpu.VMEM(stats.shape, jnp.float32),
            pltpu.VMEM((rows, HEAD), jnp.bfloat16),
            pltpu.VMEM((n, rows, HEAD), jnp.bfloat16),
            pltpu.VMEM((m, per, width), jnp.float32),
            pltpu.VMEM((m, per, width), jnp.float32),
            pltpu.SemaphoreType.DMA((8, max(n, m))),
        ],
        compiler_params=pltpu.CompilerParams(collective_id=1, has_side_effects=True),
        cost_estimate=pl.CostEstimate(
            flops=2 * 2 * rows * out_weight.shape[0] * width,
            bytes_accessed=acc.size * 4 + stats.size * 8 + out_weight.size * 2,
            transcendentals=n * rows * HEAD,
        ),
    )(acc, stats, out_weight)


def _pick_kernel(limit, index_ref, src_hbm, out_hbm, buf, sems, out_sem):
    count = buf.shape[0]

    def start(j, carry):
        k = index_ref[j]

        @pl.when(k < limit)
        def _():
            pltpu.make_async_copy(src_hbm.at[jnp.minimum(k, limit - 1)], buf.at[j], sems.at[j]).start()

        @pl.when(k >= limit)
        def _():
            buf[j] = jnp.zeros(buf.shape[1:], buf.dtype)

        return carry

    def send(j, carry):
        k = index_ref[j]

        @pl.when(k < limit)
        def _():
            pltpu.make_async_copy(src_hbm.at[0], buf.at[j], sems.at[j]).wait()

        pltpu.make_async_copy(buf.at[j], out_hbm.at[j], out_sem.at[j]).start()
        return carry

    def finish(j, carry):
        pltpu.make_async_copy(buf.at[j], out_hbm.at[j], out_sem.at[j]).wait()
        return carry

    lax.fori_loop(0, count, start, 0)
    lax.fori_loop(0, count, send, 0)
    lax.fori_loop(0, count, finish, 0)


def pick_blocks(index, source, limit):
    count = index.shape[0]
    shape = (count,) + source.shape[1:]
    nbytes = count * source[0].size * source.dtype.itemsize
    return pl.pallas_call(
        functools.partial(_pick_kernel, limit),
        out_shape=jax.ShapeDtypeStruct(shape, source.dtype),
        in_specs=[
            pl.BlockSpec(memory_space=pltpu.SMEM),
            pl.BlockSpec(memory_space=pl.ANY),
        ],
        out_specs=pl.BlockSpec(memory_space=pl.ANY),
        scratch_shapes=[
            pltpu.VMEM(shape, source.dtype),
            pltpu.SemaphoreType.DMA((count,)),
            pltpu.SemaphoreType.DMA((count,)),
        ],
        cost_estimate=pl.CostEstimate(flops=0, bytes_accessed=2 * nbytes, transcendentals=0),
    )(index, source)


def rotate(values, positions):
    half_width = values.shape[-1] // 2
    frequencies = rope_base ** (
        -(jnp.arange(half_width, dtype=jnp.float32) * 2.0 / values.shape[-1])
    )
    angles = positions[..., None] * frequencies
    cosine_table = jnp.cos(angles)
    sine_table = jnp.sin(angles)
    lower_half = values[..., :half_width]
    upper_half = values[..., half_width:]
    return jnp.concatenate(
        [
            lower_half * cosine_table - upper_half * sine_table,
            upper_half * cosine_table + lower_half * sine_table,
        ],
        axis=-1,
    )


def body(
    normed,
    qkv_weight,
    out_weight,
    kv_cache,
    lengths,
    slot_request,
    slot_block,
    send_list,
    recv_list,
):
    group_size = HEADS // KV_HEADS
    scale_factor = HEAD ** (-0.5)
    requests = lengths.shape[0]
    slot_count = kv_cache.shape[0]
    n_seq = lax.axis_size("seq")
    n_head = lax.axis_size("head")
    me_seq = lax.axis_index("seq")
    rows = normed.shape[0]
    rows_per = rows // n_seq
    groups = qkv_weight.shape[1] // HEAD

    half_width = HEAD // 2
    frequencies = np.float32(rope_base) ** (
        -(np.arange(half_width, dtype=np.float32) * np.float32(2.0) / np.float32(HEAD))
    )
    freq_row = jnp.asarray(np.concatenate([frequencies, frequencies])[None, :].astype(np.float32))
    qkv, outgoing = qkv_exchange(
        normed, qkv_weight, freq_row, lengths, send_list.transpose(0, 2, 1), kv_cache, n_seq
    )
    qkv = qkv.reshape(requests, POS, 1, groups, HEAD)
    local_kv = 1

    outgoing = outgoing.reshape((lax.axis_size("seq"), -1) + kv_cache.shape[1:])
    incoming = lax.all_to_all(outgoing, "seq", split_axis=0, concat_axis=0, tiled=True)
    incoming = incoming.reshape((-1,) + kv_cache.shape[1:])
    arrivals = incoming.shape[0]
    source_of = (
        jnp.full((slot_count + 1,), arrivals, jnp.int32)
        .at[recv_list.reshape(-1)]
        .set(jnp.arange(arrivals, dtype=jnp.int32), mode="drop")[:slot_count]
    )
    queries = qkv[:, :, :, :group_size]
    keys_new = qkv[:, :, :, group_size]
    values_new = qkv[:, :, :, group_size + 1]

    slot_clip = jnp.minimum(slot_request, requests - 1)
    live_slot = slot_request < requests
    token_pos = slot_block[:, None] * BLOCK + jnp.arange(BLOCK, dtype=jnp.int32)[None, :]
    token_valid = (token_pos < lengths[slot_clip][:, None]) & live_slot[:, None]
    cache_view = kv_cache.reshape(slot_count, 2, BLOCK, local_kv, HEAD)
    gathered = queries[slot_clip]
    scores = (
        jnp.einsum(
            "sptgd,sbtd->stgpb", gathered, cache_view[:, 0], preferred_element_type=jnp.float32
        )
        * scale_factor
    )
    scores = jnp.where(token_valid[:, None, None, None, :], scores, neg_large)
    slot_max = jnp.max(scores, axis=-1)
    weights = jnp.where(
        token_valid[:, None, None, None, :], jnp.exp(scores - slot_max[..., None]), 0.0
    )
    slot_sum = jnp.sum(weights, axis=-1)
    slot_acc = jnp.einsum(
        "stgpb,sbtd->stgpd",
        weights.astype(jnp.bfloat16),
        cache_view[:, 1],
        preferred_element_type=jnp.float32,
    )
    flat_width = local_kv * group_size * POS
    slot_max_flat = slot_max.reshape(slot_count, flat_width)
    member = slot_request[:, None] == jnp.arange(requests, dtype=jnp.int32)[None, :]
    request_max = jnp.max(
        jnp.where(member[:, None, :], slot_max_flat[:, :, None], neg_large), axis=0
    ).T
    rescale = jnp.exp(slot_max_flat - request_max[slot_clip])
    member_float = member.astype(jnp.float32).T
    request_sum = jnp.dot(
        member_float,
        slot_sum.reshape(slot_count, flat_width) * rescale,
        precision=lax.Precision.HIGHEST,
    )
    scaled_acc = (slot_acc.reshape(slot_count, flat_width, HEAD) * rescale[:, :, None]).reshape(
        slot_count, flat_width * HEAD
    )
    request_acc = jnp.dot(member_float, scaled_acc, precision=lax.Precision.HIGHEST).reshape(
        requests, flat_width, HEAD
    )

    new_scores = (
        jnp.einsum("rptgd,rqtd->rtgpq", queries, keys_new, preferred_element_type=jnp.float32)
        * scale_factor
    )
    causal = jnp.arange(POS)[:, None] >= jnp.arange(POS)[None, :]
    new_scores = jnp.where(causal, new_scores, neg_large)
    new_max = jnp.max(new_scores, axis=-1)
    new_weights = jnp.where(causal, jnp.exp(new_scores - new_max[..., None]), 0.0)
    new_sum = jnp.sum(new_weights, axis=-1).reshape(requests, flat_width)
    new_acc = jnp.einsum(
        "rtgpq,rqtd->rtgpd",
        new_weights.astype(jnp.bfloat16),
        values_new,
        preferred_element_type=jnp.float32,
    ).reshape(requests, flat_width, HEAD)
    first = me_seq == 0
    new_max = jnp.where(first, new_max.reshape(requests, flat_width), neg_large)
    new_sum = jnp.where(first, new_sum, 0.0)
    new_acc = jnp.where(first, new_acc, 0.0)
    part_max = jnp.maximum(request_max, new_max)
    keep_old = jnp.exp(request_max - part_max)
    keep_new = jnp.exp(new_max - part_max)
    part_sum = request_sum * keep_old + new_sum * keep_new
    part_acc = request_acc * keep_old[..., None] + new_acc * keep_new[..., None]

    def by_chunk(values):
        lead = values.reshape(2, requests // 2, group_size, POS, -1).transpose(2, 0, 1, 3, 4)
        return lead.reshape(n_seq, requests * group_size * POS // n_seq, -1)

    chunk_rows = requests * flat_width // n_seq
    stats = jnp.concatenate(
        [
            by_chunk(part_max),
            by_chunk(part_sum),
            jnp.zeros((n_seq, chunk_rows, HEAD - 2), jnp.float32),
        ],
        axis=-1,
    )
    acc_chunks = by_chunk(part_acc).astype(jnp.bfloat16)
    source_of, acc_chunks, stats = lax.optimization_barrier((source_of, acc_chunks, stats))
    projected = attend_exchange(acc_chunks, stats, out_weight, n_head)
    moved_cache = pick_blocks(source_of, incoming, arrivals)
    return (projected, moved_cache)


def solution(mesh):
    placed = (
        P(None, "seq"),
        P("seq", "head"),
        P("head", "seq"),
        P("seq", None, None, "head"),
        P(),
        P("seq"),
        P("seq"),
        P("seq", None, None),
        P("seq", None, None),
    )
    return jax.shard_map(
        body,
        mesh=mesh,
        in_specs=placed,
        out_specs=(P("head", "seq"), P("seq", None, None, "head")),
        check_vma=False,
    )
```

```python
import functools

import jax
import numpy as np
import jax.numpy as jnp
from jax import lax
from jax.experimental import pallas as pl
from jax.experimental.pallas import tpu as pltpu
from jax.sharding import PartitionSpec as P

HEADS = 64
KV_HEADS = 8
HEAD = 128
POS = 4
BLOCK = 128

MESH = pl.DeviceIdType.MESH

rope_base = 500000.0
neg_large = -1e30


def _barrier(peers):
    barrier = pltpu.get_barrier_semaphore()
    for device in peers:
        pl.semaphore_signal(barrier, inc=1, device_id=device, device_id_type=MESH)
    pl.semaphore_wait(barrier, len(peers))


def _send_all(axis, n, me, src_of, land, send_sem, recv_sem):
    copies = []
    for i in range(1, n):
        peer = lax.rem(me + i, n)
        copy = pltpu.make_async_remote_copy(
            src_ref=src_of(peer),
            dst_ref=land.at[me],
            send_sem=send_sem.at[peer],
            recv_sem=recv_sem.at[me],
            device_id={axis: peer},
            device_id_type=MESH,
        )
        copy.start()
        copies.append(copy)
    return copies


def _wait_all(axis, n, me, land, send_sem, recv_sem):
    for i in range(1, n):
        src = lax.rem(me + n - i, n)
        pltpu.make_async_remote_copy(
            src_ref=land.at[src],
            dst_ref=land.at[src],
            send_sem=send_sem.at[src],
            recv_sem=recv_sem.at[src],
            device_id={axis: src},
            device_id_type=MESH,
        ).wait_recv()


def _qkv_kernel(
    n, limit, x_hbm, w_hbm, freq_ref, lengths_ref, pick_hbm, kv_hbm, out_ref, sent_hbm,
    x_vmem, w_vmem, part_ref, pick_ref, land_a, mine, land_b, sems, kv_vmem, sent_vmem, local_sems,
):
    me = lax.axis_index("seq")
    loads = [
        pltpu.make_async_copy(x_hbm, x_vmem, local_sems.at[2]),
        pltpu.make_async_copy(w_hbm, w_vmem, local_sems.at[3]),
        pltpu.make_async_copy(pick_hbm, pick_ref, local_sems.at[4]),
    ]
    for load in loads:
        load.start()
    kv_in = pltpu.make_async_copy(kv_hbm, kv_vmem, local_sems.at[0])
    kv_in.start()
    barrier = pltpu.get_barrier_semaphore()
    for i in range(1, n):
        pl.semaphore_signal(
            barrier, inc=1, device_id={"seq": lax.rem(me + i, n)}, device_id_type=MESH
        )
    for load in loads:
        load.wait()
    product = jnp.dot(x_vmem[...], w_vmem[...], preferred_element_type=jnp.float32)
    groups = product.shape[1] // HEAD
    per = part_ref.shape[1] // groups
    for j in range(n):
        for k in range(per):
            row = product[per * j + k : per * j + k + 1]
            for g in range(groups):
                part_ref[j, k * groups + g : k * groups + g + 1, :] = row[:, g * HEAD : (g + 1) * HEAD]
    land_a[me] = part_ref[me]
    pl.semaphore_wait(barrier, n - 1)
    sent_a = _send_all("seq", n, me, lambda p: part_ref.at[p], land_a, sems.at[0], sems.at[1])
    kv_in.wait()

    def pick(j, carry):
        per = pick_ref.shape[1]
        sent_vmem[j] = kv_vmem[jnp.minimum(pick_ref[0, j % per, j // per], limit - 1)]
        return carry

    lax.fori_loop(0, sent_vmem.shape[0], pick, 0)
    kv_out = pltpu.make_async_copy(sent_vmem, sent_hbm, local_sems.at[1])
    kv_out.start()
    _wait_all("seq", n, me, land_a, sems.at[0], sems.at[1])
    total = land_a[0]
    for i in range(1, n):
        total = total + land_a[i]
    g = total.shape[0] // 2
    first_row = 2 * me
    second_row = first_row + 1
    pos_a = (lengths_ref[first_row // POS] + first_row % POS).astype(jnp.float32)
    pos_b = (lengths_ref[second_row // POS] + second_row % POS).astype(jnp.float32)
    row = lax.broadcasted_iota(jnp.int32, total.shape, 0)
    lane = lax.broadcasted_iota(jnp.int32, total.shape, 1)
    angle = jnp.where(row < g, pos_a, pos_b) * freq_ref[...]
    value_row = (row == g - 1) | (row == 2 * g - 1)
    cosine = jnp.where(value_row, 1.0, jnp.cos(angle))
    sine = jnp.where(value_row, 0.0, jnp.where(lane < HEAD // 2, -jnp.sin(angle), jnp.sin(angle)))
    turned = pltpu.roll(total, HEAD // 2, 1)
    rotated = (total * cosine + turned * sine).astype(mine.dtype)
    mine[...] = rotated
    land_b[me] = rotated
    sent_b = _send_all("seq", n, me, lambda p: mine, land_b, sems.at[2], sems.at[3])
    _wait_all("seq", n, me, land_b, sems.at[2], sems.at[3])
    for copy in sent_a + sent_b:
        copy.wait_send()
    out_ref[...] = land_b[...]
    kv_out.wait()


def qkv_exchange(normed, qkv_weight, freq, lengths, pick, kv_cache, n):
    rows = normed.shape[0]
    groups = qkv_weight.shape[1] // HEAD
    chunk = (n, rows // n * groups, HEAD)
    picked = (pick.size,) + kv_cache.shape[1:]
    return pl.pallas_call(
        functools.partial(_qkv_kernel, n, kv_cache.shape[0]),
        out_shape=(
            jax.ShapeDtypeStruct(chunk, jnp.bfloat16),
            jax.ShapeDtypeStruct(picked, kv_cache.dtype),
        ),
        in_specs=[pl.BlockSpec(memory_space=pl.ANY)] * 2
        + [pl.BlockSpec(memory_space=pltpu.VMEM), pl.BlockSpec(memory_space=pltpu.SMEM)]
        + [pl.BlockSpec(memory_space=pl.ANY)] * 2,
        out_specs=(pl.BlockSpec(memory_space=pltpu.VMEM), pl.BlockSpec(memory_space=pl.ANY)),
        scratch_shapes=[
            pltpu.VMEM(normed.shape, normed.dtype),
            pltpu.VMEM(qkv_weight.shape, qkv_weight.dtype),
            pltpu.VMEM(chunk, jnp.float32),
            pltpu.SMEM(pick.shape, pick.dtype),
            pltpu.VMEM(chunk, jnp.float32),
            pltpu.VMEM(chunk[1:], jnp.bfloat16),
            pltpu.VMEM(chunk, jnp.bfloat16),
            pltpu.SemaphoreType.DMA((4, n)),
            pltpu.VMEM(kv_cache.shape, kv_cache.dtype),
            pltpu.VMEM(picked, kv_cache.dtype),
            pltpu.SemaphoreType.DMA((5,)),
        ],
        compiler_params=pltpu.CompilerParams(collective_id=0, has_side_effects=True),
        cost_estimate=pl.CostEstimate(
            flops=2 * rows * normed.shape[1] * qkv_weight.shape[1],
            bytes_accessed=qkv_weight.size * 2 + 2 * kv_cache.size * kv_cache.dtype.itemsize,
            transcendentals=0,
        ),
    )(normed, qkv_weight, freq, lengths, pick, kv_cache)


def _attend_kernel(
    n, m, rows, acc_ref, stats_ref, w_ref, out_ref, land_p, land_s, mine, land_a, part_c, land_c,
    sems,
):
    me = lax.axis_index("seq")
    me_h = lax.axis_index("head")
    land_p[me] = acc_ref[me]
    land_s[me] = stats_ref[me]
    _barrier(
        [{"seq": lax.rem(me + i, n)} for i in range(1, n)]
        + [{"head": lax.rem(me_h + i, m)} for i in range(1, m)]
    )
    sent_p = _send_all("seq", n, me, lambda p: acc_ref.at[p], land_p, sems.at[0], sems.at[1])
    sent_s = _send_all("seq", n, me, lambda p: stats_ref.at[p], land_s, sems.at[6], sems.at[7])
    _wait_all("seq", n, me, land_s, sems.at[6], sems.at[7])
    _wait_all("seq", n, me, land_p, sems.at[0], sems.at[1])
    top = land_s[0, :, 0:1]
    for i in range(1, n):
        top = jnp.maximum(top, land_s[i, :, 0:1])
    numerator = jnp.zeros((rows, HEAD), jnp.float32)
    denominator = jnp.zeros((rows, 1), jnp.float32)
    for i in range(n):
        scale = jnp.exp(land_s[i, :, 0:1] - top)
        denominator = denominator + land_s[i, :, 1:2] * scale
        numerator = numerator + land_p[i].astype(jnp.float32) * scale
    attended = (numerator / denominator).astype(mine.dtype)
    mine[...] = attended
    land_a[me] = attended
    sent_a = _send_all("seq", n, me, lambda p: mine, land_a, sems.at[2], sems.at[3])
    _wait_all("seq", n, me, land_a, sems.at[2], sems.at[3])
    heads = n // 2
    projected = None
    for g in range(heads):
        lhs = land_a[2 * g : 2 * g + 2].reshape(2 * rows, HEAD)
        term = jnp.dot(lhs, w_ref[g * HEAD : (g + 1) * HEAD, :], preferred_element_type=jnp.float32)
        projected = term if projected is None else projected + term
    per = part_c.shape[1]
    for j in range(m):
        part_c[j] = projected[j * per : (j + 1) * per]
    land_c[me_h] = part_c[me_h]
    sent_c = _send_all("head", m, me_h, lambda p: part_c.at[p], land_c, sems.at[4], sems.at[5])
    _wait_all("head", m, me_h, land_c, sems.at[4], sems.at[5])
    total = land_c[0]
    for j in range(1, m):
        total = total + land_c[j]
    for copy in sent_p + sent_s + sent_a + sent_c:
        copy.wait_send()
    out_ref[...] = total.astype(out_ref.dtype)


def attend_exchange(acc, stats, out_weight, m):
    n, rows, _ = acc.shape
    width = out_weight.shape[1]
    per = 2 * rows // m
    return pl.pallas_call(
        functools.partial(_attend_kernel, n, m, rows),
        out_shape=jax.ShapeDtypeStruct((per, width), jnp.bfloat16),
        in_specs=[pl.BlockSpec(memory_space=pltpu.VMEM)] * 3,
        out_specs=pl.BlockSpec(memory_space=pltpu.VMEM),
        scratch_shapes=[
            pltpu.VMEM(acc.shape, acc.dtype),
            pltpu.VMEM(stats.shape, jnp.float32),
            pltpu.VMEM((rows, HEAD), jnp.bfloat16),
            pltpu.VMEM((n, rows, HEAD), jnp.bfloat16),
            pltpu.VMEM((m, per, width), jnp.float32),
            pltpu.VMEM((m, per, width), jnp.float32),
            pltpu.SemaphoreType.DMA((8, max(n, m))),
        ],
        compiler_params=pltpu.CompilerParams(collective_id=1, has_side_effects=True),
        cost_estimate=pl.CostEstimate(
            flops=2 * 2 * rows * out_weight.shape[0] * width,
            bytes_accessed=acc.size * 4 + stats.size * 8 + out_weight.size * 2,
            transcendentals=n * rows * HEAD,
        ),
    )(acc, stats, out_weight)


def _place_kernel(limit, index_ref, src_hbm, out_hbm, buf, res, sems):
    load = pltpu.make_async_copy(src_hbm, buf, sems.at[0])
    load.start()
    load.wait()
    count = res.shape[0]
    half = count // 2

    def put(j, carry):
        k = index_ref[j]
        block = buf[jnp.minimum(k, limit - 1)]
        res[j] = jnp.where(k < limit, block, jnp.zeros_like(block))
        return carry

    lax.fori_loop(0, half, put, 0)
    first = pltpu.make_async_copy(res.at[pl.ds(0, half)], out_hbm.at[pl.ds(0, half)], sems.at[1])
    first.start()
    lax.fori_loop(half, count, put, 0)
    second = pltpu.make_async_copy(
        res.at[pl.ds(half, count - half)], out_hbm.at[pl.ds(half, count - half)], sems.at[2]
    )
    second.start()
    first.wait()
    second.wait()


def pick_blocks(index, source, limit):
    count = index.shape[0]
    shape = (count,) + source.shape[1:]
    nbytes = count * source[0].size * source.dtype.itemsize
    return pl.pallas_call(
        functools.partial(_place_kernel, limit),
        out_shape=jax.ShapeDtypeStruct(shape, source.dtype),
        in_specs=[
            pl.BlockSpec(memory_space=pltpu.SMEM),
            pl.BlockSpec(memory_space=pl.ANY),
        ],
        out_specs=pl.BlockSpec(memory_space=pl.ANY),
        scratch_shapes=[
            pltpu.VMEM(source.shape, source.dtype),
            pltpu.VMEM(shape, source.dtype),
            pltpu.SemaphoreType.DMA((3,)),
        ],
        cost_estimate=pl.CostEstimate(flops=0, bytes_accessed=2 * nbytes, transcendentals=0),
    )(index, source)


def rotate(values, positions):
    half_width = values.shape[-1] // 2
    frequencies = rope_base ** (
        -(jnp.arange(half_width, dtype=jnp.float32) * 2.0 / values.shape[-1])
    )
    angles = positions[..., None] * frequencies
    cosine_table = jnp.cos(angles)
    sine_table = jnp.sin(angles)
    lower_half = values[..., :half_width]
    upper_half = values[..., half_width:]
    return jnp.concatenate(
        [
            lower_half * cosine_table - upper_half * sine_table,
            upper_half * cosine_table + lower_half * sine_table,
        ],
        axis=-1,
    )


def body(
    normed,
    qkv_weight,
    out_weight,
    kv_cache,
    lengths,
    slot_request,
    slot_block,
    send_list,
    recv_list,
):
    group_size = HEADS // KV_HEADS
    scale_factor = HEAD ** (-0.5)
    requests = lengths.shape[0]
    slot_count = kv_cache.shape[0]
    n_seq = lax.axis_size("seq")
    n_head = lax.axis_size("head")
    me_seq = lax.axis_index("seq")
    rows = normed.shape[0]
    rows_per = rows // n_seq
    groups = qkv_weight.shape[1] // HEAD

    half_width = HEAD // 2
    frequencies = np.float32(rope_base) ** (
        -(np.arange(half_width, dtype=np.float32) * np.float32(2.0) / np.float32(HEAD))
    )
    freq_row = jnp.asarray(np.concatenate([frequencies, frequencies])[None, :].astype(np.float32))
    qkv, outgoing = qkv_exchange(
        normed, qkv_weight, freq_row, lengths, send_list.transpose(0, 2, 1), kv_cache, n_seq
    )
    qkv = qkv.reshape(requests, POS, 1, groups, HEAD)
    local_kv = 1

    outgoing = outgoing.reshape((lax.axis_size("seq"), -1) + kv_cache.shape[1:])
    incoming = lax.all_to_all(outgoing, "seq", split_axis=0, concat_axis=0, tiled=True)
    incoming = incoming.reshape((-1,) + kv_cache.shape[1:])
    arrivals = incoming.shape[0]
    source_of = (
        jnp.full((slot_count + 1,), arrivals, jnp.int32)
        .at[recv_list.reshape(-1)]
        .set(jnp.arange(arrivals, dtype=jnp.int32), mode="drop")[:slot_count]
    )
    queries = qkv[:, :, :, :group_size]
    keys_new = qkv[:, :, :, group_size]
    values_new = qkv[:, :, :, group_size + 1]

    slot_clip = jnp.minimum(slot_request, requests - 1)
    live_slot = slot_request < requests
    token_pos = slot_block[:, None] * BLOCK + jnp.arange(BLOCK, dtype=jnp.int32)[None, :]
    token_valid = (token_pos < lengths[slot_clip][:, None]) & live_slot[:, None]
    cache_view = kv_cache.reshape(slot_count, 2, BLOCK, local_kv, HEAD)
    gathered = queries[slot_clip]
    scores = (
        jnp.einsum(
            "sptgd,sbtd->stgpb", gathered, cache_view[:, 0], preferred_element_type=jnp.float32
        )
        * scale_factor
    )
    scores = jnp.where(token_valid[:, None, None, None, :], scores, neg_large)
    slot_max = jnp.max(scores, axis=-1)
    weights = jnp.where(
        token_valid[:, None, None, None, :], jnp.exp(scores - slot_max[..., None]), 0.0
    )
    slot_sum = jnp.sum(weights, axis=-1)
    slot_acc = jnp.einsum(
        "stgpb,sbtd->stgpd",
        weights.astype(jnp.bfloat16),
        cache_view[:, 1],
        preferred_element_type=jnp.float32,
    )
    flat_width = local_kv * group_size * POS
    slot_max_flat = slot_max.reshape(slot_count, flat_width)
    member = slot_request[:, None] == jnp.arange(requests, dtype=jnp.int32)[None, :]
    request_max = jnp.max(
        jnp.where(member[:, None, :], slot_max_flat[:, :, None], neg_large), axis=0
    ).T
    rescale = jnp.exp(slot_max_flat - request_max[slot_clip])
    member_float = member.astype(jnp.float32).T
    request_sum = jnp.dot(
        member_float,
        slot_sum.reshape(slot_count, flat_width) * rescale,
        precision=lax.Precision.HIGHEST,
    )
    scaled_acc = (slot_acc.reshape(slot_count, flat_width, HEAD) * rescale[:, :, None]).reshape(
        slot_count, flat_width * HEAD
    )
    request_acc = jnp.dot(member_float, scaled_acc, precision=lax.Precision.HIGHEST).reshape(
        requests, flat_width, HEAD
    )

    new_scores = (
        jnp.einsum("rptgd,rqtd->rtgpq", queries, keys_new, preferred_element_type=jnp.float32)
        * scale_factor
    )
    causal = jnp.arange(POS)[:, None] >= jnp.arange(POS)[None, :]
    new_scores = jnp.where(causal, new_scores, neg_large)
    new_max = jnp.max(new_scores, axis=-1)
    new_weights = jnp.where(causal, jnp.exp(new_scores - new_max[..., None]), 0.0)
    new_sum = jnp.sum(new_weights, axis=-1).reshape(requests, flat_width)
    new_acc = jnp.einsum(
        "rtgpq,rqtd->rtgpd",
        new_weights.astype(jnp.bfloat16),
        values_new,
        preferred_element_type=jnp.float32,
    ).reshape(requests, flat_width, HEAD)
    first = me_seq == 0
    new_max = jnp.where(first, new_max.reshape(requests, flat_width), neg_large)
    new_sum = jnp.where(first, new_sum, 0.0)
    new_acc = jnp.where(first, new_acc, 0.0)
    part_max = jnp.maximum(request_max, new_max)
    keep_old = jnp.exp(request_max - part_max)
    keep_new = jnp.exp(new_max - part_max)
    part_sum = request_sum * keep_old + new_sum * keep_new
    part_acc = request_acc * keep_old[..., None] + new_acc * keep_new[..., None]

    def by_chunk(values):
        lead = values.reshape(2, requests // 2, group_size, POS, -1).transpose(2, 0, 1, 3, 4)
        return lead.reshape(n_seq, requests * group_size * POS // n_seq, -1)

    chunk_rows = requests * flat_width // n_seq
    stats = jnp.concatenate(
        [
            by_chunk(part_max),
            by_chunk(part_sum),
            jnp.zeros((n_seq, chunk_rows, HEAD - 2), jnp.float32),
        ],
        axis=-1,
    )
    acc_chunks = by_chunk(part_acc).astype(jnp.bfloat16)
    source_of, acc_chunks, stats = lax.optimization_barrier((source_of, acc_chunks, stats))
    projected = attend_exchange(acc_chunks, stats, out_weight, n_head)
    moved_cache = pick_blocks(source_of, incoming, arrivals)
    return (projected, moved_cache)


def solution(mesh):
    placed = (
        P(None, "seq"),
        P("seq", "head"),
        P("head", "seq"),
        P("seq", None, None, "head"),
        P(),
        P("seq"),
        P("seq"),
        P("seq", None, None),
        P("seq", None, None),
    )
    return jax.shard_map(
        body,
        mesh=mesh,
        in_specs=placed,
        out_specs=(P("head", "seq"), P("seq", None, None, "head")),
        check_vma=False,
    )
```

```python
import functools

import jax
import numpy as np
import jax.numpy as jnp
from jax import lax
from jax.experimental import pallas as pl
from jax.experimental.pallas import tpu as pltpu
from jax.sharding import PartitionSpec as P

HEADS = 64
KV_HEADS = 8
HEAD = 128
POS = 4
BLOCK = 128

MESH = pl.DeviceIdType.MESH

rope_base = 500000.0
neg_large = -1e30


def _barrier(peers):
    barrier = pltpu.get_barrier_semaphore()
    for device in peers:
        pl.semaphore_signal(barrier, inc=1, device_id=device, device_id_type=MESH)
    pl.semaphore_wait(barrier, len(peers))


def _send_all(axis, n, me, src_of, land, send_sem, recv_sem):
    copies = []
    for i in range(1, n):
        peer = lax.rem(me + i, n)
        copy = pltpu.make_async_remote_copy(
            src_ref=src_of(peer),
            dst_ref=land.at[me],
            send_sem=send_sem.at[peer],
            recv_sem=recv_sem.at[me],
            device_id={axis: peer},
            device_id_type=MESH,
        )
        copy.start()
        copies.append(copy)
    return copies


def _wait_all(axis, n, me, land, send_sem, recv_sem):
    for i in range(1, n):
        src = lax.rem(me + n - i, n)
        pltpu.make_async_remote_copy(
            src_ref=land.at[src],
            dst_ref=land.at[src],
            send_sem=send_sem.at[src],
            recv_sem=recv_sem.at[src],
            device_id={axis: src},
            device_id_type=MESH,
        ).wait_recv()


def _qkv_kernel(
    n, limit, x_hbm, w_hbm, freq_ref, lengths_ref, pick_hbm, kv_hbm, out_ref, sent_hbm,
    x_vmem, w_vmem, part_ref, pick_ref, land_a, mine, land_b, sems, kv_vmem, sent_vmem, local_sems,
):
    me = lax.axis_index("seq")
    loads = [
        pltpu.make_async_copy(x_hbm, x_vmem, local_sems.at[2]),
        pltpu.make_async_copy(w_hbm, w_vmem, local_sems.at[3]),
        pltpu.make_async_copy(pick_hbm, pick_ref, local_sems.at[4]),
    ]
    for load in loads:
        load.start()
    kv_in = pltpu.make_async_copy(kv_hbm, kv_vmem, local_sems.at[0])
    kv_in.start()
    barrier = pltpu.get_barrier_semaphore()
    for i in range(1, n):
        pl.semaphore_signal(
            barrier, inc=1, device_id={"seq": lax.rem(me + i, n)}, device_id_type=MESH
        )
    for load in loads:
        load.wait()
    product = jnp.dot(x_vmem[...], w_vmem[...], preferred_element_type=jnp.float32)
    groups = product.shape[1] // HEAD
    per = part_ref.shape[1] // groups
    for j in range(n):
        for k in range(per):
            row = product[per * j + k : per * j + k + 1]
            for g in range(groups):
                part_ref[j, k * groups + g : k * groups + g + 1, :] = row[:, g * HEAD : (g + 1) * HEAD]
    land_a[me] = part_ref[me]
    pl.semaphore_wait(barrier, n - 1)
    sent_a = _send_all("seq", n, me, lambda p: part_ref.at[p], land_a, sems.at[0], sems.at[1])
    kv_in.wait()

    def pick(j, carry):
        per = pick_ref.shape[1]
        sent_vmem[j] = kv_vmem[jnp.minimum(pick_ref[0, j % per, j // per], limit - 1)]
        return carry

    lax.fori_loop(0, sent_vmem.shape[0], pick, 0)
    kv_out = pltpu.make_async_copy(sent_vmem, sent_hbm, local_sems.at[1])
    kv_out.start()
    _wait_all("seq", n, me, land_a, sems.at[0], sems.at[1])
    total = land_a[0]
    for i in range(1, n):
        total = total + land_a[i]
    g = total.shape[0] // 2
    first_row = 2 * me
    second_row = first_row + 1
    pos_a = (lengths_ref[first_row // POS] + first_row % POS).astype(jnp.float32)
    pos_b = (lengths_ref[second_row // POS] + second_row % POS).astype(jnp.float32)
    row = lax.broadcasted_iota(jnp.int32, total.shape, 0)
    lane = lax.broadcasted_iota(jnp.int32, total.shape, 1)
    angle = jnp.where(row < g, pos_a, pos_b) * freq_ref[...]
    value_row = (row == g - 1) | (row == 2 * g - 1)
    cosine = jnp.where(value_row, 1.0, jnp.cos(angle))
    sine = jnp.where(value_row, 0.0, jnp.where(lane < HEAD // 2, -jnp.sin(angle), jnp.sin(angle)))
    turned = pltpu.roll(total, HEAD // 2, 1)
    rotated = (total * cosine + turned * sine).astype(mine.dtype)
    mine[...] = rotated
    land_b[me] = rotated
    sent_b = _send_all("seq", n, me, lambda p: mine, land_b, sems.at[2], sems.at[3])
    _wait_all("seq", n, me, land_b, sems.at[2], sems.at[3])
    for copy in sent_a + sent_b:
        copy.wait_send()
    out_ref[...] = land_b[...]
    kv_out.wait()


def qkv_exchange(normed, qkv_weight, freq, lengths, pick, kv_cache, n):
    rows = normed.shape[0]
    groups = qkv_weight.shape[1] // HEAD
    chunk = (n, rows // n * groups, HEAD)
    picked = (pick.size,) + kv_cache.shape[1:]
    return pl.pallas_call(
        functools.partial(_qkv_kernel, n, kv_cache.shape[0]),
        out_shape=(
            jax.ShapeDtypeStruct(chunk, jnp.bfloat16),
            jax.ShapeDtypeStruct(picked, kv_cache.dtype),
        ),
        in_specs=[pl.BlockSpec(memory_space=pl.ANY)] * 2
        + [pl.BlockSpec(memory_space=pltpu.VMEM), pl.BlockSpec(memory_space=pltpu.SMEM)]
        + [pl.BlockSpec(memory_space=pl.ANY)] * 2,
        out_specs=(pl.BlockSpec(memory_space=pltpu.VMEM), pl.BlockSpec(memory_space=pl.ANY)),
        scratch_shapes=[
            pltpu.VMEM(normed.shape, normed.dtype),
            pltpu.VMEM(qkv_weight.shape, qkv_weight.dtype),
            pltpu.VMEM(chunk, jnp.float32),
            pltpu.SMEM(pick.shape, pick.dtype),
            pltpu.VMEM(chunk, jnp.float32),
            pltpu.VMEM(chunk[1:], jnp.bfloat16),
            pltpu.VMEM(chunk, jnp.bfloat16),
            pltpu.SemaphoreType.DMA((4, n)),
            pltpu.VMEM(kv_cache.shape, kv_cache.dtype),
            pltpu.VMEM(picked, kv_cache.dtype),
            pltpu.SemaphoreType.DMA((5,)),
        ],
        compiler_params=pltpu.CompilerParams(collective_id=0, has_side_effects=True),
        cost_estimate=pl.CostEstimate(
            flops=2 * rows * normed.shape[1] * qkv_weight.shape[1],
            bytes_accessed=qkv_weight.size * 2 + 2 * kv_cache.size * kv_cache.dtype.itemsize,
            transcendentals=0,
        ),
    )(normed, qkv_weight, freq, lengths, pick, kv_cache)


def _attend_kernel(
    n, m, rows, acc_ref, stats_ref, w_ref, out_ref, land_p, land_s, mine, land_a, part_c, land_c,
    sems,
):
    me = lax.axis_index("seq")
    me_h = lax.axis_index("head")
    land_p[me] = acc_ref[me]
    land_s[me] = stats_ref[me]
    _barrier(
        [{"seq": lax.rem(me + i, n)} for i in range(1, n)]
        + [{"head": lax.rem(me_h + i, m)} for i in range(1, m)]
    )
    sent_p = _send_all("seq", n, me, lambda p: acc_ref.at[p], land_p, sems.at[0], sems.at[1])
    sent_s = _send_all("seq", n, me, lambda p: stats_ref.at[p], land_s, sems.at[6], sems.at[7])
    _wait_all("seq", n, me, land_s, sems.at[6], sems.at[7])
    _wait_all("seq", n, me, land_p, sems.at[0], sems.at[1])
    columns = [land_s[i].T for i in range(n)]
    top = columns[0][:rows, 0:1]
    for i in range(1, n):
        top = jnp.maximum(top, columns[i][:rows, 0:1])
    numerator = jnp.zeros((rows, HEAD), jnp.float32)
    denominator = jnp.zeros((rows, 1), jnp.float32)
    for i in range(n):
        scale = jnp.exp(columns[i][:rows, 0:1] - top)
        denominator = denominator + columns[i][rows : 2 * rows, 0:1] * scale
        numerator = numerator + land_p[i].astype(jnp.float32) * scale
    attended = (numerator / denominator).astype(mine.dtype)
    mine[...] = attended
    land_a[me] = attended
    sent_a = _send_all("seq", n, me, lambda p: mine, land_a, sems.at[2], sems.at[3])
    _wait_all("seq", n, me, land_a, sems.at[2], sems.at[3])
    heads = n // 2
    projected = None
    for g in range(heads):
        lhs = land_a[2 * g : 2 * g + 2].reshape(2 * rows, HEAD)
        term = jnp.dot(lhs, w_ref[g * HEAD : (g + 1) * HEAD, :], preferred_element_type=jnp.float32)
        projected = term if projected is None else projected + term
    per = part_c.shape[1]
    for j in range(m):
        part_c[j] = projected[j * per : (j + 1) * per]
    land_c[me_h] = part_c[me_h]
    sent_c = _send_all("head", m, me_h, lambda p: part_c.at[p], land_c, sems.at[4], sems.at[5])
    _wait_all("head", m, me_h, land_c, sems.at[4], sems.at[5])
    total = land_c[0]
    for j in range(1, m):
        total = total + land_c[j]
    for copy in sent_p + sent_s + sent_a + sent_c:
        copy.wait_send()
    out_ref[...] = total.astype(out_ref.dtype)


def attend_exchange(acc, stats, out_weight, m):
    n, rows, _ = acc.shape
    width = out_weight.shape[1]
    per = 2 * rows // m
    return pl.pallas_call(
        functools.partial(_attend_kernel, n, m, rows),
        out_shape=jax.ShapeDtypeStruct((per, width), jnp.bfloat16),
        in_specs=[pl.BlockSpec(memory_space=pltpu.VMEM)] * 3,
        out_specs=pl.BlockSpec(memory_space=pltpu.VMEM),
        scratch_shapes=[
            pltpu.VMEM(acc.shape, acc.dtype),
            pltpu.VMEM(stats.shape, jnp.float32),
            pltpu.VMEM((rows, HEAD), jnp.bfloat16),
            pltpu.VMEM((n, rows, HEAD), jnp.bfloat16),
            pltpu.VMEM((m, per, width), jnp.float32),
            pltpu.VMEM((m, per, width), jnp.float32),
            pltpu.SemaphoreType.DMA((8, max(n, m))),
        ],
        compiler_params=pltpu.CompilerParams(collective_id=1, has_side_effects=True),
        cost_estimate=pl.CostEstimate(
            flops=2 * 2 * rows * out_weight.shape[0] * width,
            bytes_accessed=acc.size * 4 + stats.size * 8 + out_weight.size * 2,
            transcendentals=n * rows * HEAD,
        ),
    )(acc, stats, out_weight)


def _pick_kernel(limit, index_ref, src_hbm, out_hbm, buf, sems, out_sem):
    count = buf.shape[0]

    def start(j, carry):
        k = index_ref[j]

        @pl.when(k < limit)
        def _():
            pltpu.make_async_copy(src_hbm.at[jnp.minimum(k, limit - 1)], buf.at[j], sems.at[j]).start()

        @pl.when(k >= limit)
        def _():
            buf[j] = jnp.zeros(buf.shape[1:], buf.dtype)

        return carry

    def send(j, carry):
        k = index_ref[j]

        @pl.when(k < limit)
        def _():
            pltpu.make_async_copy(src_hbm.at[0], buf.at[j], sems.at[j]).wait()

        pltpu.make_async_copy(buf.at[j], out_hbm.at[j], out_sem.at[j]).start()
        return carry

    def finish(j, carry):
        pltpu.make_async_copy(buf.at[j], out_hbm.at[j], out_sem.at[j]).wait()
        return carry

    lax.fori_loop(0, count, start, 0)
    lax.fori_loop(0, count, send, 0)
    lax.fori_loop(0, count, finish, 0)


def pick_blocks(index, source, limit):
    count = index.shape[0]
    shape = (count,) + source.shape[1:]
    nbytes = count * source[0].size * source.dtype.itemsize
    return pl.pallas_call(
        functools.partial(_pick_kernel, limit),
        out_shape=jax.ShapeDtypeStruct(shape, source.dtype),
        in_specs=[
            pl.BlockSpec(memory_space=pltpu.SMEM),
            pl.BlockSpec(memory_space=pl.ANY),
        ],
        out_specs=pl.BlockSpec(memory_space=pl.ANY),
        scratch_shapes=[
            pltpu.VMEM(shape, source.dtype),
            pltpu.SemaphoreType.DMA((count,)),
            pltpu.SemaphoreType.DMA((count,)),
        ],
        cost_estimate=pl.CostEstimate(flops=0, bytes_accessed=2 * nbytes, transcendentals=0),
    )(index, source)


def rotate(values, positions):
    half_width = values.shape[-1] // 2
    frequencies = rope_base ** (
        -(jnp.arange(half_width, dtype=jnp.float32) * 2.0 / values.shape[-1])
    )
    angles = positions[..., None] * frequencies
    cosine_table = jnp.cos(angles)
    sine_table = jnp.sin(angles)
    lower_half = values[..., :half_width]
    upper_half = values[..., half_width:]
    return jnp.concatenate(
        [
            lower_half * cosine_table - upper_half * sine_table,
            upper_half * cosine_table + lower_half * sine_table,
        ],
        axis=-1,
    )


def body(
    normed,
    qkv_weight,
    out_weight,
    kv_cache,
    lengths,
    slot_request,
    slot_block,
    send_list,
    recv_list,
):
    group_size = HEADS // KV_HEADS
    scale_factor = HEAD ** (-0.5)
    requests = lengths.shape[0]
    slot_count = kv_cache.shape[0]
    n_seq = lax.axis_size("seq")
    n_head = lax.axis_size("head")
    me_seq = lax.axis_index("seq")
    rows = normed.shape[0]
    rows_per = rows // n_seq
    groups = qkv_weight.shape[1] // HEAD

    half_width = HEAD // 2
    frequencies = np.float32(rope_base) ** (
        -(np.arange(half_width, dtype=np.float32) * np.float32(2.0) / np.float32(HEAD))
    )
    freq_row = jnp.asarray(np.concatenate([frequencies, frequencies])[None, :].astype(np.float32))
    qkv, outgoing = qkv_exchange(
        normed, qkv_weight, freq_row, lengths, send_list.transpose(0, 2, 1), kv_cache, n_seq
    )
    qkv = qkv.reshape(requests, POS, 1, groups, HEAD)
    local_kv = 1

    outgoing = outgoing.reshape((lax.axis_size("seq"), -1) + kv_cache.shape[1:])
    incoming = lax.all_to_all(outgoing, "seq", split_axis=0, concat_axis=0, tiled=True)
    incoming = incoming.reshape((-1,) + kv_cache.shape[1:])
    arrivals = incoming.shape[0]
    source_of = (
        jnp.full((slot_count + 1,), arrivals, jnp.int32)
        .at[recv_list.reshape(-1)]
        .set(jnp.arange(arrivals, dtype=jnp.int32), mode="drop")[:slot_count]
    )
    queries = qkv[:, :, :, :group_size]
    keys_new = qkv[:, :, :, group_size]
    values_new = qkv[:, :, :, group_size + 1]

    slot_clip = jnp.minimum(slot_request, requests - 1)
    live_slot = slot_request < requests
    token_pos = slot_block[:, None] * BLOCK + jnp.arange(BLOCK, dtype=jnp.int32)[None, :]
    token_valid = (token_pos < lengths[slot_clip][:, None]) & live_slot[:, None]
    cache_view = kv_cache.reshape(slot_count, 2, BLOCK, local_kv, HEAD)
    gathered = queries[slot_clip]
    scores = (
        jnp.einsum(
            "sptgd,sbtd->stgpb", gathered, cache_view[:, 0], preferred_element_type=jnp.float32
        )
        * scale_factor
    )
    scores = jnp.where(token_valid[:, None, None, None, :], scores, neg_large)
    slot_max = jnp.max(scores, axis=-1)
    weights = jnp.where(
        token_valid[:, None, None, None, :], jnp.exp(scores - slot_max[..., None]), 0.0
    )
    slot_sum = jnp.sum(weights, axis=-1)
    slot_acc = jnp.einsum(
        "stgpb,sbtd->stgpd",
        weights.astype(jnp.bfloat16),
        cache_view[:, 1],
        preferred_element_type=jnp.float32,
    )
    flat_width = local_kv * group_size * POS
    slot_max_flat = slot_max.reshape(slot_count, flat_width)
    member = slot_request[:, None] == jnp.arange(requests, dtype=jnp.int32)[None, :]
    request_max = jnp.max(
        jnp.where(member[:, None, :], slot_max_flat[:, :, None], neg_large), axis=0
    ).T
    rescale = jnp.exp(slot_max_flat - request_max[slot_clip])
    member_float = member.astype(jnp.float32).T
    request_sum = jnp.dot(
        member_float,
        slot_sum.reshape(slot_count, flat_width) * rescale,
        precision=lax.Precision.HIGHEST,
    )
    scaled_acc = (slot_acc.reshape(slot_count, flat_width, HEAD) * rescale[:, :, None]).reshape(
        slot_count, flat_width * HEAD
    )
    request_acc = jnp.dot(member_float, scaled_acc, precision=lax.Precision.HIGHEST).reshape(
        requests, flat_width, HEAD
    )

    new_scores = (
        jnp.einsum("rptgd,rqtd->rtgpq", queries, keys_new, preferred_element_type=jnp.float32)
        * scale_factor
    )
    causal = jnp.arange(POS)[:, None] >= jnp.arange(POS)[None, :]
    new_scores = jnp.where(causal, new_scores, neg_large)
    new_max = jnp.max(new_scores, axis=-1)
    new_weights = jnp.where(causal, jnp.exp(new_scores - new_max[..., None]), 0.0)
    new_sum = jnp.sum(new_weights, axis=-1).reshape(requests, flat_width)
    new_acc = jnp.einsum(
        "rtgpq,rqtd->rtgpd",
        new_weights.astype(jnp.bfloat16),
        values_new,
        preferred_element_type=jnp.float32,
    ).reshape(requests, flat_width, HEAD)
    first = me_seq == 0
    new_max = jnp.where(first, new_max.reshape(requests, flat_width), neg_large)
    new_sum = jnp.where(first, new_sum, 0.0)
    new_acc = jnp.where(first, new_acc, 0.0)
    part_max = jnp.maximum(request_max, new_max)
    keep_old = jnp.exp(request_max - part_max)
    keep_new = jnp.exp(new_max - part_max)
    part_sum = request_sum * keep_old + new_sum * keep_new
    part_acc = request_acc * keep_old[..., None] + new_acc * keep_new[..., None]

    def by_chunk(values):
        lead = values.reshape(2, requests // 2, group_size, POS, -1).transpose(2, 0, 1, 3, 4)
        return lead.reshape(n_seq, requests * group_size * POS // n_seq, -1)

    chunk_rows = requests * flat_width // n_seq
    stats_row = jnp.concatenate(
        [
            by_chunk(part_max).reshape(n_seq, 1, chunk_rows),
            by_chunk(part_sum).reshape(n_seq, 1, chunk_rows),
            jnp.zeros((n_seq, 1, HEAD - 2 * chunk_rows), jnp.float32),
        ],
        axis=-1,
    )
    stats = jnp.concatenate([stats_row, jnp.zeros((n_seq, 7, HEAD), jnp.float32)], axis=1)
    acc_chunks = by_chunk(part_acc).astype(jnp.bfloat16)
    source_of, acc_chunks, stats = lax.optimization_barrier((source_of, acc_chunks, stats))
    projected = attend_exchange(acc_chunks, stats, out_weight, n_head)
    moved_cache = pick_blocks(source_of, incoming, arrivals)
    return (projected, moved_cache)


def solution(mesh):
    placed = (
        P(None, "seq"),
        P("seq", "head"),
        P("head", "seq"),
        P("seq", None, None, "head"),
        P(),
        P("seq"),
        P("seq"),
        P("seq", None, None),
        P("seq", None, None),
    )
    return jax.shard_map(
        body,
        mesh=mesh,
        in_specs=placed,
        out_specs=(P("head", "seq"), P("seq", None, None, "head")),
        check_vma=False,
    )
```

```python
import functools

import jax
import numpy as np
import jax.numpy as jnp
from jax import lax
from jax.experimental import pallas as pl
from jax.experimental.pallas import tpu as pltpu
from jax.sharding import PartitionSpec as P

HEADS = 64
KV_HEADS = 8
HEAD = 128
POS = 4
BLOCK = 128

MESH = pl.DeviceIdType.MESH

rope_base = 500000.0
neg_large = -1e30


def _barrier(peers):
    barrier = pltpu.get_barrier_semaphore()
    for device in peers:
        pl.semaphore_signal(barrier, inc=1, device_id=device, device_id_type=MESH)
    pl.semaphore_wait(barrier, len(peers))


def _send_all(axis, n, me, src_of, land, send_sem, recv_sem):
    copies = []
    for i in range(1, n):
        peer = lax.rem(me + i, n)
        copy = pltpu.make_async_remote_copy(
            src_ref=src_of(peer),
            dst_ref=land.at[me],
            send_sem=send_sem.at[peer],
            recv_sem=recv_sem.at[me],
            device_id={axis: peer},
            device_id_type=MESH,
        )
        copy.start()
        copies.append(copy)
    return copies


def _wait_all(axis, n, me, land, send_sem, recv_sem):
    for i in range(1, n):
        src = lax.rem(me + n - i, n)
        pltpu.make_async_remote_copy(
            src_ref=land.at[src],
            dst_ref=land.at[src],
            send_sem=send_sem.at[src],
            recv_sem=recv_sem.at[src],
            device_id={axis: src},
            device_id_type=MESH,
        ).wait_recv()


def _qkv_kernel(
    n, limit, x_hbm, w_hbm, freq_ref, lengths_ref, pick_hbm, kv_hbm, out_ref, sent_hbm,
    x_vmem, w_vmem, part_ref, pick_ref, land_a, mine, land_b, sems, kv_vmem, sent_vmem, local_sems,
):
    me = lax.axis_index("seq")
    loads = [
        pltpu.make_async_copy(x_hbm, x_vmem, local_sems.at[2]),
        pltpu.make_async_copy(w_hbm, w_vmem, local_sems.at[3]),
        pltpu.make_async_copy(pick_hbm, pick_ref, local_sems.at[4]),
    ]
    for load in loads:
        load.start()
    kv_in = pltpu.make_async_copy(kv_hbm, kv_vmem, local_sems.at[0])
    kv_in.start()
    barrier = pltpu.get_barrier_semaphore()
    for i in range(1, n):
        pl.semaphore_signal(
            barrier, inc=1, device_id={"seq": lax.rem(me + i, n)}, device_id_type=MESH
        )
    for load in loads:
        load.wait()
    product = jnp.dot(x_vmem[...], w_vmem[...], preferred_element_type=jnp.float32)
    groups = product.shape[1] // HEAD
    per = part_ref.shape[1] // groups
    for j in range(n):
        for k in range(per):
            row = product[per * j + k : per * j + k + 1]
            for g in range(groups):
                part_ref[j, k * groups + g : k * groups + g + 1, :] = row[:, g * HEAD : (g + 1) * HEAD]
    land_a[me] = part_ref[me]
    pl.semaphore_wait(barrier, n - 1)
    sent_a = _send_all("seq", n, me, lambda p: part_ref.at[p], land_a, sems.at[0], sems.at[1])
    kv_in.wait()

    def pick(j, carry):
        per = pick_ref.shape[1]
        sent_vmem[j] = kv_vmem[jnp.minimum(pick_ref[0, j % per, j // per], limit - 1)]
        return carry

    lax.fori_loop(0, sent_vmem.shape[0], pick, 0)
    kv_out = pltpu.make_async_copy(sent_vmem, sent_hbm, local_sems.at[1])
    kv_out.start()
    _wait_all("seq", n, me, land_a, sems.at[0], sems.at[1])
    total = land_a[0]
    for i in range(1, n):
        total = total + land_a[i]
    g = total.shape[0] // 2
    first_row = 2 * me
    second_row = first_row + 1
    pos_a = (lengths_ref[first_row // POS] + first_row % POS).astype(jnp.float32)
    pos_b = (lengths_ref[second_row // POS] + second_row % POS).astype(jnp.float32)
    row = lax.broadcasted_iota(jnp.int32, total.shape, 0)
    lane = lax.broadcasted_iota(jnp.int32, total.shape, 1)
    angle = jnp.where(row < g, pos_a, pos_b) * freq_ref[...]
    value_row = (row == g - 1) | (row == 2 * g - 1)
    cosine = jnp.where(value_row, 1.0, jnp.cos(angle))
    sine = jnp.where(value_row, 0.0, jnp.where(lane < HEAD // 2, -jnp.sin(angle), jnp.sin(angle)))
    turned = pltpu.roll(total, HEAD // 2, 1)
    rotated = (total * cosine + turned * sine).astype(mine.dtype)
    mine[...] = rotated
    land_b[me] = rotated
    sent_b = _send_all("seq", n, me, lambda p: mine, land_b, sems.at[2], sems.at[3])
    _wait_all("seq", n, me, land_b, sems.at[2], sems.at[3])
    for copy in sent_a + sent_b:
        copy.wait_send()
    out_ref[...] = land_b[...]
    kv_out.wait()


def qkv_exchange(normed, qkv_weight, freq, lengths, pick, kv_cache, n):
    rows = normed.shape[0]
    groups = qkv_weight.shape[1] // HEAD
    chunk = (n, rows // n * groups, HEAD)
    picked = (pick.size,) + kv_cache.shape[1:]
    return pl.pallas_call(
        functools.partial(_qkv_kernel, n, kv_cache.shape[0]),
        out_shape=(
            jax.ShapeDtypeStruct(chunk, jnp.bfloat16),
            jax.ShapeDtypeStruct(picked, kv_cache.dtype),
        ),
        in_specs=[pl.BlockSpec(memory_space=pl.ANY)] * 2
        + [pl.BlockSpec(memory_space=pltpu.VMEM), pl.BlockSpec(memory_space=pltpu.SMEM)]
        + [pl.BlockSpec(memory_space=pl.ANY)] * 2,
        out_specs=(pl.BlockSpec(memory_space=pltpu.VMEM), pl.BlockSpec(memory_space=pl.ANY)),
        scratch_shapes=[
            pltpu.VMEM(normed.shape, normed.dtype),
            pltpu.VMEM(qkv_weight.shape, qkv_weight.dtype),
            pltpu.VMEM(chunk, jnp.float32),
            pltpu.SMEM(pick.shape, pick.dtype),
            pltpu.VMEM(chunk, jnp.float32),
            pltpu.VMEM(chunk[1:], jnp.bfloat16),
            pltpu.VMEM(chunk, jnp.bfloat16),
            pltpu.SemaphoreType.DMA((4, n)),
            pltpu.VMEM(kv_cache.shape, kv_cache.dtype),
            pltpu.VMEM(picked, kv_cache.dtype),
            pltpu.SemaphoreType.DMA((5,)),
        ],
        compiler_params=pltpu.CompilerParams(collective_id=0, has_side_effects=True),
        cost_estimate=pl.CostEstimate(
            flops=2 * rows * normed.shape[1] * qkv_weight.shape[1],
            bytes_accessed=qkv_weight.size * 2 + 2 * kv_cache.size * kv_cache.dtype.itemsize,
            transcendentals=0,
        ),
    )(normed, qkv_weight, freq, lengths, pick, kv_cache)


def _attend_kernel(
    n, m, rows, acc_ref, stats_ref, w_ref, out_ref, land_p, land_s, mine, land_a, part_c, land_c,
    sems,
):
    me = lax.axis_index("seq")
    me_h = lax.axis_index("head")
    land_p[me] = acc_ref[me]
    land_s[me] = stats_ref[me]
    _barrier(
        [{"seq": lax.rem(me + i, n)} for i in range(1, n)]
        + [{"head": lax.rem(me_h + i, m)} for i in range(1, m)]
    )
    sent_p = _send_all("seq", n, me, lambda p: acc_ref.at[p], land_p, sems.at[0], sems.at[1])
    sent_s = _send_all("seq", n, me, lambda p: stats_ref.at[p], land_s, sems.at[6], sems.at[7])
    _wait_all("seq", n, me, land_s, sems.at[6], sems.at[7])
    _wait_all("seq", n, me, land_p, sems.at[0], sems.at[1])
    columns = [land_s[i].T for i in range(n)]
    top = columns[0][:rows, 0:1]
    for i in range(1, n):
        top = jnp.maximum(top, columns[i][:rows, 0:1])
    numerator = jnp.zeros((rows, HEAD), jnp.float32)
    denominator = jnp.zeros((rows, 1), jnp.float32)
    for i in range(n):
        scale = jnp.exp(columns[i][:rows, 0:1] - top)
        denominator = denominator + columns[i][rows : 2 * rows, 0:1] * scale
        numerator = numerator + land_p[i].astype(jnp.float32) * scale
    attended = (numerator / denominator).astype(mine.dtype)
    mine[...] = attended
    land_a[me] = attended
    sent_a = _send_all("seq", n, me, lambda p: mine, land_a, sems.at[2], sems.at[3])
    _wait_all("seq", n, me, land_a, sems.at[2], sems.at[3])
    heads = n // 2
    projected = None
    for g in range(heads):
        lhs = land_a[2 * g : 2 * g + 2].reshape(2 * rows, HEAD)
        term = jnp.dot(lhs, w_ref[g * HEAD : (g + 1) * HEAD, :], preferred_element_type=jnp.float32)
        projected = term if projected is None else projected + term
    per = projected.shape[0] // m
    pieces = projected.shape[1] // HEAD
    for j in range(m):
        for q in range(pieces):
            part_c[j, q * per : (q + 1) * per, :] = projected[j * per : (j + 1) * per, q * HEAD : (q + 1) * HEAD]
    land_c[me_h] = part_c[me_h]
    sent_c = _send_all("head", m, me_h, lambda p: part_c.at[p], land_c, sems.at[4], sems.at[5])
    _wait_all("head", m, me_h, land_c, sems.at[4], sems.at[5])
    total = land_c[0]
    for j in range(1, m):
        total = total + land_c[j]
    for copy in sent_p + sent_s + sent_a + sent_c:
        copy.wait_send()
    for q in range(pieces):
        out_ref[:, q * HEAD : (q + 1) * HEAD] = total[q * per : (q + 1) * per].astype(out_ref.dtype)


def attend_exchange(acc, stats, out_weight, m):
    n, rows, _ = acc.shape
    width = out_weight.shape[1]
    per = 2 * rows // m
    return pl.pallas_call(
        functools.partial(_attend_kernel, n, m, rows),
        out_shape=jax.ShapeDtypeStruct((per, width), jnp.bfloat16),
        in_specs=[pl.BlockSpec(memory_space=pltpu.VMEM)] * 3,
        out_specs=pl.BlockSpec(memory_space=pltpu.VMEM),
        scratch_shapes=[
            pltpu.VMEM(acc.shape, acc.dtype),
            pltpu.VMEM(stats.shape, jnp.float32),
            pltpu.VMEM((rows, HEAD), jnp.bfloat16),
            pltpu.VMEM((n, rows, HEAD), jnp.bfloat16),
            pltpu.VMEM((m, per * width // HEAD, HEAD), jnp.float32),
            pltpu.VMEM((m, per * width // HEAD, HEAD), jnp.float32),
            pltpu.SemaphoreType.DMA((8, max(n, m))),
        ],
        compiler_params=pltpu.CompilerParams(collective_id=1, has_side_effects=True),
        cost_estimate=pl.CostEstimate(
            flops=2 * 2 * rows * out_weight.shape[0] * width,
            bytes_accessed=acc.size * 4 + stats.size * 8 + out_weight.size * 2,
            transcendentals=n * rows * HEAD,
        ),
    )(acc, stats, out_weight)


def _pick_kernel(limit, index_ref, src_hbm, out_hbm, buf, sems, out_sem):
    count = buf.shape[0]

    def start(j, carry):
        k = index_ref[j]

        @pl.when(k < limit)
        def _():
            pltpu.make_async_copy(src_hbm.at[jnp.minimum(k, limit - 1)], buf.at[j], sems.at[j]).start()

        @pl.when(k >= limit)
        def _():
            buf[j] = jnp.zeros(buf.shape[1:], buf.dtype)

        return carry

    def send(j, carry):
        k = index_ref[j]

        @pl.when(k < limit)
        def _():
            pltpu.make_async_copy(src_hbm.at[0], buf.at[j], sems.at[j]).wait()

        pltpu.make_async_copy(buf.at[j], out_hbm.at[j], out_sem.at[j]).start()
        return carry

    def finish(j, carry):
        pltpu.make_async_copy(buf.at[j], out_hbm.at[j], out_sem.at[j]).wait()
        return carry

    lax.fori_loop(0, count, start, 0)
    lax.fori_loop(0, count, send, 0)
    lax.fori_loop(0, count, finish, 0)


def pick_blocks(index, source, limit):
    count = index.shape[0]
    shape = (count,) + source.shape[1:]
    nbytes = count * source[0].size * source.dtype.itemsize
    return pl.pallas_call(
        functools.partial(_pick_kernel, limit),
        out_shape=jax.ShapeDtypeStruct(shape, source.dtype),
        in_specs=[
            pl.BlockSpec(memory_space=pltpu.SMEM),
            pl.BlockSpec(memory_space=pl.ANY),
        ],
        out_specs=pl.BlockSpec(memory_space=pl.ANY),
        scratch_shapes=[
            pltpu.VMEM(shape, source.dtype),
            pltpu.SemaphoreType.DMA((count,)),
            pltpu.SemaphoreType.DMA((count,)),
        ],
        cost_estimate=pl.CostEstimate(flops=0, bytes_accessed=2 * nbytes, transcendentals=0),
    )(index, source)


def rotate(values, positions):
    half_width = values.shape[-1] // 2
    frequencies = rope_base ** (
        -(jnp.arange(half_width, dtype=jnp.float32) * 2.0 / values.shape[-1])
    )
    angles = positions[..., None] * frequencies
    cosine_table = jnp.cos(angles)
    sine_table = jnp.sin(angles)
    lower_half = values[..., :half_width]
    upper_half = values[..., half_width:]
    return jnp.concatenate(
        [
            lower_half * cosine_table - upper_half * sine_table,
            upper_half * cosine_table + lower_half * sine_table,
        ],
        axis=-1,
    )


def body(
    normed,
    qkv_weight,
    out_weight,
    kv_cache,
    lengths,
    slot_request,
    slot_block,
    send_list,
    recv_list,
):
    group_size = HEADS // KV_HEADS
    scale_factor = HEAD ** (-0.5)
    requests = lengths.shape[0]
    slot_count = kv_cache.shape[0]
    n_seq = lax.axis_size("seq")
    n_head = lax.axis_size("head")
    me_seq = lax.axis_index("seq")
    rows = normed.shape[0]
    rows_per = rows // n_seq
    groups = qkv_weight.shape[1] // HEAD

    half_width = HEAD // 2
    frequencies = np.float32(rope_base) ** (
        -(np.arange(half_width, dtype=np.float32) * np.float32(2.0) / np.float32(HEAD))
    )
    freq_row = jnp.asarray(np.concatenate([frequencies, frequencies])[None, :].astype(np.float32))
    qkv, outgoing = qkv_exchange(
        normed, qkv_weight, freq_row, lengths, send_list.transpose(0, 2, 1), kv_cache, n_seq
    )
    qkv = qkv.reshape(requests, POS, 1, groups, HEAD)
    local_kv = 1

    outgoing = outgoing.reshape((lax.axis_size("seq"), -1) + kv_cache.shape[1:])
    incoming = lax.all_to_all(outgoing, "seq", split_axis=0, concat_axis=0, tiled=True)
    incoming = incoming.reshape((-1,) + kv_cache.shape[1:])
    arrivals = incoming.shape[0]
    source_of = (
        jnp.full((slot_count + 1,), arrivals, jnp.int32)
        .at[recv_list.reshape(-1)]
        .set(jnp.arange(arrivals, dtype=jnp.int32), mode="drop")[:slot_count]
    )
    queries = qkv[:, :, :, :group_size]
    keys_new = qkv[:, :, :, group_size]
    values_new = qkv[:, :, :, group_size + 1]

    slot_clip = jnp.minimum(slot_request, requests - 1)
    live_slot = slot_request < requests
    token_pos = slot_block[:, None] * BLOCK + jnp.arange(BLOCK, dtype=jnp.int32)[None, :]
    token_valid = (token_pos < lengths[slot_clip][:, None]) & live_slot[:, None]
    cache_view = kv_cache.reshape(slot_count, 2, BLOCK, local_kv, HEAD)
    gathered = queries[slot_clip]
    scores = (
        jnp.einsum(
            "sptgd,sbtd->stgpb", gathered, cache_view[:, 0], preferred_element_type=jnp.float32
        )
        * scale_factor
    )
    scores = jnp.where(token_valid[:, None, None, None, :], scores, neg_large)
    slot_max = jnp.max(scores, axis=-1)
    weights = jnp.where(
        token_valid[:, None, None, None, :], jnp.exp(scores - slot_max[..., None]), 0.0
    )
    slot_sum = jnp.sum(weights, axis=-1)
    slot_acc = jnp.einsum(
        "stgpb,sbtd->stgpd",
        weights.astype(jnp.bfloat16),
        cache_view[:, 1],
        preferred_element_type=jnp.float32,
    )
    flat_width = local_kv * group_size * POS
    slot_max_flat = slot_max.reshape(slot_count, flat_width)
    member = slot_request[:, None] == jnp.arange(requests, dtype=jnp.int32)[None, :]
    request_max = jnp.max(
        jnp.where(member[:, None, :], slot_max_flat[:, :, None], neg_large), axis=0
    ).T
    rescale = jnp.exp(slot_max_flat - request_max[slot_clip])
    member_float = member.astype(jnp.float32).T
    request_sum = jnp.dot(
        member_float,
        slot_sum.reshape(slot_count, flat_width) * rescale,
        precision=lax.Precision.HIGHEST,
    )
    scaled_acc = (slot_acc.reshape(slot_count, flat_width, HEAD) * rescale[:, :, None]).reshape(
        slot_count, flat_width * HEAD
    )
    request_acc = jnp.dot(member_float, scaled_acc, precision=lax.Precision.HIGHEST).reshape(
        requests, flat_width, HEAD
    )

    new_scores = (
        jnp.einsum("rptgd,rqtd->rtgpq", queries, keys_new, preferred_element_type=jnp.float32)
        * scale_factor
    )
    causal = jnp.arange(POS)[:, None] >= jnp.arange(POS)[None, :]
    new_scores = jnp.where(causal, new_scores, neg_large)
    new_max = jnp.max(new_scores, axis=-1)
    new_weights = jnp.where(causal, jnp.exp(new_scores - new_max[..., None]), 0.0)
    new_sum = jnp.sum(new_weights, axis=-1).reshape(requests, flat_width)
    new_acc = jnp.einsum(
        "rtgpq,rqtd->rtgpd",
        new_weights.astype(jnp.bfloat16),
        values_new,
        preferred_element_type=jnp.float32,
    ).reshape(requests, flat_width, HEAD)
    first = me_seq == 0
    new_max = jnp.where(first, new_max.reshape(requests, flat_width), neg_large)
    new_sum = jnp.where(first, new_sum, 0.0)
    new_acc = jnp.where(first, new_acc, 0.0)
    part_max = jnp.maximum(request_max, new_max)
    keep_old = jnp.exp(request_max - part_max)
    keep_new = jnp.exp(new_max - part_max)
    part_sum = request_sum * keep_old + new_sum * keep_new
    part_acc = request_acc * keep_old[..., None] + new_acc * keep_new[..., None]

    def by_chunk(values):
        lead = values.reshape(2, requests // 2, group_size, POS, -1).transpose(2, 0, 1, 3, 4)
        return lead.reshape(n_seq, requests * group_size * POS // n_seq, -1)

    chunk_rows = requests * flat_width // n_seq
    stats_row = jnp.concatenate(
        [
            by_chunk(part_max).reshape(n_seq, 1, chunk_rows),
            by_chunk(part_sum).reshape(n_seq, 1, chunk_rows),
            jnp.zeros((n_seq, 1, HEAD - 2 * chunk_rows), jnp.float32),
        ],
        axis=-1,
    )
    stats = jnp.concatenate([stats_row, jnp.zeros((n_seq, 7, HEAD), jnp.float32)], axis=1)
    acc_chunks = by_chunk(part_acc).astype(jnp.bfloat16)
    source_of, acc_chunks, stats = lax.optimization_barrier((source_of, acc_chunks, stats))
    projected = attend_exchange(acc_chunks, stats, out_weight, n_head)
    moved_cache = pick_blocks(source_of, incoming, arrivals)
    return (projected, moved_cache)


def solution(mesh):
    placed = (
        P(None, "seq"),
        P("seq", "head"),
        P("head", "seq"),
        P("seq", None, None, "head"),
        P(),
        P("seq"),
        P("seq"),
        P("seq", None, None),
        P("seq", None, None),
    )
    return jax.shard_map(
        body,
        mesh=mesh,
        in_specs=placed,
        out_specs=(P("head", "seq"), P("seq", None, None, "head")),
        check_vma=False,
    )
```

```python
import functools

import jax
import numpy as np
import jax.numpy as jnp
from jax import lax
from jax.experimental import pallas as pl
from jax.experimental.pallas import tpu as pltpu
from jax.sharding import PartitionSpec as P

HEADS = 64
KV_HEADS = 8
HEAD = 128
POS = 4
BLOCK = 128

MESH = pl.DeviceIdType.MESH

rope_base = 500000.0
neg_large = -1e30


def _barrier(peers):
    barrier = pltpu.get_barrier_semaphore()
    for device in peers:
        pl.semaphore_signal(barrier, inc=1, device_id=device, device_id_type=MESH)
    pl.semaphore_wait(barrier, len(peers))


def _send_all(axis, n, me, src_of, land, send_sem, recv_sem):
    copies = []
    for i in range(1, n):
        peer = lax.rem(me + i, n)
        copy = pltpu.make_async_remote_copy(
            src_ref=src_of(peer),
            dst_ref=land.at[me],
            send_sem=send_sem.at[peer],
            recv_sem=recv_sem.at[me],
            device_id={axis: peer},
            device_id_type=MESH,
        )
        copy.start()
        copies.append(copy)
    return copies


def _wait_all(axis, n, me, land, send_sem, recv_sem):
    for i in range(1, n):
        src = lax.rem(me + n - i, n)
        pltpu.make_async_remote_copy(
            src_ref=land.at[src],
            dst_ref=land.at[src],
            send_sem=send_sem.at[src],
            recv_sem=recv_sem.at[src],
            device_id={axis: src},
            device_id_type=MESH,
        ).wait_recv()


def _qkv_kernel(
    n, limit, x_hbm, w_hbm, freq_ref, lengths_ref, pick_hbm, kv_hbm, out_ref, sent_hbm,
    x_vmem, w_vmem, part_ref, pick_ref, land_a, mine, land_b, sems, kv_vmem, sent_vmem, local_sems,
):
    me = lax.axis_index("seq")
    loads = [
        pltpu.make_async_copy(x_hbm, x_vmem, local_sems.at[2]),
        pltpu.make_async_copy(w_hbm, w_vmem, local_sems.at[3]),
        pltpu.make_async_copy(pick_hbm, pick_ref, local_sems.at[4]),
    ]
    for load in loads:
        load.start()
    kv_in = pltpu.make_async_copy(kv_hbm, kv_vmem, local_sems.at[0])
    kv_in.start()
    barrier = pltpu.get_barrier_semaphore()
    for i in range(1, n):
        pl.semaphore_signal(
            barrier, inc=1, device_id={"seq": lax.rem(me + i, n)}, device_id_type=MESH
        )
    for load in loads:
        load.wait()
    product = jnp.dot(x_vmem[...], w_vmem[...], preferred_element_type=jnp.float32)
    groups = product.shape[1] // HEAD
    per = part_ref.shape[1] // groups
    for j in range(n):
        for k in range(per):
            row = product[per * j + k : per * j + k + 1]
            for g in range(groups):
                part_ref[j, k * groups + g : k * groups + g + 1, :] = row[:, g * HEAD : (g + 1) * HEAD]
    land_a[me] = part_ref[me]
    pl.semaphore_wait(barrier, n - 1)
    sent_a = _send_all("seq", n, me, lambda p: part_ref.at[p], land_a, sems.at[0], sems.at[1])
    kv_in.wait()

    def pick(j, carry):
        per = pick_ref.shape[1]
        sent_vmem[j] = kv_vmem[jnp.minimum(pick_ref[0, j % per, j // per], limit - 1)]
        return carry

    lax.fori_loop(0, sent_vmem.shape[0], pick, 0)
    kv_out = pltpu.make_async_copy(sent_vmem, sent_hbm, local_sems.at[1])
    kv_out.start()
    _wait_all("seq", n, me, land_a, sems.at[0], sems.at[1])
    total = land_a[0]
    for i in range(1, n):
        total = total + land_a[i]
    g = total.shape[0] // 2
    first_row = 2 * me
    second_row = first_row + 1
    pos_a = (lengths_ref[first_row // POS] + first_row % POS).astype(jnp.float32)
    pos_b = (lengths_ref[second_row // POS] + second_row % POS).astype(jnp.float32)
    row = lax.broadcasted_iota(jnp.int32, total.shape, 0)
    lane = lax.broadcasted_iota(jnp.int32, total.shape, 1)
    angle = jnp.where(row < g, pos_a, pos_b) * freq_ref[...]
    value_row = (row == g - 1) | (row == 2 * g - 1)
    cosine = jnp.where(value_row, 1.0, jnp.cos(angle))
    sine = jnp.where(value_row, 0.0, jnp.where(lane < HEAD // 2, -jnp.sin(angle), jnp.sin(angle)))
    turned = pltpu.roll(total, HEAD // 2, 1)
    rotated = (total * cosine + turned * sine).astype(mine.dtype)
    mine[...] = rotated
    land_b[me] = rotated
    sent_b = _send_all("seq", n, me, lambda p: mine, land_b, sems.at[2], sems.at[3])
    _wait_all("seq", n, me, land_b, sems.at[2], sems.at[3])
    for copy in sent_a + sent_b:
        copy.wait_send()
    out_ref[...] = land_b[...]
    kv_out.wait()


def qkv_exchange(normed, qkv_weight, freq, lengths, pick, kv_cache, n):
    rows = normed.shape[0]
    groups = qkv_weight.shape[1] // HEAD
    chunk = (n, rows // n * groups, HEAD)
    picked = (pick.size,) + kv_cache.shape[1:]
    return pl.pallas_call(
        functools.partial(_qkv_kernel, n, kv_cache.shape[0]),
        out_shape=(
            jax.ShapeDtypeStruct(chunk, jnp.bfloat16),
            jax.ShapeDtypeStruct(picked, kv_cache.dtype),
        ),
        in_specs=[pl.BlockSpec(memory_space=pl.ANY)] * 2
        + [pl.BlockSpec(memory_space=pltpu.VMEM), pl.BlockSpec(memory_space=pltpu.SMEM)]
        + [pl.BlockSpec(memory_space=pl.ANY)] * 2,
        out_specs=(pl.BlockSpec(memory_space=pltpu.VMEM), pl.BlockSpec(memory_space=pl.ANY)),
        scratch_shapes=[
            pltpu.VMEM(normed.shape, normed.dtype),
            pltpu.VMEM(qkv_weight.shape, qkv_weight.dtype),
            pltpu.VMEM(chunk, jnp.float32),
            pltpu.SMEM(pick.shape, pick.dtype),
            pltpu.VMEM(chunk, jnp.float32),
            pltpu.VMEM(chunk[1:], jnp.bfloat16),
            pltpu.VMEM(chunk, jnp.bfloat16),
            pltpu.SemaphoreType.DMA((4, n)),
            pltpu.VMEM(kv_cache.shape, kv_cache.dtype),
            pltpu.VMEM(picked, kv_cache.dtype),
            pltpu.SemaphoreType.DMA((5,)),
        ],
        compiler_params=pltpu.CompilerParams(collective_id=0, has_side_effects=True),
        cost_estimate=pl.CostEstimate(
            flops=2 * rows * normed.shape[1] * qkv_weight.shape[1],
            bytes_accessed=qkv_weight.size * 2 + 2 * kv_cache.size * kv_cache.dtype.itemsize,
            transcendentals=0,
        ),
    )(normed, qkv_weight, freq, lengths, pick, kv_cache)


def _attend_kernel(
    n, m, rows, limit, acc_ref, stats_ref, w_ref, place_ref, got_hbm, out_ref, moved_hbm,
    land_p, land_s, mine, land_a, part_c, land_c, sems, got_vmem, moved_vmem, local_sems,
):
    me = lax.axis_index("seq")
    me_h = lax.axis_index("head")
    got_in = pltpu.make_async_copy(got_hbm, got_vmem, local_sems.at[0])
    got_in.start()
    land_p[me] = acc_ref[me]
    land_s[me] = stats_ref[me]
    _barrier(
        [{"seq": lax.rem(me + i, n)} for i in range(1, n)]
        + [{"head": lax.rem(me_h + i, m)} for i in range(1, m)]
    )
    sent_p = _send_all("seq", n, me, lambda p: acc_ref.at[p], land_p, sems.at[0], sems.at[1])
    sent_s = _send_all("seq", n, me, lambda p: stats_ref.at[p], land_s, sems.at[6], sems.at[7])
    got_in.wait()

    def place(k, carry):
        src = place_ref[k]
        block = got_vmem[jnp.minimum(src, limit - 1)]
        moved_vmem[k] = jnp.where(src < limit, block, jnp.zeros_like(block))
        return carry

    lax.fori_loop(0, moved_vmem.shape[0], place, 0)
    moved_out = pltpu.make_async_copy(moved_vmem, moved_hbm, local_sems.at[1])
    moved_out.start()
    _wait_all("seq", n, me, land_s, sems.at[6], sems.at[7])
    _wait_all("seq", n, me, land_p, sems.at[0], sems.at[1])
    columns = [land_s[i].T for i in range(n)]
    top = columns[0][:rows, 0:1]
    for i in range(1, n):
        top = jnp.maximum(top, columns[i][:rows, 0:1])
    numerator = jnp.zeros((rows, HEAD), jnp.float32)
    denominator = jnp.zeros((rows, 1), jnp.float32)
    for i in range(n):
        scale = jnp.exp(columns[i][:rows, 0:1] - top)
        denominator = denominator + columns[i][rows : 2 * rows, 0:1] * scale
        numerator = numerator + land_p[i].astype(jnp.float32) * scale
    attended = (numerator / denominator).astype(mine.dtype)
    mine[...] = attended
    land_a[me] = attended
    sent_a = _send_all("seq", n, me, lambda p: mine, land_a, sems.at[2], sems.at[3])
    _wait_all("seq", n, me, land_a, sems.at[2], sems.at[3])
    heads = n // 2
    projected = None
    for g in range(heads):
        lhs = land_a[2 * g : 2 * g + 2].reshape(2 * rows, HEAD)
        term = jnp.dot(lhs, w_ref[g * HEAD : (g + 1) * HEAD, :], preferred_element_type=jnp.float32)
        projected = term if projected is None else projected + term
    per = part_c.shape[1]
    for j in range(m):
        part_c[j] = projected[j * per : (j + 1) * per]
    land_c[me_h] = part_c[me_h]
    sent_c = _send_all("head", m, me_h, lambda p: part_c.at[p], land_c, sems.at[4], sems.at[5])
    _wait_all("head", m, me_h, land_c, sems.at[4], sems.at[5])
    total = land_c[0]
    for j in range(1, m):
        total = total + land_c[j]
    for copy in sent_p + sent_s + sent_a + sent_c:
        copy.wait_send()
    out_ref[...] = total.astype(out_ref.dtype)
    moved_out.wait()


def attend_exchange(acc, stats, out_weight, m, place, got):
    n, rows, _ = acc.shape
    width = out_weight.shape[1]
    per = 2 * rows // m
    moved = (place.shape[0],) + got.shape[1:]
    return pl.pallas_call(
        functools.partial(_attend_kernel, n, m, rows, got.shape[0]),
        out_shape=(
            jax.ShapeDtypeStruct((per, width), jnp.bfloat16),
            jax.ShapeDtypeStruct(moved, got.dtype),
        ),
        in_specs=[pl.BlockSpec(memory_space=pltpu.VMEM)] * 3
        + [pl.BlockSpec(memory_space=pltpu.SMEM), pl.BlockSpec(memory_space=pl.ANY)],
        out_specs=(pl.BlockSpec(memory_space=pltpu.VMEM), pl.BlockSpec(memory_space=pl.ANY)),
        scratch_shapes=[
            pltpu.VMEM(acc.shape, acc.dtype),
            pltpu.VMEM(stats.shape, jnp.float32),
            pltpu.VMEM((rows, HEAD), jnp.bfloat16),
            pltpu.VMEM((n, rows, HEAD), jnp.bfloat16),
            pltpu.VMEM((m, per, width), jnp.float32),
            pltpu.VMEM((m, per, width), jnp.float32),
            pltpu.SemaphoreType.DMA((8, max(n, m))),
            pltpu.VMEM(got.shape, got.dtype),
            pltpu.VMEM(moved, got.dtype),
            pltpu.SemaphoreType.DMA((2,)),
        ],
        compiler_params=pltpu.CompilerParams(collective_id=1, has_side_effects=True),
        cost_estimate=pl.CostEstimate(
            flops=2 * 2 * rows * out_weight.shape[0] * width,
            bytes_accessed=acc.size * 4 + stats.size * 8 + out_weight.size * 2 + 2 * got.size * 2,
            transcendentals=n * rows * HEAD,
        ),
    )(acc, stats, out_weight, place, got)


def _pick_kernel(limit, index_ref, src_hbm, out_hbm, buf, sems, out_sem):
    count = buf.shape[0]

    def start(j, carry):
        k = index_ref[j]

        @pl.when(k < limit)
        def _():
            pltpu.make_async_copy(src_hbm.at[jnp.minimum(k, limit - 1)], buf.at[j], sems.at[j]).start()

        @pl.when(k >= limit)
        def _():
            buf[j] = jnp.zeros(buf.shape[1:], buf.dtype)

        return carry

    def send(j, carry):
        k = index_ref[j]

        @pl.when(k < limit)
        def _():
            pltpu.make_async_copy(src_hbm.at[0], buf.at[j], sems.at[j]).wait()

        pltpu.make_async_copy(buf.at[j], out_hbm.at[j], out_sem.at[j]).start()
        return carry

    def finish(j, carry):
        pltpu.make_async_copy(buf.at[j], out_hbm.at[j], out_sem.at[j]).wait()
        return carry

    lax.fori_loop(0, count, start, 0)
    lax.fori_loop(0, count, send, 0)
    lax.fori_loop(0, count, finish, 0)


def pick_blocks(index, source, limit):
    count = index.shape[0]
    shape = (count,) + source.shape[1:]
    nbytes = count * source[0].size * source.dtype.itemsize
    return pl.pallas_call(
        functools.partial(_pick_kernel, limit),
        out_shape=jax.ShapeDtypeStruct(shape, source.dtype),
        in_specs=[
            pl.BlockSpec(memory_space=pltpu.SMEM),
            pl.BlockSpec(memory_space=pl.ANY),
        ],
        out_specs=pl.BlockSpec(memory_space=pl.ANY),
        scratch_shapes=[
            pltpu.VMEM(shape, source.dtype),
            pltpu.SemaphoreType.DMA((count,)),
            pltpu.SemaphoreType.DMA((count,)),
        ],
        cost_estimate=pl.CostEstimate(flops=0, bytes_accessed=2 * nbytes, transcendentals=0),
    )(index, source)


def rotate(values, positions):
    half_width = values.shape[-1] // 2
    frequencies = rope_base ** (
        -(jnp.arange(half_width, dtype=jnp.float32) * 2.0 / values.shape[-1])
    )
    angles = positions[..., None] * frequencies
    cosine_table = jnp.cos(angles)
    sine_table = jnp.sin(angles)
    lower_half = values[..., :half_width]
    upper_half = values[..., half_width:]
    return jnp.concatenate(
        [
            lower_half * cosine_table - upper_half * sine_table,
            upper_half * cosine_table + lower_half * sine_table,
        ],
        axis=-1,
    )


def body(
    normed,
    qkv_weight,
    out_weight,
    kv_cache,
    lengths,
    slot_request,
    slot_block,
    send_list,
    recv_list,
):
    group_size = HEADS // KV_HEADS
    scale_factor = HEAD ** (-0.5)
    requests = lengths.shape[0]
    slot_count = kv_cache.shape[0]
    n_seq = lax.axis_size("seq")
    n_head = lax.axis_size("head")
    me_seq = lax.axis_index("seq")
    rows = normed.shape[0]
    rows_per = rows // n_seq
    groups = qkv_weight.shape[1] // HEAD

    half_width = HEAD // 2
    frequencies = np.float32(rope_base) ** (
        -(np.arange(half_width, dtype=np.float32) * np.float32(2.0) / np.float32(HEAD))
    )
    freq_row = jnp.asarray(np.concatenate([frequencies, frequencies])[None, :].astype(np.float32))
    qkv, outgoing = qkv_exchange(
        normed, qkv_weight, freq_row, lengths, send_list.transpose(0, 2, 1), kv_cache, n_seq
    )
    qkv = qkv.reshape(requests, POS, 1, groups, HEAD)
    local_kv = 1

    outgoing = outgoing.reshape((lax.axis_size("seq"), -1) + kv_cache.shape[1:])
    incoming = lax.all_to_all(outgoing, "seq", split_axis=0, concat_axis=0, tiled=True)
    incoming = incoming.reshape((-1,) + kv_cache.shape[1:])
    arrivals = incoming.shape[0]
    source_of = (
        jnp.full((slot_count + 1,), arrivals, jnp.int32)
        .at[recv_list.reshape(-1)]
        .set(jnp.arange(arrivals, dtype=jnp.int32), mode="drop")[:slot_count]
    )
    queries = qkv[:, :, :, :group_size]
    keys_new = qkv[:, :, :, group_size]
    values_new = qkv[:, :, :, group_size + 1]

    slot_clip = jnp.minimum(slot_request, requests - 1)
    live_slot = slot_request < requests
    token_pos = slot_block[:, None] * BLOCK + jnp.arange(BLOCK, dtype=jnp.int32)[None, :]
    token_valid = (token_pos < lengths[slot_clip][:, None]) & live_slot[:, None]
    cache_view = kv_cache.reshape(slot_count, 2, BLOCK, local_kv, HEAD)
    gathered = queries[slot_clip]
    scores = (
        jnp.einsum(
            "sptgd,sbtd->stgpb", gathered, cache_view[:, 0], preferred_element_type=jnp.float32
        )
        * scale_factor
    )
    scores = jnp.where(token_valid[:, None, None, None, :], scores, neg_large)
    slot_max = jnp.max(scores, axis=-1)
    weights = jnp.where(
        token_valid[:, None, None, None, :], jnp.exp(scores - slot_max[..., None]), 0.0
    )
    slot_sum = jnp.sum(weights, axis=-1)
    slot_acc = jnp.einsum(
        "stgpb,sbtd->stgpd",
        weights.astype(jnp.bfloat16),
        cache_view[:, 1],
        preferred_element_type=jnp.float32,
    )
    flat_width = local_kv * group_size * POS
    slot_max_flat = slot_max.reshape(slot_count, flat_width)
    member = slot_request[:, None] == jnp.arange(requests, dtype=jnp.int32)[None, :]
    request_max = jnp.max(
        jnp.where(member[:, None, :], slot_max_flat[:, :, None], neg_large), axis=0
    ).T
    rescale = jnp.exp(slot_max_flat - request_max[slot_clip])
    member_float = member.astype(jnp.float32).T
    request_sum = jnp.dot(
        member_float,
        slot_sum.reshape(slot_count, flat_width) * rescale,
        precision=lax.Precision.HIGHEST,
    )
    scaled_acc = (slot_acc.reshape(slot_count, flat_width, HEAD) * rescale[:, :, None]).reshape(
        slot_count, flat_width * HEAD
    )
    request_acc = jnp.dot(member_float, scaled_acc, precision=lax.Precision.HIGHEST).reshape(
        requests, flat_width, HEAD
    )

    new_scores = (
        jnp.einsum("rptgd,rqtd->rtgpq", queries, keys_new, preferred_element_type=jnp.float32)
        * scale_factor
    )
    causal = jnp.arange(POS)[:, None] >= jnp.arange(POS)[None, :]
    new_scores = jnp.where(causal, new_scores, neg_large)
    new_max = jnp.max(new_scores, axis=-1)
    new_weights = jnp.where(causal, jnp.exp(new_scores - new_max[..., None]), 0.0)
    new_sum = jnp.sum(new_weights, axis=-1).reshape(requests, flat_width)
    new_acc = jnp.einsum(
        "rtgpq,rqtd->rtgpd",
        new_weights.astype(jnp.bfloat16),
        values_new,
        preferred_element_type=jnp.float32,
    ).reshape(requests, flat_width, HEAD)
    first = me_seq == 0
    new_max = jnp.where(first, new_max.reshape(requests, flat_width), neg_large)
    new_sum = jnp.where(first, new_sum, 0.0)
    new_acc = jnp.where(first, new_acc, 0.0)
    part_max = jnp.maximum(request_max, new_max)
    keep_old = jnp.exp(request_max - part_max)
    keep_new = jnp.exp(new_max - part_max)
    part_sum = request_sum * keep_old + new_sum * keep_new
    part_acc = request_acc * keep_old[..., None] + new_acc * keep_new[..., None]

    def by_chunk(values):
        lead = values.reshape(2, requests // 2, group_size, POS, -1).transpose(2, 0, 1, 3, 4)
        return lead.reshape(n_seq, requests * group_size * POS // n_seq, -1)

    chunk_rows = requests * flat_width // n_seq
    stats_row = jnp.concatenate(
        [
            by_chunk(part_max).reshape(n_seq, 1, chunk_rows),
            by_chunk(part_sum).reshape(n_seq, 1, chunk_rows),
            jnp.zeros((n_seq, 1, HEAD - 2 * chunk_rows), jnp.float32),
        ],
        axis=-1,
    )
    stats = jnp.concatenate([stats_row, jnp.zeros((n_seq, 7, HEAD), jnp.float32)], axis=1)
    acc_chunks = by_chunk(part_acc).astype(jnp.bfloat16)
    source_of, acc_chunks, stats = lax.optimization_barrier((source_of, acc_chunks, stats))
    projected, moved_cache = attend_exchange(acc_chunks, stats, out_weight, n_head, source_of, incoming)
    return (projected, moved_cache)


def solution(mesh):
    placed = (
        P(None, "seq"),
        P("seq", "head"),
        P("head", "seq"),
        P("seq", None, None, "head"),
        P(),
        P("seq"),
        P("seq"),
        P("seq", None, None),
        P("seq", None, None),
    )
    return jax.shard_map(
        body,
        mesh=mesh,
        in_specs=placed,
        out_specs=(P("head", "seq"), P("seq", None, None, "head")),
        check_vma=False,
    )
```

```python
import functools

import jax
import numpy as np
import jax.numpy as jnp
from jax import lax
from jax.experimental import pallas as pl
from jax.experimental.pallas import tpu as pltpu
from jax.sharding import PartitionSpec as P

HEADS = 64
KV_HEADS = 8
HEAD = 128
POS = 4
BLOCK = 128

MESH = pl.DeviceIdType.MESH

rope_base = 500000.0
neg_large = -1e30


def _barrier(peers):
    barrier = pltpu.get_barrier_semaphore()
    for device in peers:
        pl.semaphore_signal(barrier, inc=1, device_id=device, device_id_type=MESH)
    pl.semaphore_wait(barrier, len(peers))


def _send_all(axis, n, me, src_of, land, send_sem, recv_sem):
    copies = []
    for i in range(1, n):
        peer = lax.rem(me + i, n)
        copy = pltpu.make_async_remote_copy(
            src_ref=src_of(peer),
            dst_ref=land.at[me],
            send_sem=send_sem.at[peer],
            recv_sem=recv_sem.at[me],
            device_id={axis: peer},
            device_id_type=MESH,
        )
        copy.start()
        copies.append(copy)
    return copies


def _wait_all(axis, n, me, land, send_sem, recv_sem):
    for i in range(1, n):
        src = lax.rem(me + n - i, n)
        pltpu.make_async_remote_copy(
            src_ref=land.at[src],
            dst_ref=land.at[src],
            send_sem=send_sem.at[src],
            recv_sem=recv_sem.at[src],
            device_id={axis: src},
            device_id_type=MESH,
        ).wait_recv()


def _qkv_kernel(
    n, limit, x_hbm, w_hbm, freq_ref, lengths_ref, pick_hbm, kv_hbm, out_ref, sent_hbm,
    x_vmem, w_vmem, part_ref, pick_ref, land_a, mine, land_b, sems, kv_vmem, sent_vmem, local_sems,
):
    me = lax.axis_index("seq")
    loads = [
        pltpu.make_async_copy(x_hbm, x_vmem, local_sems.at[2]),
        pltpu.make_async_copy(w_hbm, w_vmem, local_sems.at[3]),
        pltpu.make_async_copy(pick_hbm, pick_ref, local_sems.at[4]),
    ]
    for load in loads:
        load.start()
    kv_in = pltpu.make_async_copy(kv_hbm, kv_vmem, local_sems.at[0])
    kv_in.start()
    barrier = pltpu.get_barrier_semaphore()
    for i in range(1, n):
        pl.semaphore_signal(
            barrier, inc=1, device_id={"seq": lax.rem(me + i, n)}, device_id_type=MESH
        )
    for load in loads:
        load.wait()
    product = jnp.dot(x_vmem[...], w_vmem[...], preferred_element_type=jnp.float32)
    groups = product.shape[1] // HEAD
    per = part_ref.shape[1] // groups
    for j in range(n):
        for k in range(per):
            row = product[per * j + k : per * j + k + 1]
            for g in range(groups):
                part_ref[j, k * groups + g : k * groups + g + 1, :] = row[:, g * HEAD : (g + 1) * HEAD]
    land_a[me] = part_ref[me]
    pl.semaphore_wait(barrier, n - 1)
    sent_a = _send_all("seq", n, me, lambda p: part_ref.at[p], land_a, sems.at[0], sems.at[1])
    _wait_all("seq", n, me, land_a, sems.at[0], sems.at[1])
    total = land_a[0]
    for i in range(1, n):
        total = total + land_a[i]
    g = total.shape[0] // 2
    first_row = 2 * me
    second_row = first_row + 1
    pos_a = (lengths_ref[first_row // POS] + first_row % POS).astype(jnp.float32)
    pos_b = (lengths_ref[second_row // POS] + second_row % POS).astype(jnp.float32)
    row = lax.broadcasted_iota(jnp.int32, total.shape, 0)
    lane = lax.broadcasted_iota(jnp.int32, total.shape, 1)
    angle = jnp.where(row < g, pos_a, pos_b) * freq_ref[...]
    value_row = (row == g - 1) | (row == 2 * g - 1)
    cosine = jnp.where(value_row, 1.0, jnp.cos(angle))
    sine = jnp.where(value_row, 0.0, jnp.where(lane < HEAD // 2, -jnp.sin(angle), jnp.sin(angle)))
    turned = pltpu.roll(total, HEAD // 2, 1)
    rotated = (total * cosine + turned * sine).astype(mine.dtype)
    mine[...] = rotated
    land_b[me] = rotated
    sent_b = _send_all("seq", n, me, lambda p: mine, land_b, sems.at[2], sems.at[3])
    kv_in.wait()

    def pick(j, carry):
        per = pick_ref.shape[1]
        sent_vmem[j] = kv_vmem[jnp.minimum(pick_ref[0, j % per, j // per], limit - 1)]
        return carry

    lax.fori_loop(0, sent_vmem.shape[0], pick, 0)
    kv_out = pltpu.make_async_copy(sent_vmem, sent_hbm, local_sems.at[1])
    kv_out.start()
    _wait_all("seq", n, me, land_b, sems.at[2], sems.at[3])
    for copy in sent_a + sent_b:
        copy.wait_send()
    out_ref[...] = land_b[...]
    kv_out.wait()


def qkv_exchange(normed, qkv_weight, freq, lengths, pick, kv_cache, n):
    rows = normed.shape[0]
    groups = qkv_weight.shape[1] // HEAD
    chunk = (n, rows // n * groups, HEAD)
    picked = (pick.size,) + kv_cache.shape[1:]
    return pl.pallas_call(
        functools.partial(_qkv_kernel, n, kv_cache.shape[0]),
        out_shape=(
            jax.ShapeDtypeStruct(chunk, jnp.bfloat16),
            jax.ShapeDtypeStruct(picked, kv_cache.dtype),
        ),
        in_specs=[pl.BlockSpec(memory_space=pl.ANY)] * 2
        + [pl.BlockSpec(memory_space=pltpu.VMEM), pl.BlockSpec(memory_space=pltpu.SMEM)]
        + [pl.BlockSpec(memory_space=pl.ANY)] * 2,
        out_specs=(pl.BlockSpec(memory_space=pltpu.VMEM), pl.BlockSpec(memory_space=pl.ANY)),
        scratch_shapes=[
            pltpu.VMEM(normed.shape, normed.dtype),
            pltpu.VMEM(qkv_weight.shape, qkv_weight.dtype),
            pltpu.VMEM(chunk, jnp.float32),
            pltpu.SMEM(pick.shape, pick.dtype),
            pltpu.VMEM(chunk, jnp.float32),
            pltpu.VMEM(chunk[1:], jnp.bfloat16),
            pltpu.VMEM(chunk, jnp.bfloat16),
            pltpu.SemaphoreType.DMA((4, n)),
            pltpu.VMEM(kv_cache.shape, kv_cache.dtype),
            pltpu.VMEM(picked, kv_cache.dtype),
            pltpu.SemaphoreType.DMA((5,)),
        ],
        compiler_params=pltpu.CompilerParams(collective_id=0, has_side_effects=True),
        cost_estimate=pl.CostEstimate(
            flops=2 * rows * normed.shape[1] * qkv_weight.shape[1],
            bytes_accessed=qkv_weight.size * 2 + 2 * kv_cache.size * kv_cache.dtype.itemsize,
            transcendentals=0,
        ),
    )(normed, qkv_weight, freq, lengths, pick, kv_cache)


def _attend_kernel(
    n, m, rows, acc_ref, stats_ref, w_ref, out_ref, land_p, land_s, mine, land_a, part_c, land_c,
    sems,
):
    me = lax.axis_index("seq")
    me_h = lax.axis_index("head")
    land_p[me] = acc_ref[me]
    land_s[me] = stats_ref[me]
    _barrier(
        [{"seq": lax.rem(me + i, n)} for i in range(1, n)]
        + [{"head": lax.rem(me_h + i, m)} for i in range(1, m)]
    )
    sent_p = _send_all("seq", n, me, lambda p: acc_ref.at[p], land_p, sems.at[0], sems.at[1])
    sent_s = _send_all("seq", n, me, lambda p: stats_ref.at[p], land_s, sems.at[6], sems.at[7])
    _wait_all("seq", n, me, land_s, sems.at[6], sems.at[7])
    _wait_all("seq", n, me, land_p, sems.at[0], sems.at[1])
    columns = [land_s[i].T for i in range(n)]
    top = columns[0][:rows, 0:1]
    for i in range(1, n):
        top = jnp.maximum(top, columns[i][:rows, 0:1])
    numerator = jnp.zeros((rows, HEAD), jnp.float32)
    denominator = jnp.zeros((rows, 1), jnp.float32)
    for i in range(n):
        scale = jnp.exp(columns[i][:rows, 0:1] - top)
        denominator = denominator + columns[i][rows : 2 * rows, 0:1] * scale
        numerator = numerator + land_p[i].astype(jnp.float32) * scale
    attended = (numerator / denominator).astype(mine.dtype)
    mine[...] = attended
    land_a[me] = attended
    sent_a = _send_all("seq", n, me, lambda p: mine, land_a, sems.at[2], sems.at[3])
    _wait_all("seq", n, me, land_a, sems.at[2], sems.at[3])
    heads = n // 2
    projected = None
    for g in range(heads):
        lhs = land_a[2 * g : 2 * g + 2].reshape(2 * rows, HEAD)
        term = jnp.dot(lhs, w_ref[g * HEAD : (g + 1) * HEAD, :], preferred_element_type=jnp.float32)
        projected = term if projected is None else projected + term
    per = part_c.shape[1]
    for j in range(m):
        part_c[j] = projected[j * per : (j + 1) * per]
    land_c[me_h] = part_c[me_h]
    sent_c = _send_all("head", m, me_h, lambda p: part_c.at[p], land_c, sems.at[4], sems.at[5])
    _wait_all("head", m, me_h, land_c, sems.at[4], sems.at[5])
    total = land_c[0]
    for j in range(1, m):
        total = total + land_c[j]
    for copy in sent_p + sent_s + sent_a + sent_c:
        copy.wait_send()
    out_ref[...] = total.astype(out_ref.dtype)


def attend_exchange(acc, stats, out_weight, m):
    n, rows, _ = acc.shape
    width = out_weight.shape[1]
    per = 2 * rows // m
    return pl.pallas_call(
        functools.partial(_attend_kernel, n, m, rows),
        out_shape=jax.ShapeDtypeStruct((per, width), jnp.bfloat16),
        in_specs=[pl.BlockSpec(memory_space=pltpu.VMEM)] * 3,
        out_specs=pl.BlockSpec(memory_space=pltpu.VMEM),
        scratch_shapes=[
            pltpu.VMEM(acc.shape, acc.dtype),
            pltpu.VMEM(stats.shape, jnp.float32),
            pltpu.VMEM((rows, HEAD), jnp.bfloat16),
            pltpu.VMEM((n, rows, HEAD), jnp.bfloat16),
            pltpu.VMEM((m, per, width), jnp.float32),
            pltpu.VMEM((m, per, width), jnp.float32),
            pltpu.SemaphoreType.DMA((8, max(n, m))),
        ],
        compiler_params=pltpu.CompilerParams(collective_id=1, has_side_effects=True),
        cost_estimate=pl.CostEstimate(
            flops=2 * 2 * rows * out_weight.shape[0] * width,
            bytes_accessed=acc.size * 4 + stats.size * 8 + out_weight.size * 2,
            transcendentals=n * rows * HEAD,
        ),
    )(acc, stats, out_weight)


def _pick_kernel(limit, index_ref, src_hbm, out_hbm, buf, sems, out_sem):
    count = buf.shape[0]

    def start(j, carry):
        k = index_ref[j]

        @pl.when(k < limit)
        def _():
            pltpu.make_async_copy(src_hbm.at[jnp.minimum(k, limit - 1)], buf.at[j], sems.at[j]).start()

        @pl.when(k >= limit)
        def _():
            buf[j] = jnp.zeros(buf.shape[1:], buf.dtype)

        return carry

    def send(j, carry):
        k = index_ref[j]

        @pl.when(k < limit)
        def _():
            pltpu.make_async_copy(src_hbm.at[0], buf.at[j], sems.at[j]).wait()

        pltpu.make_async_copy(buf.at[j], out_hbm.at[j], out_sem.at[j]).start()
        return carry

    def finish(j, carry):
        pltpu.make_async_copy(buf.at[j], out_hbm.at[j], out_sem.at[j]).wait()
        return carry

    lax.fori_loop(0, count, start, 0)
    lax.fori_loop(0, count, send, 0)
    lax.fori_loop(0, count, finish, 0)


def pick_blocks(index, source, limit):
    count = index.shape[0]
    shape = (count,) + source.shape[1:]
    nbytes = count * source[0].size * source.dtype.itemsize
    return pl.pallas_call(
        functools.partial(_pick_kernel, limit),
        out_shape=jax.ShapeDtypeStruct(shape, source.dtype),
        in_specs=[
            pl.BlockSpec(memory_space=pltpu.SMEM),
            pl.BlockSpec(memory_space=pl.ANY),
        ],
        out_specs=pl.BlockSpec(memory_space=pl.ANY),
        scratch_shapes=[
            pltpu.VMEM(shape, source.dtype),
            pltpu.SemaphoreType.DMA((count,)),
            pltpu.SemaphoreType.DMA((count,)),
        ],
        cost_estimate=pl.CostEstimate(flops=0, bytes_accessed=2 * nbytes, transcendentals=0),
    )(index, source)


def rotate(values, positions):
    half_width = values.shape[-1] // 2
    frequencies = rope_base ** (
        -(jnp.arange(half_width, dtype=jnp.float32) * 2.0 / values.shape[-1])
    )
    angles = positions[..., None] * frequencies
    cosine_table = jnp.cos(angles)
    sine_table = jnp.sin(angles)
    lower_half = values[..., :half_width]
    upper_half = values[..., half_width:]
    return jnp.concatenate(
        [
            lower_half * cosine_table - upper_half * sine_table,
            upper_half * cosine_table + lower_half * sine_table,
        ],
        axis=-1,
    )


def body(
    normed,
    qkv_weight,
    out_weight,
    kv_cache,
    lengths,
    slot_request,
    slot_block,
    send_list,
    recv_list,
):
    group_size = HEADS // KV_HEADS
    scale_factor = HEAD ** (-0.5)
    requests = lengths.shape[0]
    slot_count = kv_cache.shape[0]
    n_seq = lax.axis_size("seq")
    n_head = lax.axis_size("head")
    me_seq = lax.axis_index("seq")
    rows = normed.shape[0]
    rows_per = rows // n_seq
    groups = qkv_weight.shape[1] // HEAD

    half_width = HEAD // 2
    frequencies = np.float32(rope_base) ** (
        -(np.arange(half_width, dtype=np.float32) * np.float32(2.0) / np.float32(HEAD))
    )
    freq_row = jnp.asarray(np.concatenate([frequencies, frequencies])[None, :].astype(np.float32))
    qkv, outgoing = qkv_exchange(
        normed, qkv_weight, freq_row, lengths, send_list.transpose(0, 2, 1), kv_cache, n_seq
    )
    qkv = qkv.reshape(requests, POS, 1, groups, HEAD)
    local_kv = 1

    outgoing = outgoing.reshape((lax.axis_size("seq"), -1) + kv_cache.shape[1:])
    incoming = lax.all_to_all(outgoing, "seq", split_axis=0, concat_axis=0, tiled=True)
    incoming = incoming.reshape((-1,) + kv_cache.shape[1:])
    arrivals = incoming.shape[0]
    source_of = (
        jnp.full((slot_count + 1,), arrivals, jnp.int32)
        .at[recv_list.reshape(-1)]
        .set(jnp.arange(arrivals, dtype=jnp.int32), mode="drop")[:slot_count]
    )
    queries = qkv[:, :, :, :group_size]
    keys_new = qkv[:, :, :, group_size]
    values_new = qkv[:, :, :, group_size + 1]

    slot_clip = jnp.minimum(slot_request, requests - 1)
    live_slot = slot_request < requests
    token_pos = slot_block[:, None] * BLOCK + jnp.arange(BLOCK, dtype=jnp.int32)[None, :]
    token_valid = (token_pos < lengths[slot_clip][:, None]) & live_slot[:, None]
    cache_view = kv_cache.reshape(slot_count, 2, BLOCK, local_kv, HEAD)
    gathered = queries[slot_clip]
    scores = (
        jnp.einsum(
            "sptgd,sbtd->stgpb", gathered, cache_view[:, 0], preferred_element_type=jnp.float32
        )
        * scale_factor
    )
    scores = jnp.where(token_valid[:, None, None, None, :], scores, neg_large)
    slot_max = jnp.max(scores, axis=-1)
    weights = jnp.where(
        token_valid[:, None, None, None, :], jnp.exp(scores - slot_max[..., None]), 0.0
    )
    slot_sum = jnp.sum(weights, axis=-1)
    slot_acc = jnp.einsum(
        "stgpb,sbtd->stgpd",
        weights.astype(jnp.bfloat16),
        cache_view[:, 1],
        preferred_element_type=jnp.float32,
    )
    flat_width = local_kv * group_size * POS
    slot_max_flat = slot_max.reshape(slot_count, flat_width)
    member = slot_request[:, None] == jnp.arange(requests, dtype=jnp.int32)[None, :]
    request_max = jnp.max(
        jnp.where(member[:, None, :], slot_max_flat[:, :, None], neg_large), axis=0
    ).T
    rescale = jnp.exp(slot_max_flat - request_max[slot_clip])
    member_float = member.astype(jnp.float32).T
    request_sum = jnp.dot(
        member_float,
        slot_sum.reshape(slot_count, flat_width) * rescale,
        precision=lax.Precision.HIGHEST,
    )
    scaled_acc = (slot_acc.reshape(slot_count, flat_width, HEAD) * rescale[:, :, None]).reshape(
        slot_count, flat_width * HEAD
    )
    request_acc = jnp.dot(member_float, scaled_acc, precision=lax.Precision.HIGHEST).reshape(
        requests, flat_width, HEAD
    )

    new_scores = (
        jnp.einsum("rptgd,rqtd->rtgpq", queries, keys_new, preferred_element_type=jnp.float32)
        * scale_factor
    )
    causal = jnp.arange(POS)[:, None] >= jnp.arange(POS)[None, :]
    new_scores = jnp.where(causal, new_scores, neg_large)
    new_max = jnp.max(new_scores, axis=-1)
    new_weights = jnp.where(causal, jnp.exp(new_scores - new_max[..., None]), 0.0)
    new_sum = jnp.sum(new_weights, axis=-1).reshape(requests, flat_width)
    new_acc = jnp.einsum(
        "rtgpq,rqtd->rtgpd",
        new_weights.astype(jnp.bfloat16),
        values_new,
        preferred_element_type=jnp.float32,
    ).reshape(requests, flat_width, HEAD)
    first = me_seq == 0
    new_max = jnp.where(first, new_max.reshape(requests, flat_width), neg_large)
    new_sum = jnp.where(first, new_sum, 0.0)
    new_acc = jnp.where(first, new_acc, 0.0)
    part_max = jnp.maximum(request_max, new_max)
    keep_old = jnp.exp(request_max - part_max)
    keep_new = jnp.exp(new_max - part_max)
    part_sum = request_sum * keep_old + new_sum * keep_new
    part_acc = request_acc * keep_old[..., None] + new_acc * keep_new[..., None]

    def by_chunk(values):
        lead = values.reshape(2, requests // 2, group_size, POS, -1).transpose(2, 0, 1, 3, 4)
        return lead.reshape(n_seq, requests * group_size * POS // n_seq, -1)

    chunk_rows = requests * flat_width // n_seq
    stats_row = jnp.concatenate(
        [
            by_chunk(part_max).reshape(n_seq, 1, chunk_rows),
            by_chunk(part_sum).reshape(n_seq, 1, chunk_rows),
            jnp.zeros((n_seq, 1, HEAD - 2 * chunk_rows), jnp.float32),
        ],
        axis=-1,
    )
    stats = jnp.concatenate([stats_row, jnp.zeros((n_seq, 7, HEAD), jnp.float32)], axis=1)
    acc_chunks = by_chunk(part_acc).astype(jnp.bfloat16)
    source_of, acc_chunks, stats = lax.optimization_barrier((source_of, acc_chunks, stats))
    projected = attend_exchange(acc_chunks, stats, out_weight, n_head)
    moved_cache = pick_blocks(source_of, incoming, arrivals)
    return (projected, moved_cache)


def solution(mesh):
    placed = (
        P(None, "seq"),
        P("seq", "head"),
        P("head", "seq"),
        P("seq", None, None, "head"),
        P(),
        P("seq"),
        P("seq"),
        P("seq", None, None),
        P("seq", None, None),
    )
    return jax.shard_map(
        body,
        mesh=mesh,
        in_specs=placed,
        out_specs=(P("head", "seq"), P("seq", None, None, "head")),
        check_vma=False,
    )
```

```python
import functools

import jax
import numpy as np
import jax.numpy as jnp
from jax import lax
from jax.experimental import pallas as pl
from jax.experimental.pallas import tpu as pltpu
from jax.sharding import PartitionSpec as P

HEADS = 64
KV_HEADS = 8
HEAD = 128
POS = 4
BLOCK = 128

MESH = pl.DeviceIdType.MESH

rope_base = 500000.0
neg_large = -1e30


def _barrier(peers):
    barrier = pltpu.get_barrier_semaphore()
    for device in peers:
        pl.semaphore_signal(barrier, inc=1, device_id=device, device_id_type=MESH)
    pl.semaphore_wait(barrier, len(peers))


def _send_all(axis, n, me, src_of, land, send_sem, recv_sem):
    copies = []
    for i in range(1, n):
        peer = lax.rem(me + i, n)
        copy = pltpu.make_async_remote_copy(
            src_ref=src_of(peer),
            dst_ref=land.at[me],
            send_sem=send_sem.at[peer],
            recv_sem=recv_sem.at[me],
            device_id={axis: peer},
            device_id_type=MESH,
        )
        copy.start()
        copies.append(copy)
    return copies


def _wait_all(axis, n, me, land, send_sem, recv_sem):
    for i in range(1, n):
        src = lax.rem(me + n - i, n)
        pltpu.make_async_remote_copy(
            src_ref=land.at[src],
            dst_ref=land.at[src],
            send_sem=send_sem.at[src],
            recv_sem=recv_sem.at[src],
            device_id={axis: src},
            device_id_type=MESH,
        ).wait_recv()


def _qkv_kernel(
    n, limit, x_hbm, w_hbm, freq_ref, lengths_ref, pick_hbm, kv_hbm, out_ref, sent_hbm,
    x_vmem, w_vmem, part_ref, pick_ref, land_a, mine, land_b, sems, kv_vmem, sent_vmem, local_sems,
):
    me = lax.axis_index("seq")
    loads = [
        pltpu.make_async_copy(x_hbm, x_vmem, local_sems.at[2]),
        pltpu.make_async_copy(w_hbm, w_vmem, local_sems.at[3]),
        pltpu.make_async_copy(pick_hbm, pick_ref, local_sems.at[4]),
    ]
    for load in loads:
        load.start()
    kv_in = pltpu.make_async_copy(kv_hbm, kv_vmem, local_sems.at[0])
    kv_in.start()
    barrier = pltpu.get_barrier_semaphore()
    for i in range(1, n):
        pl.semaphore_signal(
            barrier, inc=1, device_id={"seq": lax.rem(me + i, n)}, device_id_type=MESH
        )
    for load in loads:
        load.wait()
    product = jnp.dot(x_vmem[...], w_vmem[...], preferred_element_type=jnp.float32)
    groups = product.shape[1] // HEAD
    per = part_ref.shape[1] // groups
    for j in range(n):
        for k in range(per):
            row = product[per * j + k : per * j + k + 1]
            for g in range(groups):
                part_ref[j, k * groups + g : k * groups + g + 1, :] = row[:, g * HEAD : (g + 1) * HEAD]
    land_a[me] = part_ref[me]
    pl.semaphore_wait(barrier, n - 1)
    sent_a = _send_all("seq", n, me, lambda p: part_ref.at[p], land_a, sems.at[0], sems.at[1])
    _wait_all("seq", n, me, land_a, sems.at[0], sems.at[1])
    total = land_a[0]
    for i in range(1, n):
        total = total + land_a[i]
    g = total.shape[0] // 2
    first_row = 2 * me
    second_row = first_row + 1
    pos_a = (lengths_ref[first_row // POS] + first_row % POS).astype(jnp.float32)
    pos_b = (lengths_ref[second_row // POS] + second_row % POS).astype(jnp.float32)
    row = lax.broadcasted_iota(jnp.int32, total.shape, 0)
    lane = lax.broadcasted_iota(jnp.int32, total.shape, 1)
    angle = jnp.where(row < g, pos_a, pos_b) * freq_ref[...]
    value_row = (row == g - 1) | (row == 2 * g - 1)
    cosine = jnp.where(value_row, 1.0, jnp.cos(angle))
    sine = jnp.where(value_row, 0.0, jnp.where(lane < HEAD // 2, -jnp.sin(angle), jnp.sin(angle)))
    turned = pltpu.roll(total, HEAD // 2, 1)
    rotated = (total * cosine + turned * sine).astype(mine.dtype)
    mine[...] = rotated
    land_b[me] = rotated
    sent_b = _send_all("seq", n, me, lambda p: mine, land_b, sems.at[2], sems.at[3])
    kv_in.wait()

    def pick(j, carry):
        per = pick_ref.shape[1]
        sent_vmem[j] = kv_vmem[jnp.minimum(pick_ref[0, j % per, j // per], limit - 1)]
        return carry

    lax.fori_loop(0, sent_vmem.shape[0], pick, 0)
    kv_out = pltpu.make_async_copy(sent_vmem, sent_hbm, local_sems.at[1])
    kv_out.start()
    _wait_all("seq", n, me, land_b, sems.at[2], sems.at[3])
    for copy in sent_a + sent_b:
        copy.wait_send()
    out_ref[...] = land_b[...]
    kv_out.wait()


def qkv_exchange(normed, qkv_weight, freq, lengths, pick, kv_cache, n):
    rows = normed.shape[0]
    groups = qkv_weight.shape[1] // HEAD
    chunk = (n, rows // n * groups, HEAD)
    picked = (pick.size,) + kv_cache.shape[1:]
    return pl.pallas_call(
        functools.partial(_qkv_kernel, n, kv_cache.shape[0]),
        out_shape=(
            jax.ShapeDtypeStruct(chunk, jnp.bfloat16),
            jax.ShapeDtypeStruct(picked, kv_cache.dtype),
        ),
        in_specs=[pl.BlockSpec(memory_space=pl.ANY)] * 2
        + [pl.BlockSpec(memory_space=pltpu.VMEM), pl.BlockSpec(memory_space=pltpu.SMEM)]
        + [pl.BlockSpec(memory_space=pl.ANY)] * 2,
        out_specs=(pl.BlockSpec(memory_space=pltpu.VMEM), pl.BlockSpec(memory_space=pl.ANY)),
        scratch_shapes=[
            pltpu.VMEM(normed.shape, normed.dtype),
            pltpu.VMEM(qkv_weight.shape, qkv_weight.dtype),
            pltpu.VMEM(chunk, jnp.float32),
            pltpu.SMEM(pick.shape, pick.dtype),
            pltpu.VMEM(chunk, jnp.float32),
            pltpu.VMEM(chunk[1:], jnp.bfloat16),
            pltpu.VMEM(chunk, jnp.bfloat16),
            pltpu.SemaphoreType.DMA((4, n)),
            pltpu.VMEM(kv_cache.shape, kv_cache.dtype),
            pltpu.VMEM(picked, kv_cache.dtype),
            pltpu.SemaphoreType.DMA((5,)),
        ],
        compiler_params=pltpu.CompilerParams(collective_id=0, has_side_effects=True),
        cost_estimate=pl.CostEstimate(
            flops=2 * rows * normed.shape[1] * qkv_weight.shape[1],
            bytes_accessed=qkv_weight.size * 2 + 2 * kv_cache.size * kv_cache.dtype.itemsize,
            transcendentals=0,
        ),
    )(normed, qkv_weight, freq, lengths, pick, kv_cache)


def _attend_kernel(
    n, m, rows, acc_ref, stats_ref, w_ref, out_ref, land_p, land_s, mine, land_a, part_c, land_c,
    sems,
):
    me = lax.axis_index("seq")
    me_h = lax.axis_index("head")
    land_p[me] = acc_ref[me]
    land_s[me] = stats_ref[me]
    _barrier(
        [{"seq": lax.rem(me + i, n)} for i in range(1, n)]
        + [{"head": lax.rem(me_h + i, m)} for i in range(1, m)]
    )
    sent_p = _send_all("seq", n, me, lambda p: acc_ref.at[p], land_p, sems.at[0], sems.at[1])
    sent_s = _send_all("seq", n, me, lambda p: stats_ref.at[p], land_s, sems.at[6], sems.at[7])
    _wait_all("seq", n, me, land_s, sems.at[6], sems.at[7])
    _wait_all("seq", n, me, land_p, sems.at[0], sems.at[1])
    columns = [land_s[i].T for i in range(n)]
    top = columns[0][:rows, 0:1]
    for i in range(1, n):
        top = jnp.maximum(top, columns[i][:rows, 0:1])
    numerator = jnp.zeros((rows, HEAD), jnp.float32)
    denominator = jnp.zeros((rows, 1), jnp.float32)
    for i in range(n):
        scale = jnp.exp(columns[i][:rows, 0:1] - top)
        denominator = denominator + columns[i][rows : 2 * rows, 0:1] * scale
        numerator = numerator + land_p[i].astype(jnp.float32) * scale
    attended = (numerator / denominator).astype(mine.dtype)
    mine[...] = attended
    land_a[me] = attended
    ring = 4
    z, y = me // ring, me % ring
    sent_a = []
    for i in range(1, ring):
        peer = z * ring + lax.rem(y + i, ring)
        copy = pltpu.make_async_remote_copy(
            src_ref=mine,
            dst_ref=land_a.at[me],
            send_sem=sems.at[2, peer],
            recv_sem=sems.at[3, me],
            device_id={"seq": peer},
            device_id_type=MESH,
        )
        copy.start()
        sent_a.append(copy)
    for i in range(1, ring):
        src = z * ring + lax.rem(y + ring - i, ring)
        pltpu.make_async_remote_copy(
            src_ref=mine,
            dst_ref=land_a.at[src],
            send_sem=sems.at[2, src],
            recv_sem=sems.at[3, src],
            device_id={"seq": src},
            device_id_type=MESH,
        ).wait_recv()
    block = pl.ds(z * ring, ring)
    for i in range(1, n // ring):
        peer = lax.rem(z + i, n // ring) * ring + y
        copy = pltpu.make_async_remote_copy(
            src_ref=land_a.at[block],
            dst_ref=land_a.at[block],
            send_sem=sems.at[8, peer],
            recv_sem=sems.at[9, me],
            device_id={"seq": peer},
            device_id_type=MESH,
        )
        copy.start()
        sent_a.append(copy)
    for i in range(1, n // ring):
        zs = lax.rem(z + n // ring - i, n // ring)
        src = zs * ring + y
        pltpu.make_async_remote_copy(
            src_ref=land_a.at[pl.ds(zs * ring, ring)],
            dst_ref=land_a.at[pl.ds(zs * ring, ring)],
            send_sem=sems.at[8, src],
            recv_sem=sems.at[9, src],
            device_id={"seq": src},
            device_id_type=MESH,
        ).wait_recv()
    heads = n // 2
    projected = None
    for g in range(heads):
        lhs = land_a[2 * g : 2 * g + 2].reshape(2 * rows, HEAD)
        term = jnp.dot(lhs, w_ref[g * HEAD : (g + 1) * HEAD, :], preferred_element_type=jnp.float32)
        projected = term if projected is None else projected + term
    per = part_c.shape[1]
    for j in range(m):
        part_c[j] = projected[j * per : (j + 1) * per]
    land_c[me_h] = part_c[me_h]
    sent_c = _send_all("head", m, me_h, lambda p: part_c.at[p], land_c, sems.at[4], sems.at[5])
    _wait_all("head", m, me_h, land_c, sems.at[4], sems.at[5])
    total = land_c[0]
    for j in range(1, m):
        total = total + land_c[j]
    for copy in sent_p + sent_s + sent_a + sent_c:
        copy.wait_send()
    out_ref[...] = total.astype(out_ref.dtype)


def attend_exchange(acc, stats, out_weight, m):
    n, rows, _ = acc.shape
    width = out_weight.shape[1]
    per = 2 * rows // m
    return pl.pallas_call(
        functools.partial(_attend_kernel, n, m, rows),
        out_shape=jax.ShapeDtypeStruct((per, width), jnp.bfloat16),
        in_specs=[pl.BlockSpec(memory_space=pltpu.VMEM)] * 3,
        out_specs=pl.BlockSpec(memory_space=pltpu.VMEM),
        scratch_shapes=[
            pltpu.VMEM(acc.shape, acc.dtype),
            pltpu.VMEM(stats.shape, jnp.float32),
            pltpu.VMEM((rows, HEAD), jnp.bfloat16),
            pltpu.VMEM((n, rows, HEAD), jnp.bfloat16),
            pltpu.VMEM((m, per, width), jnp.float32),
            pltpu.VMEM((m, per, width), jnp.float32),
            pltpu.SemaphoreType.DMA((10, max(n, m))),
        ],
        compiler_params=pltpu.CompilerParams(collective_id=1, has_side_effects=True),
        cost_estimate=pl.CostEstimate(
            flops=2 * 2 * rows * out_weight.shape[0] * width,
            bytes_accessed=acc.size * 4 + stats.size * 8 + out_weight.size * 2,
            transcendentals=n * rows * HEAD,
        ),
    )(acc, stats, out_weight)


def _pick_kernel(limit, index_ref, src_hbm, out_hbm, buf, sems, out_sem):
    count = buf.shape[0]

    def start(j, carry):
        k = index_ref[j]

        @pl.when(k < limit)
        def _():
            pltpu.make_async_copy(src_hbm.at[jnp.minimum(k, limit - 1)], buf.at[j], sems.at[j]).start()

        @pl.when(k >= limit)
        def _():
            buf[j] = jnp.zeros(buf.shape[1:], buf.dtype)

        return carry

    def send(j, carry):
        k = index_ref[j]

        @pl.when(k < limit)
        def _():
            pltpu.make_async_copy(src_hbm.at[0], buf.at[j], sems.at[j]).wait()

        pltpu.make_async_copy(buf.at[j], out_hbm.at[j], out_sem.at[j]).start()
        return carry

    def finish(j, carry):
        pltpu.make_async_copy(buf.at[j], out_hbm.at[j], out_sem.at[j]).wait()
        return carry

    lax.fori_loop(0, count, start, 0)
    lax.fori_loop(0, count, send, 0)
    lax.fori_loop(0, count, finish, 0)


def pick_blocks(index, source, limit):
    count = index.shape[0]
    shape = (count,) + source.shape[1:]
    nbytes = count * source[0].size * source.dtype.itemsize
    return pl.pallas_call(
        functools.partial(_pick_kernel, limit),
        out_shape=jax.ShapeDtypeStruct(shape, source.dtype),
        in_specs=[
            pl.BlockSpec(memory_space=pltpu.SMEM),
            pl.BlockSpec(memory_space=pl.ANY),
        ],
        out_specs=pl.BlockSpec(memory_space=pl.ANY),
        scratch_shapes=[
            pltpu.VMEM(shape, source.dtype),
            pltpu.SemaphoreType.DMA((count,)),
            pltpu.SemaphoreType.DMA((count,)),
        ],
        cost_estimate=pl.CostEstimate(flops=0, bytes_accessed=2 * nbytes, transcendentals=0),
    )(index, source)


def rotate(values, positions):
    half_width = values.shape[-1] // 2
    frequencies = rope_base ** (
        -(jnp.arange(half_width, dtype=jnp.float32) * 2.0 / values.shape[-1])
    )
    angles = positions[..., None] * frequencies
    cosine_table = jnp.cos(angles)
    sine_table = jnp.sin(angles)
    lower_half = values[..., :half_width]
    upper_half = values[..., half_width:]
    return jnp.concatenate(
        [
            lower_half * cosine_table - upper_half * sine_table,
            upper_half * cosine_table + lower_half * sine_table,
        ],
        axis=-1,
    )


def body(
    normed,
    qkv_weight,
    out_weight,
    kv_cache,
    lengths,
    slot_request,
    slot_block,
    send_list,
    recv_list,
):
    group_size = HEADS // KV_HEADS
    scale_factor = HEAD ** (-0.5)
    requests = lengths.shape[0]
    slot_count = kv_cache.shape[0]
    n_seq = lax.axis_size("seq")
    n_head = lax.axis_size("head")
    me_seq = lax.axis_index("seq")
    rows = normed.shape[0]
    rows_per = rows // n_seq
    groups = qkv_weight.shape[1] // HEAD

    half_width = HEAD // 2
    frequencies = np.float32(rope_base) ** (
        -(np.arange(half_width, dtype=np.float32) * np.float32(2.0) / np.float32(HEAD))
    )
    freq_row = jnp.asarray(np.concatenate([frequencies, frequencies])[None, :].astype(np.float32))
    qkv, outgoing = qkv_exchange(
        normed, qkv_weight, freq_row, lengths, send_list.transpose(0, 2, 1), kv_cache, n_seq
    )
    qkv = qkv.reshape(requests, POS, 1, groups, HEAD)
    local_kv = 1

    outgoing = outgoing.reshape((lax.axis_size("seq"), -1) + kv_cache.shape[1:])
    incoming = lax.all_to_all(outgoing, "seq", split_axis=0, concat_axis=0, tiled=True)
    incoming = incoming.reshape((-1,) + kv_cache.shape[1:])
    arrivals = incoming.shape[0]
    source_of = (
        jnp.full((slot_count + 1,), arrivals, jnp.int32)
        .at[recv_list.reshape(-1)]
        .set(jnp.arange(arrivals, dtype=jnp.int32), mode="drop")[:slot_count]
    )
    queries = qkv[:, :, :, :group_size]
    keys_new = qkv[:, :, :, group_size]
    values_new = qkv[:, :, :, group_size + 1]

    slot_clip = jnp.minimum(slot_request, requests - 1)
    live_slot = slot_request < requests
    token_pos = slot_block[:, None] * BLOCK + jnp.arange(BLOCK, dtype=jnp.int32)[None, :]
    token_valid = (token_pos < lengths[slot_clip][:, None]) & live_slot[:, None]
    cache_view = kv_cache.reshape(slot_count, 2, BLOCK, local_kv, HEAD)
    gathered = queries[slot_clip]
    scores = (
        jnp.einsum(
            "sptgd,sbtd->stgpb", gathered, cache_view[:, 0], preferred_element_type=jnp.float32
        )
        * scale_factor
    )
    scores = jnp.where(token_valid[:, None, None, None, :], scores, neg_large)
    slot_max = jnp.max(scores, axis=-1)
    weights = jnp.where(
        token_valid[:, None, None, None, :], jnp.exp(scores - slot_max[..., None]), 0.0
    )
    slot_sum = jnp.sum(weights, axis=-1)
    slot_acc = jnp.einsum(
        "stgpb,sbtd->stgpd",
        weights.astype(jnp.bfloat16),
        cache_view[:, 1],
        preferred_element_type=jnp.float32,
    )
    flat_width = local_kv * group_size * POS
    slot_max_flat = slot_max.reshape(slot_count, flat_width)
    member = slot_request[:, None] == jnp.arange(requests, dtype=jnp.int32)[None, :]
    request_max = jnp.max(
        jnp.where(member[:, None, :], slot_max_flat[:, :, None], neg_large), axis=0
    ).T
    rescale = jnp.exp(slot_max_flat - request_max[slot_clip])
    member_float = member.astype(jnp.float32).T
    request_sum = jnp.dot(
        member_float,
        slot_sum.reshape(slot_count, flat_width) * rescale,
        precision=lax.Precision.HIGHEST,
    )
    scaled_acc = (slot_acc.reshape(slot_count, flat_width, HEAD) * rescale[:, :, None]).reshape(
        slot_count, flat_width * HEAD
    )
    request_acc = jnp.dot(member_float, scaled_acc, precision=lax.Precision.HIGHEST).reshape(
        requests, flat_width, HEAD
    )

    new_scores = (
        jnp.einsum("rptgd,rqtd->rtgpq", queries, keys_new, preferred_element_type=jnp.float32)
        * scale_factor
    )
    causal = jnp.arange(POS)[:, None] >= jnp.arange(POS)[None, :]
    new_scores = jnp.where(causal, new_scores, neg_large)
    new_max = jnp.max(new_scores, axis=-1)
    new_weights = jnp.where(causal, jnp.exp(new_scores - new_max[..., None]), 0.0)
    new_sum = jnp.sum(new_weights, axis=-1).reshape(requests, flat_width)
    new_acc = jnp.einsum(
        "rtgpq,rqtd->rtgpd",
        new_weights.astype(jnp.bfloat16),
        values_new,
        preferred_element_type=jnp.float32,
    ).reshape(requests, flat_width, HEAD)
    first = me_seq == 0
    new_max = jnp.where(first, new_max.reshape(requests, flat_width), neg_large)
    new_sum = jnp.where(first, new_sum, 0.0)
    new_acc = jnp.where(first, new_acc, 0.0)
    part_max = jnp.maximum(request_max, new_max)
    keep_old = jnp.exp(request_max - part_max)
    keep_new = jnp.exp(new_max - part_max)
    part_sum = request_sum * keep_old + new_sum * keep_new
    part_acc = request_acc * keep_old[..., None] + new_acc * keep_new[..., None]

    def by_chunk(values):
        lead = values.reshape(2, requests // 2, group_size, POS, -1).transpose(2, 0, 1, 3, 4)
        return lead.reshape(n_seq, requests * group_size * POS // n_seq, -1)

    chunk_rows = requests * flat_width // n_seq
    stats_row = jnp.concatenate(
        [
            by_chunk(part_max).reshape(n_seq, 1, chunk_rows),
            by_chunk(part_sum).reshape(n_seq, 1, chunk_rows),
            jnp.zeros((n_seq, 1, HEAD - 2 * chunk_rows), jnp.float32),
        ],
        axis=-1,
    )
    stats = jnp.concatenate([stats_row, jnp.zeros((n_seq, 7, HEAD), jnp.float32)], axis=1)
    acc_chunks = by_chunk(part_acc).astype(jnp.bfloat16)
    source_of, acc_chunks, stats = lax.optimization_barrier((source_of, acc_chunks, stats))
    projected = attend_exchange(acc_chunks, stats, out_weight, n_head)
    moved_cache = pick_blocks(source_of, incoming, arrivals)
    return (projected, moved_cache)


def solution(mesh):
    placed = (
        P(None, "seq"),
        P("seq", "head"),
        P("head", "seq"),
        P("seq", None, None, "head"),
        P(),
        P("seq"),
        P("seq"),
        P("seq", None, None),
        P("seq", None, None),
    )
    return jax.shard_map(
        body,
        mesh=mesh,
        in_specs=placed,
        out_specs=(P("head", "seq"), P("seq", None, None, "head")),
        check_vma=False,
    )
```

```python
import functools

import jax
import numpy as np
import jax.numpy as jnp
from jax import lax
from jax.experimental import pallas as pl
from jax.experimental.pallas import tpu as pltpu
from jax.sharding import PartitionSpec as P

HEADS = 64
KV_HEADS = 8
HEAD = 128
POS = 4
BLOCK = 128

MESH = pl.DeviceIdType.MESH

rope_base = 500000.0
neg_large = -1e30


def _barrier(peers):
    barrier = pltpu.get_barrier_semaphore()
    for device in peers:
        pl.semaphore_signal(barrier, inc=1, device_id=device, device_id_type=MESH)
    pl.semaphore_wait(barrier, len(peers))


def _send_all(axis, n, me, src_of, land, send_sem, recv_sem):
    copies = []
    for i in range(1, n):
        peer = lax.rem(me + i, n)
        copy = pltpu.make_async_remote_copy(
            src_ref=src_of(peer),
            dst_ref=land.at[me],
            send_sem=send_sem.at[peer],
            recv_sem=recv_sem.at[me],
            device_id={axis: peer},
            device_id_type=MESH,
        )
        copy.start()
        copies.append(copy)
    return copies


def _wait_all(axis, n, me, land, send_sem, recv_sem):
    for i in range(1, n):
        src = lax.rem(me + n - i, n)
        pltpu.make_async_remote_copy(
            src_ref=land.at[src],
            dst_ref=land.at[src],
            send_sem=send_sem.at[src],
            recv_sem=recv_sem.at[src],
            device_id={axis: src},
            device_id_type=MESH,
        ).wait_recv()


def _qkv_kernel(
    n, limit, x_hbm, w_hbm, freq_ref, lengths_ref, pick_hbm, kv_hbm, out_ref, sent_hbm,
    x_vmem, w_vmem, part_ref, pick_ref, land_a, mine, land_b, sems, kv_vmem, sent_vmem, local_sems,
):
    me = lax.axis_index("seq")
    loads = [
        pltpu.make_async_copy(x_hbm, x_vmem, local_sems.at[2]),
        pltpu.make_async_copy(w_hbm, w_vmem, local_sems.at[3]),
        pltpu.make_async_copy(pick_hbm, pick_ref, local_sems.at[4]),
    ]
    for load in loads:
        load.start()
    barrier = pltpu.get_barrier_semaphore()
    for i in range(1, n):
        pl.semaphore_signal(
            barrier, inc=1, device_id={"seq": lax.rem(me + i, n)}, device_id_type=MESH
        )
    for load in loads:
        load.wait()
    kv_in = pltpu.make_async_copy(kv_hbm, kv_vmem, local_sems.at[0])
    kv_in.start()
    product = jnp.dot(x_vmem[...], w_vmem[...], preferred_element_type=jnp.float32)
    groups = product.shape[1] // HEAD
    per = part_ref.shape[1] // groups
    for j in range(n):
        for k in range(per):
            row = product[per * j + k : per * j + k + 1]
            for g in range(groups):
                part_ref[j, k * groups + g : k * groups + g + 1, :] = row[:, g * HEAD : (g + 1) * HEAD]
    land_a[me] = part_ref[me]
    pl.semaphore_wait(barrier, n - 1)
    sent_a = _send_all("seq", n, me, lambda p: part_ref.at[p], land_a, sems.at[0], sems.at[1])
    _wait_all("seq", n, me, land_a, sems.at[0], sems.at[1])
    total = land_a[0]
    for i in range(1, n):
        total = total + land_a[i]
    g = total.shape[0] // 2
    first_row = 2 * me
    second_row = first_row + 1
    pos_a = (lengths_ref[first_row // POS] + first_row % POS).astype(jnp.float32)
    pos_b = (lengths_ref[second_row // POS] + second_row % POS).astype(jnp.float32)
    row = lax.broadcasted_iota(jnp.int32, total.shape, 0)
    lane = lax.broadcasted_iota(jnp.int32, total.shape, 1)
    angle = jnp.where(row < g, pos_a, pos_b) * freq_ref[...]
    value_row = (row == g - 1) | (row == 2 * g - 1)
    cosine = jnp.where(value_row, 1.0, jnp.cos(angle))
    sine = jnp.where(value_row, 0.0, jnp.where(lane < HEAD // 2, -jnp.sin(angle), jnp.sin(angle)))
    turned = pltpu.roll(total, HEAD // 2, 1)
    rotated = (total * cosine + turned * sine).astype(mine.dtype)
    mine[...] = rotated
    land_b[me] = rotated
    sent_b = _send_all("seq", n, me, lambda p: mine, land_b, sems.at[2], sems.at[3])
    kv_in.wait()

    def pick(j, carry):
        per = pick_ref.shape[1]
        sent_vmem[j] = kv_vmem[jnp.minimum(pick_ref[0, j % per, j // per], limit - 1)]
        return carry

    lax.fori_loop(0, sent_vmem.shape[0], pick, 0)
    kv_out = pltpu.make_async_copy(sent_vmem, sent_hbm, local_sems.at[1])
    kv_out.start()
    _wait_all("seq", n, me, land_b, sems.at[2], sems.at[3])
    for copy in sent_a + sent_b:
        copy.wait_send()
    out_ref[...] = land_b[...]
    kv_out.wait()


def qkv_exchange(normed, qkv_weight, freq, lengths, pick, kv_cache, n):
    rows = normed.shape[0]
    groups = qkv_weight.shape[1] // HEAD
    chunk = (n, rows // n * groups, HEAD)
    picked = (pick.size,) + kv_cache.shape[1:]
    return pl.pallas_call(
        functools.partial(_qkv_kernel, n, kv_cache.shape[0]),
        out_shape=(
            jax.ShapeDtypeStruct(chunk, jnp.bfloat16),
            jax.ShapeDtypeStruct(picked, kv_cache.dtype),
        ),
        in_specs=[pl.BlockSpec(memory_space=pl.ANY)] * 2
        + [pl.BlockSpec(memory_space=pltpu.VMEM), pl.BlockSpec(memory_space=pltpu.SMEM)]
        + [pl.BlockSpec(memory_space=pl.ANY)] * 2,
        out_specs=(pl.BlockSpec(memory_space=pltpu.VMEM), pl.BlockSpec(memory_space=pl.ANY)),
        scratch_shapes=[
            pltpu.VMEM(normed.shape, normed.dtype),
            pltpu.VMEM(qkv_weight.shape, qkv_weight.dtype),
            pltpu.VMEM(chunk, jnp.float32),
            pltpu.SMEM(pick.shape, pick.dtype),
            pltpu.VMEM(chunk, jnp.float32),
            pltpu.VMEM(chunk[1:], jnp.bfloat16),
            pltpu.VMEM(chunk, jnp.bfloat16),
            pltpu.SemaphoreType.DMA((4, n)),
            pltpu.VMEM(kv_cache.shape, kv_cache.dtype),
            pltpu.VMEM(picked, kv_cache.dtype),
            pltpu.SemaphoreType.DMA((5,)),
        ],
        compiler_params=pltpu.CompilerParams(collective_id=0, has_side_effects=True),
        cost_estimate=pl.CostEstimate(
            flops=2 * rows * normed.shape[1] * qkv_weight.shape[1],
            bytes_accessed=qkv_weight.size * 2 + 2 * kv_cache.size * kv_cache.dtype.itemsize,
            transcendentals=0,
        ),
    )(normed, qkv_weight, freq, lengths, pick, kv_cache)


def _attend_kernel(
    n, m, rows, acc_ref, stats_ref, w_ref, out_ref, land_p, land_s, mine, land_a, part_c, land_c,
    sems,
):
    me = lax.axis_index("seq")
    me_h = lax.axis_index("head")
    land_p[me] = acc_ref[me]
    land_s[me] = stats_ref[me]
    _barrier(
        [{"seq": lax.rem(me + i, n)} for i in range(1, n)]
        + [{"head": lax.rem(me_h + i, m)} for i in range(1, m)]
    )
    sent_p = _send_all("seq", n, me, lambda p: acc_ref.at[p], land_p, sems.at[0], sems.at[1])
    sent_s = _send_all("seq", n, me, lambda p: stats_ref.at[p], land_s, sems.at[6], sems.at[7])
    _wait_all("seq", n, me, land_s, sems.at[6], sems.at[7])
    _wait_all("seq", n, me, land_p, sems.at[0], sems.at[1])
    columns = [land_s[i].T for i in range(n)]
    top = columns[0][:rows, 0:1]
    for i in range(1, n):
        top = jnp.maximum(top, columns[i][:rows, 0:1])
    numerator = jnp.zeros((rows, HEAD), jnp.float32)
    denominator = jnp.zeros((rows, 1), jnp.float32)
    for i in range(n):
        scale = jnp.exp(columns[i][:rows, 0:1] - top)
        denominator = denominator + columns[i][rows : 2 * rows, 0:1] * scale
        numerator = numerator + land_p[i].astype(jnp.float32) * scale
    attended = (numerator / denominator).astype(mine.dtype)
    mine[...] = attended
    land_a[me] = attended
    sent_a = _send_all("seq", n, me, lambda p: mine, land_a, sems.at[2], sems.at[3])
    _wait_all("seq", n, me, land_a, sems.at[2], sems.at[3])
    heads = n // 2
    projected = None
    for g in range(heads):
        lhs = land_a[2 * g : 2 * g + 2].reshape(2 * rows, HEAD)
        term = jnp.dot(lhs, w_ref[g * HEAD : (g + 1) * HEAD, :], preferred_element_type=jnp.float32)
        projected = term if projected is None else projected + term
    per = part_c.shape[1]
    for j in range(m):
        part_c[j] = projected[j * per : (j + 1) * per]
    land_c[me_h] = part_c[me_h]
    sent_c = _send_all("head", m, me_h, lambda p: part_c.at[p], land_c, sems.at[4], sems.at[5])
    _wait_all("head", m, me_h, land_c, sems.at[4], sems.at[5])
    total = land_c[0]
    for j in range(1, m):
        total = total + land_c[j]
    for copy in sent_p + sent_s + sent_a + sent_c:
        copy.wait_send()
    out_ref[...] = total.astype(out_ref.dtype)


def attend_exchange(acc, stats, out_weight, m):
    n, rows, _ = acc.shape
    width = out_weight.shape[1]
    per = 2 * rows // m
    return pl.pallas_call(
        functools.partial(_attend_kernel, n, m, rows),
        out_shape=jax.ShapeDtypeStruct((per, width), jnp.bfloat16),
        in_specs=[pl.BlockSpec(memory_space=pltpu.VMEM)] * 3,
        out_specs=pl.BlockSpec(memory_space=pltpu.VMEM),
        scratch_shapes=[
            pltpu.VMEM(acc.shape, acc.dtype),
            pltpu.VMEM(stats.shape, jnp.float32),
            pltpu.VMEM((rows, HEAD), jnp.bfloat16),
            pltpu.VMEM((n, rows, HEAD), jnp.bfloat16),
            pltpu.VMEM((m, per, width), jnp.float32),
            pltpu.VMEM((m, per, width), jnp.float32),
            pltpu.SemaphoreType.DMA((8, max(n, m))),
        ],
        compiler_params=pltpu.CompilerParams(collective_id=1, has_side_effects=True),
        cost_estimate=pl.CostEstimate(
            flops=2 * 2 * rows * out_weight.shape[0] * width,
            bytes_accessed=acc.size * 4 + stats.size * 8 + out_weight.size * 2,
            transcendentals=n * rows * HEAD,
        ),
    )(acc, stats, out_weight)


def _pick_kernel(limit, index_ref, src_hbm, out_hbm, buf, sems, out_sem):
    count = buf.shape[0]

    def start(j, carry):
        k = index_ref[j]

        @pl.when(k < limit)
        def _():
            pltpu.make_async_copy(src_hbm.at[jnp.minimum(k, limit - 1)], buf.at[j], sems.at[j]).start()

        @pl.when(k >= limit)
        def _():
            buf[j] = jnp.zeros(buf.shape[1:], buf.dtype)

        return carry

    def send(j, carry):
        k = index_ref[j]

        @pl.when(k < limit)
        def _():
            pltpu.make_async_copy(src_hbm.at[0], buf.at[j], sems.at[j]).wait()

        pltpu.make_async_copy(buf.at[j], out_hbm.at[j], out_sem.at[j]).start()
        return carry

    def finish(j, carry):
        pltpu.make_async_copy(buf.at[j], out_hbm.at[j], out_sem.at[j]).wait()
        return carry

    lax.fori_loop(0, count, start, 0)
    lax.fori_loop(0, count, send, 0)
    lax.fori_loop(0, count, finish, 0)


def pick_blocks(index, source, limit):
    count = index.shape[0]
    shape = (count,) + source.shape[1:]
    nbytes = count * source[0].size * source.dtype.itemsize
    return pl.pallas_call(
        functools.partial(_pick_kernel, limit),
        out_shape=jax.ShapeDtypeStruct(shape, source.dtype),
        in_specs=[
            pl.BlockSpec(memory_space=pltpu.SMEM),
            pl.BlockSpec(memory_space=pl.ANY),
        ],
        out_specs=pl.BlockSpec(memory_space=pl.ANY),
        scratch_shapes=[
            pltpu.VMEM(shape, source.dtype),
            pltpu.SemaphoreType.DMA((count,)),
            pltpu.SemaphoreType.DMA((count,)),
        ],
        cost_estimate=pl.CostEstimate(flops=0, bytes_accessed=2 * nbytes, transcendentals=0),
    )(index, source)


def rotate(values, positions):
    half_width = values.shape[-1] // 2
    frequencies = rope_base ** (
        -(jnp.arange(half_width, dtype=jnp.float32) * 2.0 / values.shape[-1])
    )
    angles = positions[..., None] * frequencies
    cosine_table = jnp.cos(angles)
    sine_table = jnp.sin(angles)
    lower_half = values[..., :half_width]
    upper_half = values[..., half_width:]
    return jnp.concatenate(
        [
            lower_half * cosine_table - upper_half * sine_table,
            upper_half * cosine_table + lower_half * sine_table,
        ],
        axis=-1,
    )


def body(
    normed,
    qkv_weight,
    out_weight,
    kv_cache,
    lengths,
    slot_request,
    slot_block,
    send_list,
    recv_list,
):
    group_size = HEADS // KV_HEADS
    scale_factor = HEAD ** (-0.5)
    requests = lengths.shape[0]
    slot_count = kv_cache.shape[0]
    n_seq = lax.axis_size("seq")
    n_head = lax.axis_size("head")
    me_seq = lax.axis_index("seq")
    rows = normed.shape[0]
    rows_per = rows // n_seq
    groups = qkv_weight.shape[1] // HEAD

    half_width = HEAD // 2
    frequencies = np.float32(rope_base) ** (
        -(np.arange(half_width, dtype=np.float32) * np.float32(2.0) / np.float32(HEAD))
    )
    freq_row = jnp.asarray(np.concatenate([frequencies, frequencies])[None, :].astype(np.float32))
    qkv, outgoing = qkv_exchange(
        normed, qkv_weight, freq_row, lengths, send_list.transpose(0, 2, 1), kv_cache, n_seq
    )
    qkv = qkv.reshape(requests, POS, 1, groups, HEAD)
    local_kv = 1

    outgoing = outgoing.reshape((lax.axis_size("seq"), -1) + kv_cache.shape[1:])
    incoming = lax.all_to_all(outgoing, "seq", split_axis=0, concat_axis=0, tiled=True)
    incoming = incoming.reshape((-1,) + kv_cache.shape[1:])
    arrivals = incoming.shape[0]
    source_of = (
        jnp.full((slot_count + 1,), arrivals, jnp.int32)
        .at[recv_list.reshape(-1)]
        .set(jnp.arange(arrivals, dtype=jnp.int32), mode="drop")[:slot_count]
    )
    queries = qkv[:, :, :, :group_size]
    keys_new = qkv[:, :, :, group_size]
    values_new = qkv[:, :, :, group_size + 1]

    slot_clip = jnp.minimum(slot_request, requests - 1)
    live_slot = slot_request < requests
    token_pos = slot_block[:, None] * BLOCK + jnp.arange(BLOCK, dtype=jnp.int32)[None, :]
    token_valid = (token_pos < lengths[slot_clip][:, None]) & live_slot[:, None]
    cache_view = kv_cache.reshape(slot_count, 2, BLOCK, local_kv, HEAD)
    gathered = queries[slot_clip]
    scores = (
        jnp.einsum(
            "sptgd,sbtd->stgpb", gathered, cache_view[:, 0], preferred_element_type=jnp.float32
        )
        * scale_factor
    )
    scores = jnp.where(token_valid[:, None, None, None, :], scores, neg_large)
    slot_max = jnp.max(scores, axis=-1)
    weights = jnp.where(
        token_valid[:, None, None, None, :], jnp.exp(scores - slot_max[..., None]), 0.0
    )
    slot_sum = jnp.sum(weights, axis=-1)
    slot_acc = jnp.einsum(
        "stgpb,sbtd->stgpd",
        weights.astype(jnp.bfloat16),
        cache_view[:, 1],
        preferred_element_type=jnp.float32,
    )
    flat_width = local_kv * group_size * POS
    slot_max_flat = slot_max.reshape(slot_count, flat_width)
    member = slot_request[:, None] == jnp.arange(requests, dtype=jnp.int32)[None, :]
    request_max = jnp.max(
        jnp.where(member[:, None, :], slot_max_flat[:, :, None], neg_large), axis=0
    ).T
    rescale = jnp.exp(slot_max_flat - request_max[slot_clip])
    member_float = member.astype(jnp.float32).T
    request_sum = jnp.dot(
        member_float,
        slot_sum.reshape(slot_count, flat_width) * rescale,
        precision=lax.Precision.HIGHEST,
    )
    scaled_acc = (slot_acc.reshape(slot_count, flat_width, HEAD) * rescale[:, :, None]).reshape(
        slot_count, flat_width * HEAD
    )
    request_acc = jnp.dot(member_float, scaled_acc, precision=lax.Precision.HIGHEST).reshape(
        requests, flat_width, HEAD
    )

    new_scores = (
        jnp.einsum("rptgd,rqtd->rtgpq", queries, keys_new, preferred_element_type=jnp.float32)
        * scale_factor
    )
    causal = jnp.arange(POS)[:, None] >= jnp.arange(POS)[None, :]
    new_scores = jnp.where(causal, new_scores, neg_large)
    new_max = jnp.max(new_scores, axis=-1)
    new_weights = jnp.where(causal, jnp.exp(new_scores - new_max[..., None]), 0.0)
    new_sum = jnp.sum(new_weights, axis=-1).reshape(requests, flat_width)
    new_acc = jnp.einsum(
        "rtgpq,rqtd->rtgpd",
        new_weights.astype(jnp.bfloat16),
        values_new,
        preferred_element_type=jnp.float32,
    ).reshape(requests, flat_width, HEAD)
    first = me_seq == 0
    new_max = jnp.where(first, new_max.reshape(requests, flat_width), neg_large)
    new_sum = jnp.where(first, new_sum, 0.0)
    new_acc = jnp.where(first, new_acc, 0.0)
    part_max = jnp.maximum(request_max, new_max)
    keep_old = jnp.exp(request_max - part_max)
    keep_new = jnp.exp(new_max - part_max)
    part_sum = request_sum * keep_old + new_sum * keep_new
    part_acc = request_acc * keep_old[..., None] + new_acc * keep_new[..., None]

    def by_chunk(values):
        lead = values.reshape(2, requests // 2, group_size, POS, -1).transpose(2, 0, 1, 3, 4)
        return lead.reshape(n_seq, requests * group_size * POS // n_seq, -1)

    chunk_rows = requests * flat_width // n_seq
    stats_row = jnp.concatenate(
        [
            by_chunk(part_max).reshape(n_seq, 1, chunk_rows),
            by_chunk(part_sum).reshape(n_seq, 1, chunk_rows),
            jnp.zeros((n_seq, 1, HEAD - 2 * chunk_rows), jnp.float32),
        ],
        axis=-1,
    )
    stats = jnp.concatenate([stats_row, jnp.zeros((n_seq, 7, HEAD), jnp.float32)], axis=1)
    acc_chunks = by_chunk(part_acc).astype(jnp.bfloat16)
    source_of, acc_chunks, stats = lax.optimization_barrier((source_of, acc_chunks, stats))
    projected = attend_exchange(acc_chunks, stats, out_weight, n_head)
    moved_cache = pick_blocks(source_of, incoming, arrivals)
    return (projected, moved_cache)


def solution(mesh):
    placed = (
        P(None, "seq"),
        P("seq", "head"),
        P("head", "seq"),
        P("seq", None, None, "head"),
        P(),
        P("seq"),
        P("seq"),
        P("seq", None, None),
        P("seq", None, None),
    )
    return jax.shard_map(
        body,
        mesh=mesh,
        in_specs=placed,
        out_specs=(P("head", "seq"), P("seq", None, None, "head")),
        check_vma=False,
    )
```
